128 devices in a mesh: sky: 32 (over y, z, core), band: 4 (over x).
Axes of the slice: x: 4, y: 4, z: 4, core: 2. Of those that a mesh axis runs over, the one named last changes fastest.
Arguments:
- band_maps: float32 [16, 512, 1024], P('band', 'sky'), may hold values from -64 to 64
- cycle_weight: float32 [512], P('sky'), may hold values from 0.5 to 2
- cycle_len: int32 [512], P('sky'), may hold values from 4 to 1024, as said below
- m_order: int32 [1024], replicated, may hold values from 0 to 1023, each once
- legendre: bfloat16 [1024, 1024, 512], P(('sky', 'band')), may hold values from -4 to 4
- band_start: int32 [1], replicated, may hold values from 256 to 1023
Outputs:
- clean_map: float32 [512, 1024], P('sky', 'band')
The draws below stay inside these ranges and needn't reach their ends.
Inputs may be any that keep to these rules, and one draw needn't show every extreme that they name: `cycle_len`: each cycle slot holds a polar-cap cycle of 4 i pixels, every i from 1 to 256 on exactly two cycle slots. `m_order`: each azimuthal order 0 to 1023 is served by exactly one order slot.
All inputs are finite; a program needn't handle non-finite values.
Results may differ from the reference program's by a relative error of at most 0.0023.
Values may be sent and summed in bfloat16 or wider, within the bound.
A program may use at most 128 MiB of HBM per device.

```python
import math
import jax
import jax.numpy as jnp
from jax import lax

BANDS = 16
M = 1024
MP = 32
LB = 1024
DOM = 4
CYCLES = 512
RLEN = 1024
ND = 128


def cap_lengths(key):
    order = jax.random.permutation(jax.random.fold_in(key, 11), CYCLES)
    return 4 * (order % (CYCLES // 2) + 1)


def draw_cycle_len(key, part):
    return cap_lengths(key).astype(jnp.int32)


def draw_band_maps(key, part):
    lengths = cap_lengths(key).astype(jnp.float32)
    keys = jax.random.split(jax.random.fold_in(key, 23), 4)
    pixels = jnp.arange(RLEN).astype(jnp.float32)
    azimuth = jnp.pi * (2.0 * pixels[None, :] + 1.0) / lengths[:, None]
    centre = jax.random.uniform(keys[0], (BANDS, 1, 1), jnp.float32, -jnp.pi, jnp.pi)
    level = jnp.exp(jax.random.uniform(keys[1], (BANDS, 1, 1), jnp.float32, math.log(0.3), math.log(3.0)))
    envelope = jnp.exp(1.5 * jnp.cos(azimuth[None] - centre))
    common = jax.random.truncated_normal(keys[2], -4.0, 4.0, (CYCLES, RLEN), jnp.float32)
    noise = jax.random.truncated_normal(keys[3], -4.0, 4.0, (BANDS, CYCLES, RLEN), jnp.float32)
    return (common[None] + level * envelope * noise).astype(jnp.float32)


def block_scale(own_key, dims, pieces, smallest, largest):
    def one(dim, blocks):
        steps = jax.random.uniform(jax.random.fold_in(jax.random.fold_in(own_key, 6), dim), (blocks,), jnp.float32, smallest / len(pieces), largest / len(pieces))
        return jnp.repeat(jnp.exp(steps), dims[dim] // blocks).reshape((-1,) + (1,) * (len(dims) - dim - 1))

    gain = one(*pieces[0])
    for cut in pieces[1:]:
        gain = gain * one(*cut)
    return gain


def centred(key, extent, spread, limit, cuts=(), kind=jnp.bfloat16):
    result = spread * jax.random.normal(key, extent, jnp.float32)
    if cuts:
        result = result * block_scale(key, extent, cuts, -0.22, 0.18)
    return jnp.clip(result, -limit, limit).astype(kind)


def setup_inputs(seed: int = 0) -> dict:
    streams_of = jax.random.split(jax.random.key(seed), 7)
    return {
        "band_maps": draw_band_maps(jax.random.fold_in(streams_of[6], 71), 0),
        "cycle_weight": jnp.clip(jnp.exp(math.log(2.0) - 1.3862944 * jax.random.uniform(streams_of[1], (CYCLES,), jnp.float32) ** block_scale(streams_of[1], (CYCLES,), ((0, 32),), -0.2, 0.2)), 0.5, 2.0),
        "cycle_len": draw_cycle_len(jax.random.fold_in(streams_of[6], 71), 0),
        "m_order": jax.random.permutation(streams_of[3], M).astype(jnp.int32),
        "legendre": centred(streams_of[4], (M, LB, CYCLES), 1.0, 4.0, ((0, 128),)),
        "band_start": jax.random.randint(streams_of[5], (1,), M // 4, M).astype(jnp.int32),
    }


RIDGE = 0.05

def cycle_angles(lengths, slot_count, step_count, stride):
    pixels = lax.broadcasted_iota(jnp.int32, (1, 1, slot_count), 2)
    orders = lax.broadcasted_iota(jnp.int32, (1, step_count, 1), 1)
    length = lengths.astype(jnp.int32)[:, None, None]
    half_turns = orders * stride * (2 * pixels + 1) % (2 * length)
    angles = half_turns.astype(jnp.float32) * (jnp.pi / length.astype(jnp.float32))
    return (jnp.cos(angles), jnp.sin(angles))

def cycle_tables(lengths, slot_count):
    phase_cos, phase_sin = cycle_angles(lengths, slot_count, MP, 1)
    block_cos, block_sin = cycle_angles(lengths, slot_count, M // MP, MP)
    return (phase_cos, phase_sin, jnp.stack([block_cos, block_sin], axis=1))

def cycle_analysis(weighted, tables):
    phase_cos, phase_sin, block_stack = tables
    stacked = jnp.stack([weighted[:, :, None, :] * phase_cos[None], -(weighted[:, :, None, :] * phase_sin[None])], axis=2)
    products = jnp.einsum('brjpk,rtqk->brjtpq', stacked, block_stack, precision=lax.Precision.HIGHEST)
    real_part = products[:, :, 0, 0] + products[:, :, 1, 1]
    imag_part = products[:, :, 1, 0] - products[:, :, 0, 1]
    joined = jnp.stack([real_part, imag_part], axis=2)
    return joined.reshape(joined.shape[0], joined.shape[1], 2, M)

def cycle_synthesis(natural, tables):
    phase_cos, phase_sin, block_stack = tables
    shaped = natural.reshape(natural.shape[0], natural.shape[1], 2, MP, M // MP)
    first = lax.broadcasted_iota(jnp.int32, (MP, M // MP), 0)
    second = lax.broadcasted_iota(jnp.int32, (MP, M // MP), 1)
    doubling = jnp.where((first == 0) & (second == 0), 1.0, 2.0).astype(jnp.float32)
    scaled = shaped * doubling
    from_real = jnp.einsum('brpq,rtqk->brtpk', scaled[:, :, 0], block_stack, precision=lax.Precision.HIGHEST)
    from_imag = jnp.einsum('brpq,rtqk->brtpk', scaled[:, :, 1], block_stack, precision=lax.Precision.HIGHEST)
    sum_real = from_real[:, :, 0] - from_imag[:, :, 1]
    sum_imag = from_real[:, :, 1] + from_imag[:, :, 0]
    return lax.optimization_barrier(jnp.sum(sum_real * phase_cos[None] - sum_imag * phase_sin[None], axis=2))

def keep_weight(my_orders, start_value):
    window = jnp.arange(LB, dtype=jnp.int32)
    degree = start_value + window
    needlet_taper = jnp.sin(jnp.pi * (window.astype(jnp.float32) + 0.5) / LB) / math.sqrt(LB)
    return jnp.where(degree[None, :] >= my_orders[:, None], needlet_taper[None, :], 0.0).astype(jnp.float32)

def unit_solve(factor):
    count = factor.shape[-1]
    forward = []
    for row_at in range(count):
        running = jnp.ones(factor.shape[:-2], jnp.float32)
        for col_at in range(row_at):
            running = running - factor[..., row_at, col_at] * forward[col_at]
        forward.append(running / factor[..., row_at, row_at])
    backward = [None] * count
    for row_at in reversed(range(count)):
        running = forward[row_at]
        for col_at in range(row_at + 1, count):
            running = running - factor[..., col_at, row_at] * backward[col_at]
        backward[row_at] = running / factor[..., row_at, row_at]
    return jnp.stack(backward, axis=-1)

def ilc_weights(raw_sums, counts):
    band_count = raw_sums.shape[-1]
    covariance = raw_sums / counts[:, None, None]
    trace_sum = jnp.trace(covariance, axis1=1, axis2=2)
    identity = jnp.eye(band_count, dtype=jnp.float32)
    regular = covariance + (RIDGE * trace_sum / band_count)[:, None, None] * identity
    factor = jnp.linalg.cholesky(regular)
    solved = unit_solve(factor)
    return solved / lax.optimization_barrier(jnp.sum(solved, axis=1, keepdims=True))

def reference(band_maps, cycle_weight, cycle_len, m_order, legendre, band_start):
    pixels = jnp.arange(RLEN, dtype=jnp.int32)
    inside = pixels[None, :] < cycle_len[:, None]
    weighted = jnp.where(inside[None], band_maps * cycle_weight[None, :, None], 0.0) / math.sqrt(CYCLES * RLEN)
    blocks_maps = weighted.reshape(BANDS, ND, DOM, RLEN).transpose(1, 0, 2, 3)
    blocks_len = cycle_len.reshape(ND, DOM)

    def analyse(pair):
        return cycle_analysis(pair[0], cycle_tables(pair[1], RLEN))
    coeff = lax.map(analyse, (blocks_maps, blocks_len))
    coeff = coeff.transpose(1, 0, 2, 3, 4).reshape(BANDS, CYCLES, 2, M)
    position = (m_order % MP * (M // MP) + m_order // MP).astype(jnp.int32)
    sent = jnp.take(coeff, position, axis=3).astype(jnp.bfloat16)
    slot_block = 8
    table_blocks = legendre.reshape(M // slot_block, slot_block, LB, CYCLES)
    coeff_blocks = jnp.moveaxis(sent.reshape(BANDS, CYCLES, 2, M // slot_block, slot_block), 3, 0)
    order_blocks = m_order.reshape(M // slot_block, slot_block)

    def harmonise(triple):
        table_part = triple[0].astype(jnp.float32)
        harmonic = jnp.einsum('mlr,brim->mbil', table_part, triple[1].astype(jnp.float32), precision=lax.Precision.HIGHEST)
        keep = keep_weight(triple[2], band_start[0])
        filtered = (harmonic * keep[:, None, None, :]).astype(jnp.bfloat16)
        return jnp.einsum('mlr,mbil->brim', table_part, filtered.astype(jnp.float32), precision=lax.Precision.HIGHEST)
    synthesis = lax.map(harmonise, (table_blocks, coeff_blocks, order_blocks))
    synthesis = jnp.moveaxis(synthesis, 0, 3).reshape(BANDS, CYCLES, 2, M)
    natural = jnp.take(synthesis, jnp.argsort(position).astype(jnp.int32), axis=3)
    natural_blocks = natural.reshape(BANDS, ND, DOM, 2, M).transpose(1, 0, 2, 3, 4)

    def synthesise(pair):
        return cycle_synthesis(pair[0], cycle_tables(pair[1], RLEN))
    needlet_raw = lax.map(synthesise, (natural_blocks, blocks_len))
    needlet_raw = needlet_raw.transpose(1, 0, 2, 3).reshape(BANDS, CYCLES, RLEN) / math.sqrt(M)
    needlet = jnp.where(inside[None], needlet_raw, 0.0).astype(jnp.bfloat16)
    needlet_wide = needlet.astype(jnp.float32).reshape(BANDS, ND, DOM, RLEN)
    raw_sums = jnp.einsum('bdrk,cdrk->dbc', needlet_wide, needlet_wide, precision=lax.Precision.HIGHEST)
    counts = lax.optimization_barrier(jnp.sum(cycle_len.reshape(ND, DOM), axis=1)).astype(jnp.float32)
    weights = ilc_weights(raw_sums, counts)
    clean = jnp.einsum('db,bdrk->drk', weights, needlet_wide, precision=lax.Precision.HIGHEST)
    return clean.reshape(CYCLES, RLEN)
```

```python
import functools
import math

import jax
import jax.numpy as jnp
from jax import lax
from jax.experimental import pallas as pl
from jax.experimental.pallas import tpu as pltpu
from jax.sharding import PartitionSpec as P

BANDS = 16
M = 1024
LB = 1024
DOM = 4
RIDGE = 0.05
QUARTER = 256
NDEV = 128
BPD = 4
RPD = 16
GROUPS = 2 * BPD
SLOTS = 8
MESH = pl.DeviceIdType.MESH
BF = jnp.bfloat16
F32 = jnp.float32
BACK = jnp.float32
NT = (((1,), (1,)), ((), ()))
NN = (((1,), (0,)), ((), ()))


def mm(a, b, dims, precision=None):
    return lax.dot_general(a, b, dims, precision=precision, preferred_element_type=F32)


def split(x):
    hi = x.astype(BF)
    return hi, (x - hi.astype(F32)).astype(BF)


def trig_tables(order, length):
    pixel = lax.broadcasted_iota(jnp.int32, order.shape, 1)
    turns = order * (2 * pixel + 1).astype(F32)
    lf = jnp.full((1, QUARTER), length, jnp.int32).astype(F32)
    quarter = 0.5 * lf
    count = jnp.floor(turns * (1.0 / quarter) + 0.5)
    y = (turns - count * quarter) * (math.pi / lf)
    z = y * y
    s = ((-1.9515295891e-4 * z + 8.3321608736e-3) * z - 1.6666654611e-1) * z * y + y
    c = ((2.443315711809948e-5 * z - 1.388731625493765e-3) * z + 4.166664568298827e-2) * (z * z) - 0.5 * z + 1.0
    quad = count - 4.0 * jnp.floor(count * 0.25)
    upper = quad >= 2.0
    odd = (quad == 1.0) | (quad == 3.0)
    sin = jnp.where(odd, c, s)
    cos = jnp.where(odd, s, c)
    sin = jnp.where(upper, -sin, sin)
    cos = jnp.where((quad == 1.0) | (quad == 2.0), -cos, cos)
    return cos, sin


def order_rows():
    row = lax.broadcasted_iota(jnp.int32, (32, QUARTER), 0)
    inner = (4 * (row % 8) + row // 8).astype(F32)
    outer = (32 * row).astype(F32)
    return inner, outer


def reversal():
    row = lax.broadcasted_iota(jnp.int32, (QUARTER, QUARTER), 0)
    col = lax.broadcasted_iota(jnp.int32, (QUARTER, QUARTER), 1)
    return jnp.where(row + col == QUARTER - 1, 1.0, 0.0).astype(F32)


def analysis_kernel(len_ref, weight_ref, x_ref, mcol_ref, out_ref, xs, xr, cs):
    flip = reversal()
    for tile in range(8):
        xs[tile] = x_ref[:, tile * 128:tile * 128 + 128]
    for tile in (8, 9):
        xs[tile] = jnp.zeros((BPD * RPD, 128), F32)
        xr[tile] = jnp.zeros((BPD * RPD, 128), F32)
    for block in range(4):
        turned = mm(x_ref[:, block * QUARTER:(block + 1) * QUARTER], flip, NN, lax.Precision.HIGHEST)
        xr[6 - 2 * block] = turned[:, 0:128]
        xr[7 - 2 * block] = turned[:, 128:256]
    inner, outer = order_rows()
    lane = lax.broadcasted_iota(jnp.int32, (BPD, 128), 1)
    pixel = lax.broadcasted_iota(jnp.int32, (BPD, QUARTER), 1)
    group = lax.broadcasted_iota(jnp.int32, (8, 128), 1) // 32

    def window(ref, r, offset):
        tile = offset // 128
        rest = offset - tile * 128
        shift = lax.rem(128 - rest, 128)
        pieces = [
            pltpu.roll(ref[tile + i, pl.ds(r, BPD, stride=RPD), :], shift, 1) for i in range(3)
        ]
        keep = lane < 128 - rest
        return jnp.concatenate(
            [jnp.where(keep, pieces[0], pieces[1]), jnp.where(keep, pieces[1], pieces[2])], axis=1
        )

    def one(r, carry):
        length = len_ref[r]
        quarter = length // 4
        scale = weight_ref[r] * (1.0 / math.sqrt(512 * 1024))
        inside = pixel < quarter
        x0 = jnp.concatenate([xs[i, pl.ds(r, BPD, stride=RPD), :] for i in range(2)], axis=1)
        x1 = window(xr, r, 1024 - length // 2)
        x2 = window(xs, r, length // 2)
        x3 = window(xr, r, 1024 - length)
        x0, x1, x2, x3 = [jnp.where(inside, v, 0.0) * scale for v in (x0, x1, x2, x3)]
        even = ((x0 + x3) + (x1 + x2), (x0 + x3) - (x1 + x2))
        odd = ((x0 - x3) - (x1 - x2), (x0 - x3) + (x1 - x2))
        cos_p, sin_p = trig_tables(inner, length)
        cos_q, sin_q = trig_tables(outer, length)
        cqh, cql = [jnp.concatenate([v] * 4, axis=0) for v in split(cos_q)]
        sqh, sql = [jnp.concatenate([v] * 4, axis=0) for v in split(sin_q)]

        def rows(pair, table):
            parts = []
            for b in range(BPD):
                for c in range(4):
                    source = pair[c % 2][b:b + 1]
                    parts.append(jnp.broadcast_to(source, (8, QUARTER)) * table[c * 8:c * 8 + 8])
            return split(jnp.concatenate(parts, axis=0))

        ech, ecl = rows(even, cos_p)
        esh, esl = rows(even, -sin_p)
        och, ocl = rows(odd, -cos_p)
        osh, osl = rows(odd, -sin_p)
        right_c = jnp.concatenate([cqh, cql, cqh], axis=1)
        right_s = jnp.concatenate([sqh, sql, sqh], axis=1)
        real = mm(jnp.concatenate([ech, ech, ecl], axis=1), right_c, NT) + mm(
            jnp.concatenate([esh, esh, esl], axis=1), right_s, NT
        )
        imag = mm(jnp.concatenate([och, och, ocl], axis=1), right_s, NT) + mm(
            jnp.concatenate([osh, osh, osl], axis=1), right_c, NT
        )
        for b in range(BPD):
            for part, val in enumerate((real, imag)):
                v = [val[b * 32 + c * 8:b * 32 + c * 8 + 8] for c in range(4)]
                picked = jnp.where(group == 0, v[0], jnp.where(group == 1, v[1], jnp.where(group == 2, v[2], v[3])))
                at = pl.multiple_of(((b * 2 + part) * RPD + r) * 8, 8)
                cs[pl.ds(at, 8), :] = picked
        return carry

    lax.fori_loop(0, RPD, one, 0)
    flat = jnp.concatenate([cs[pl.ds(a, 128, stride=8), :].astype(BF) for a in range(8)], axis=1)
    for block in range(8):
        target = mcol_ref[block * 128:block * 128 + 128, :]
        col = lax.broadcasted_iota(jnp.int32, (128, M), 1)
        hot = jnp.where(col == target, 1.0, 0.0).astype(BF)
        moved = mm(hot, flat, NT)
        out_ref[block * 16:block * 16 + 16] = moved.reshape(16, SLOTS, 128).astype(BF)


def analysis(cycle_len, cycle_weight, maps, mcol):
    vmem = pl.BlockSpec(memory_space=pltpu.VMEM)
    smem = pl.BlockSpec(memory_space=pltpu.SMEM)
    return pl.pallas_call(
        analysis_kernel,
        out_shape=jax.ShapeDtypeStruct((NDEV, SLOTS, 128), BF),
        in_specs=[smem, smem, vmem, vmem],
        out_specs=vmem,
        scratch_shapes=[
            pltpu.VMEM((10, BPD * RPD, 128), F32),
            pltpu.VMEM((10, BPD * RPD, 128), F32),
            pltpu.VMEM((M, 128), F32),
        ],
        compiler_params=pltpu.CompilerParams(vmem_limit_bytes=48 << 20),
        name="analysis",
    )(cycle_len, cycle_weight, maps, mcol)


def peer(offset):
    sky = lax.axis_index("sky")
    band = lax.axis_index("band")
    me = sky * 4 + band
    other = lax.rem(me + offset, NDEV)
    return me, other, (other // 4, lax.rem(other, 4))


def swap_blocks(rows, lane_group):
    rows = list(rows)
    for bit in (1, 2, 4):
        low = (lane_group // bit) % 2 == 0
        for i in range(8):
            if i & bit:
                continue
            a, b = rows[i], rows[i + bit]
            rows[i] = jnp.where(low, a, pltpu.roll(b, 16 * bit, 1))
            rows[i + bit] = jnp.where(low, pltpu.roll(a, 128 - 16 * bit, 1), b)
    return rows


def middle_kernel(order_ref, start_ref, taper_ref, msg_ref, leg_hbm, out_ref, leg, arrived, xs, ys, back,
                  leg_sem, local_sem, send_sem, recv_sem, send_sem2, recv_sem2):
    barrier = pltpu.get_barrier_semaphore()

    def greet(i, carry):
        pl.semaphore_signal(barrier, inc=1, device_id=peer(i)[2], device_id_type=MESH)
        return carry

    lax.fori_loop(1, NDEV, greet, 0)
    loads = [pltpu.make_async_copy(leg_hbm.at[i], leg.at[i], leg_sem.at[i]) for i in range(SLOTS)]
    for load in loads:
        load.start()
    me = peer(0)[0]
    own = pltpu.make_async_copy(msg_ref.at[me], arrived.at[me], local_sem)
    own.start()
    pl.semaphore_wait(barrier, NDEV - 1)

    def send_out(i, carry):
        mine, other, device = peer(i)
        pltpu.make_async_remote_copy(
            src_ref=msg_ref.at[other], dst_ref=arrived.at[mine], send_sem=send_sem, recv_sem=recv_sem,
            device_id=device, device_id_type=MESH,
        ).start()
        return carry

    lax.fori_loop(1, NDEV, send_out, 0)
    own.wait()
    everything = pltpu.make_async_remote_copy(
        src_ref=msg_ref.at[pl.ds(0, NDEV - 1)], dst_ref=arrived.at[pl.ds(0, NDEV - 1)], send_sem=send_sem,
        recv_sem=recv_sem, device_id=peer(1)[2], device_id_type=MESH,
    )
    everything.wait_recv()

    lane_group = lax.broadcasted_iota(jnp.int32, (SLOTS, 128), 1) // 16
    for tile in range(4):
        for band in range(4):
            got = [arrived[(tile * 8 + i) * 4 + band].astype(F32) for i in range(8)]
            for g, val in enumerate(swap_blocks(got, lane_group)):
                xs[tile, (band * GROUPS + g) * 8:(band * GROUPS + g) * 8 + 8, :] = val
    degree = lax.broadcasted_iota(jnp.int32, (1, LB), 1) + start_ref[0]
    for m in range(SLOTS):
        keep = jnp.where(degree >= order_ref[me * SLOTS + m], taper_ref[...], 0.0)
        coeff = jnp.concatenate(
            [xs[tile, pl.ds(m, 4 * GROUPS, stride=8), :].astype(BF) for tile in range(4)], axis=1
        )
        loads[m].wait()
        table = leg[m]
        harmonic = mm(coeff, table, NT)
        filtered = (harmonic * keep).astype(BF)
        result = mm(filtered, table, NN)
        for tile in range(4):
            ys[tile, pl.ds(m, 4 * GROUPS, stride=8), :] = result[:, tile * 128:tile * 128 + 128]
    for tile in range(4):
        for band in range(4):
            done = [ys[tile, (band * GROUPS + g) * 8:(band * GROUPS + g) * 8 + 8, :] for g in range(GROUPS)]
            for i, val in enumerate(swap_blocks(done, lane_group)):
                back[(tile * 8 + i) * 4 + band] = val.astype(back.dtype)

    own2 = pltpu.make_async_copy(back.at[me], out_ref.at[me], local_sem)
    own2.start()

    def send_back(i, carry):
        mine, other, device = peer(i)
        pltpu.make_async_remote_copy(
            src_ref=back.at[other], dst_ref=out_ref.at[mine], send_sem=send_sem2, recv_sem=recv_sem2,
            device_id=device, device_id_type=MESH,
        ).start()
        return carry

    lax.fori_loop(1, NDEV, send_back, 0)
    own2.wait()
    everything.wait_send()
    returned = pltpu.make_async_remote_copy(
        src_ref=back.at[pl.ds(0, NDEV - 1)], dst_ref=out_ref.at[pl.ds(0, NDEV - 1)], send_sem=send_sem2,
        recv_sem=recv_sem2, device_id=peer(1)[2], device_id_type=MESH,
    )
    returned.wait_recv()
    returned.wait_send()


def middle(order, start, taper, messages, legendre):
    vmem = pl.BlockSpec(memory_space=pltpu.VMEM)
    smem = pl.BlockSpec(memory_space=pltpu.SMEM)
    return pl.pallas_call(
        middle_kernel,
        out_shape=jax.ShapeDtypeStruct((NDEV, SLOTS, 128), BACK),
        in_specs=[smem, smem, vmem, vmem, pl.BlockSpec(memory_space=pl.ANY)],
        out_specs=vmem,
        scratch_shapes=[
            pltpu.VMEM((SLOTS, LB, 512), BF),
            pltpu.VMEM((NDEV, SLOTS, 128), BF),
            pltpu.VMEM((4, 4 * GROUPS * SLOTS, 128), F32),
            pltpu.VMEM((4, 4 * GROUPS * SLOTS, 128), F32),
            pltpu.VMEM((NDEV, SLOTS, 128), BACK),
            pltpu.SemaphoreType.DMA((SLOTS,)),
            pltpu.SemaphoreType.DMA,
            pltpu.SemaphoreType.DMA,
            pltpu.SemaphoreType.DMA,
            pltpu.SemaphoreType.DMA,
            pltpu.SemaphoreType.DMA,
        ],
        compiler_params=pltpu.CompilerParams(
            collective_id=0, has_side_effects=True, vmem_limit_bytes=48 << 20
        ),
        name="middle",
    )(order, start, taper, messages, legendre)


def synthesis_kernel(len_ref, back_ref, mcol_ref, out_ref, ss, nq, buf, nd):
    flip = reversal().astype(BF)
    turned = jnp.concatenate(
        [back_ref[d * 16:d * 16 + 16].astype(F32).reshape(128, 128).T for d in range(8)], axis=1
    )
    stacked = jnp.concatenate(split(turned), axis=0)
    lane1 = lax.broadcasted_iota(jnp.int32, (128, 128), 1)
    for pair in range(4):
        col = lax.broadcasted_iota(jnp.int32, (M, QUARTER), 1) + pair * QUARTER
        hot = jnp.where(col == mcol_ref[...], 1.0, 0.0).astype(BF)
        moved = mm(stacked, hot, NN)
        natural = (moved[0:128] + moved[128:256]) * (2.0 / math.sqrt(M))
        for half in range(2):
            a = pair * 2 + half
            val = natural[:, half * 128:half * 128 + 128]
            if a == 0:
                val = jnp.where(lane1 == 0, 0.5 * val, val)
            ss[pl.ds(a, 128, stride=8), :] = val
    inner, outer = order_rows()
    group = lax.broadcasted_iota(jnp.int32, (8, 128), 1) // 32
    pixel = lax.broadcasted_iota(jnp.int32, (BPD, QUARTER), 1)

    def one(r, carry):
        length = len_ref[r]
        cos_p, sin_p = trig_tables(inner, length)
        cos_q, sin_q = trig_tables(outer, length)
        th, tl = split(jnp.concatenate([cos_q, sin_q], axis=1))
        th = jnp.concatenate([th] * 4, axis=0)
        tl = jnp.concatenate([tl] * 4, axis=0)
        parts = []
        for g in range(GROUPS):
            at = pl.multiple_of((g * RPD + r) * 8, 8)
            v = ss[pl.ds(at, 8), :]
            for c in range(4):
                parts.append(jnp.where(group == c, v, 0.0))
        hi, lo = split(jnp.concatenate(parts, axis=0))
        full = mm(jnp.concatenate([hi, lo], axis=1), jnp.concatenate([th, th], axis=0), NN) + mm(hi, tl, NN)
        quarters = [[], [], [], []]
        for b in range(BPD):
            re = full[(2 * b) * 32:(2 * b) * 32 + 32]
            im = full[(2 * b + 1) * 32:(2 * b + 1) * 32 + 32]
            even = cos_p * re[:, :QUARTER] - sin_p * re[:, QUARTER:]
            odd = cos_p * im[:, QUARTER:] + sin_p * im[:, :QUARTER]
            ce, co = even[0:8] + even[16:24], even[8:16] + even[24:32]
            de, do = odd[0:8] + odd[16:24], odd[8:16] + odd[24:32]
            for i, total in enumerate((ce + co - de - do, ce - co + de - do, ce - co - de + do, ce + co + de + do)):
                quarters[i].append(jnp.sum(total, axis=0, keepdims=True))
        inside = pixel < length // 4
        for i in range(4):
            val = jnp.where(inside, jnp.concatenate(quarters[i], axis=0), 0.0)
            nq[i, r] = val.astype(BF).astype(F32)
        return carry

    lax.fori_loop(0, RPD, one, 0)
    for i in (1, 3):
        whole = nq[i].reshape(RPD * BPD, QUARTER).astype(BF)
        nq[i] = mm(whole, flip, NN).reshape(RPD, BPD, QUARTER)
    lane = lax.broadcasted_iota(jnp.int32, (BPD, 128), 1)

    def place(r, carry):
        length = len_ref[r]
        for tile in range(14):
            buf[tile] = jnp.zeros((BPD, 128), F32)
        first = nq[0, r]
        buf[2] = first[:, :128]
        buf[3] = first[:, 128:]
        for i, offset in ((1, length // 2), (2, length // 2 + QUARTER), (3, length)):
            tile = offset // 128
            rest = offset - tile * 128
            val = nq[i, r]
            low = pltpu.roll(val[:, :128], rest, 1)
            high = pltpu.roll(val[:, 128:], rest, 1)
            wrapped = lane < rest
            buf[tile] += jnp.where(wrapped, 0.0, low)
            buf[tile + 1] += jnp.where(wrapped, low, high)
            buf[tile + 2] += jnp.where(wrapped, high, 0.0)
        for tile in range(8):
            nd[tile, pl.ds(r, BPD, stride=RPD), :] = buf[tile + 2]
        return carry

    lax.fori_loop(0, RPD, place, 0)
    for t in range(4):
        out_ref[t] = jnp.concatenate([nd[2 * t], nd[2 * t + 1]], axis=1).astype(BF)


def synthesis(cycle_len, returned, mcol):
    vmem = pl.BlockSpec(memory_space=pltpu.VMEM)
    smem = pl.BlockSpec(memory_space=pltpu.SMEM)
    return pl.pallas_call(
        synthesis_kernel,
        out_shape=jax.ShapeDtypeStruct((4, BPD * RPD, QUARTER), BF),
        in_specs=[smem, vmem, vmem],
        out_specs=vmem,
        scratch_shapes=[
            pltpu.VMEM((M, 128), F32),
            pltpu.VMEM((4, RPD, BPD, QUARTER), F32),
            pltpu.VMEM((14, BPD, 128), F32),
            pltpu.VMEM((8, BPD * RPD, 128), F32),
        ],
        compiler_params=pltpu.CompilerParams(vmem_limit_bytes=48 << 20),
        name="synthesis",
    )(cycle_len, returned, mcol)


def combine_kernel(len_ref, nd_ref, out_ref, got, wide, part, parts, local_sem, send_sem, recv_sem, send_sem2, recv_sem2):
    sky = lax.axis_index("sky")
    band = lax.axis_index("band")
    others = [lax.rem(band + i, 4) for i in range(1, 4)]
    barrier = pltpu.get_barrier_semaphore()
    for other in others:
        pl.semaphore_signal(barrier, inc=1, device_id=(sky, other), device_id_type=MESH)
    own = pltpu.make_async_copy(nd_ref.at[band], got.at[band], local_sem)
    own.start()
    pl.semaphore_wait(barrier, 3)
    copies = []
    for i, other in enumerate(others):
        copy = pltpu.make_async_remote_copy(
            src_ref=nd_ref.at[other], dst_ref=got.at[band], send_sem=send_sem.at[i], recv_sem=recv_sem.at[i],
            device_id=(sky, other), device_id_type=MESH,
        )
        copy.start()
        copies.append(copy)
    own.wait()
    for copy in copies:
        copy.wait()
    for t in range(4):
        val = got[t].astype(F32)
        for half in range(2):
            wide[half, t * BPD * RPD:(t + 1) * BPD * RPD, :] = val[:, half * 128:half * 128 + 128]
    pixels = [[wide[half, pl.ds(r, BANDS, stride=RPD), :] for half in range(2)] for r in range(RPD)]
    gram = jnp.zeros((BANDS, 128), F32)
    for d in range(4):
        x = jnp.concatenate([v for r in range(DOM) for v in pixels[d * DOM + r]], axis=1).astype(BF)
        x = jnp.concatenate([x, jnp.zeros((128 - BANDS, x.shape[1]), BF)], axis=0)
        block = mm(x[:BANDS], x, NT)
        gram = gram + (pltpu.roll(block, 32 * d, 1) if d else block)
    part[...] = gram
    copies = []
    for i, other in enumerate(others):
        copy = pltpu.make_async_remote_copy(
            src_ref=part, dst_ref=parts.at[i], send_sem=send_sem2.at[i], recv_sem=recv_sem2.at[i],
            device_id=(sky, other), device_id_type=MESH,
        )
        copy.start()
        copies.append(copy)
    for copy in copies:
        copy.wait()
    here = [gram] + [parts[i] for i in range(3)]
    total = jnp.zeros((BANDS, 128), F32)
    for source in range(4):
        step = lax.rem(band - source + 4, 4)
        chosen = here[0]
        for i in range(1, 4):
            chosen = jnp.where(step == i, here[i], chosen)
        total = total + chosen
    row = lax.broadcasted_iota(jnp.int32, (BANDS, 128), 0)
    col = lax.broadcasted_iota(jnp.int32, (BANDS, 128), 1)
    for d in range(4):
        count = len_ref[d * DOM] + len_ref[d * DOM + 1] + len_ref[d * DOM + 2] + len_ref[d * DOM + 3]
        cov = pltpu.roll(total, 128 - 32 * d, 1) if d else total
        cov = cov / jnp.full((1, 128), count, jnp.int32).astype(F32)
        diagonal = jnp.where(row == col, cov, 0.0)
        trace = jnp.sum(jnp.sum(diagonal, axis=1, keepdims=True), axis=0, keepdims=True)
        work = jnp.where(col < BANDS, cov, 0.0) + jnp.where(row == col, (RIDGE / BANDS) * trace, 0.0)
        work = jnp.where(col == BANDS, 1.0, work)
        for j in range(BANDS):
            pivot = work[j:j + 1, :] / work[j:j + 1, j:j + 1]
            work = jnp.where(row == j, pivot, work - work[:, j:j + 1] * pivot)
        solved = work[:, BANDS:BANDS + 1]
        weights = solved / jnp.sum(solved, axis=0, keepdims=True)
        for r in range(DOM):
            at = d * DOM + r
            clean = [jnp.sum(weights * v, axis=0, keepdims=True) for v in pixels[at]]
            out_ref[at:at + 1, :] = jnp.concatenate(clean, axis=1)


def combine(cycle_len, blocks):
    vmem = pl.BlockSpec(memory_space=pltpu.VMEM)
    smem = pl.BlockSpec(memory_space=pltpu.SMEM)
    return pl.pallas_call(
        combine_kernel,
        out_shape=jax.ShapeDtypeStruct((RPD, QUARTER), F32),
        in_specs=[smem, vmem],
        out_specs=vmem,
        scratch_shapes=[
            pltpu.VMEM((4, BPD * RPD, QUARTER), BF),
            pltpu.VMEM((2, 4 * BPD * RPD, 128), F32),
            pltpu.VMEM((BANDS, 128), F32),
            pltpu.VMEM((3, BANDS, 128), F32),
            pltpu.SemaphoreType.DMA,
            pltpu.SemaphoreType.DMA((3,)),
            pltpu.SemaphoreType.DMA((3,)),
            pltpu.SemaphoreType.DMA((3,)),
            pltpu.SemaphoreType.DMA((3,)),
        ],
        compiler_params=pltpu.CompilerParams(collective_id=1, has_side_effects=True),
        name="combine",
    )(cycle_len, blocks)


def on_device(band_maps, cycle_weight, cycle_len, m_order, legendre, band_start):
    target = (m_order % 32 // 4 * 128 + m_order % 4 * 32 + m_order // 32)[:, None]
    window = jnp.arange(LB, dtype=jnp.int32).astype(F32)
    taper = (jnp.sin(jnp.pi * (window + 0.5) / LB) / math.sqrt(LB))[None]
    messages = analysis(cycle_len, cycle_weight, band_maps.reshape(BPD * RPD, 4 * QUARTER), target)
    returned = middle(m_order, band_start, taper, messages, legendre)
    blocks = synthesis(cycle_len, returned, target)
    return combine(cycle_len, blocks)


def solution(mesh):
    placed = (P("band", "sky", None), P("sky"), P("sky"), P(), P(("sky", "band"), None, None), P())
    return jax.shard_map(
        on_device, mesh=mesh, in_specs=placed, out_specs=P("sky", "band"), check_vma=False
    )
```

```python
import functools
import math

import jax
import jax.numpy as jnp
from jax import lax
from jax.experimental import pallas as pl
from jax.experimental.pallas import tpu as pltpu
from jax.sharding import PartitionSpec as P

BANDS = 16
M = 1024
LB = 1024
DOM = 4
RIDGE = 0.05
QUARTER = 256
NDEV = 128
BPD = 4
RPD = 16
GROUPS = 2 * BPD
SLOTS = 8
MESH = pl.DeviceIdType.MESH
BF = jnp.bfloat16
F32 = jnp.float32
BACK = jnp.float32
NT = (((1,), (1,)), ((), ()))
NN = (((1,), (0,)), ((), ()))


def mm(a, b, dims, precision=None):
    return lax.dot_general(a, b, dims, precision=precision, preferred_element_type=F32)


def split(x):
    hi = x.astype(BF)
    return hi, (x - hi.astype(F32)).astype(BF)


def trig_tables(order, length):
    pixel = lax.broadcasted_iota(jnp.int32, order.shape, 1)
    turns = order * (2 * pixel + 1).astype(F32)
    lf = jnp.full((1, QUARTER), length, jnp.int32).astype(F32)
    quarter = 0.5 * lf
    count = jnp.floor(turns * (1.0 / quarter) + 0.5)
    y = (turns - count * quarter) * (math.pi / lf)
    z = y * y
    s = ((-1.9515295891e-4 * z + 8.3321608736e-3) * z - 1.6666654611e-1) * z * y + y
    c = ((2.443315711809948e-5 * z - 1.388731625493765e-3) * z + 4.166664568298827e-2) * (z * z) - 0.5 * z + 1.0
    quad = count - 4.0 * jnp.floor(count * 0.25)
    upper = quad >= 2.0
    odd = (quad == 1.0) | (quad == 3.0)
    sin = jnp.where(odd, c, s)
    cos = jnp.where(odd, s, c)
    sin = jnp.where(upper, -sin, sin)
    cos = jnp.where((quad == 1.0) | (quad == 2.0), -cos, cos)
    return cos, sin


def order_rows():
    row = lax.broadcasted_iota(jnp.int32, (32, QUARTER), 0)
    inner = (4 * (row % 8) + row // 8).astype(F32)
    outer = (32 * row).astype(F32)
    return inner, outer


def reversal():
    row = lax.broadcasted_iota(jnp.int32, (QUARTER, QUARTER), 0)
    col = lax.broadcasted_iota(jnp.int32, (QUARTER, QUARTER), 1)
    return jnp.where(row + col == QUARTER - 1, 1.0, 0.0).astype(F32)


def window_taper(window):
    turns = 2.0 * window + 1.0
    count = jnp.floor(turns * (1.0 / LB) + 0.5)
    y = (turns - count * LB) * (math.pi / (2 * LB))
    z = y * y
    s = ((-1.9515295891e-4 * z + 8.3321608736e-3) * z - 1.6666654611e-1) * z * y + y
    c = ((2.443315711809948e-5 * z - 1.388731625493765e-3) * z + 4.166664568298827e-2) * (z * z) - 0.5 * z + 1.0
    return jnp.where(count == 0.0, s, jnp.where(count == 1.0, c, -s))


def swap_blocks(rows, lane_group):
    rows = list(rows)
    for bit in (1, 2, 4):
        low = (lane_group // bit) % 2 == 0
        for i in range(8):
            if i & bit:
                continue
            a, b = rows[i], rows[i + bit]
            rows[i] = jnp.where(low, a, pltpu.roll(b, 16 * bit, 1))
            rows[i + bit] = jnp.where(low, pltpu.roll(a, 128 - 16 * bit, 1), b)
    return rows


def whole_kernel(
    maps_hbm, weight_hbm, len_hbm, order_hbm, order_rows_hbm, leg_hbm, start_hbm, out_ref,
    maps, weight, length_of, order, order_vec, start, leg,
    xs, xr, cs, tp, th, tl, hot, msg, arrived, hx, hy, back, returned, nq, pb, nd, ndb, got, wide, part, parts,
    small_sem, leg_sem, local_sem, send_sem, recv_sem, pix_send, pix_recv, cov_send, cov_recv,
):
    sky = lax.axis_index("sky")
    band = lax.axis_index("band")
    me = sky * 4 + band
    bands = [band] + [lax.rem(band + j, 4) for j in range(1, 4)]
    others = bands[1:]

    small = [
        pltpu.make_async_copy(src, dst, small_sem.at[i])
        for i, (src, dst) in enumerate((
            (maps_hbm, maps), (len_hbm, length_of), (weight_hbm, weight), (order_rows_hbm, order_vec),
            (order_hbm, order), (start_hbm, start),
        ))
    ]
    for copy in small:
        copy.start()
    loads = [pltpu.make_async_copy(leg_hbm.at[i], leg.at[i], leg_sem.at[i]) for i in range(SLOTS)]
    for copy in loads:
        copy.start()

    barrier = pltpu.get_barrier_semaphore()

    def greet(i):
        row = lax.rem(sky + i, 32)
        for column in bands:
            pl.semaphore_signal(barrier, inc=1, device_id=(row, column), device_id_type=MESH)

    for column in others:
        pl.semaphore_signal(barrier, inc=1, device_id=(sky, column), device_id_type=MESH)
    greet(1)

    flip = reversal()
    for copy in small:
        copy.wait()
    for tile in range(8):
        xs[tile] = maps[:, tile * 128:tile * 128 + 128]
    for tile in (8, 9, 10):
        xs[tile] = jnp.zeros((BPD * RPD, 128), F32)
        xr[tile] = jnp.zeros((BPD * RPD, 128), F32)
    for block in range(4):
        turned = mm(maps[:, block * QUARTER:(block + 1) * QUARTER], flip, NN, lax.Precision.HIGHEST)
        xr[6 - 2 * block] = turned[:, 0:128]
        xr[7 - 2 * block] = turned[:, 128:256]
    inner, outer = order_rows()
    lane4 = lax.broadcasted_iota(jnp.int32, (BPD, 128), 1)
    pixel = lax.broadcasted_iota(jnp.int32, (BPD, QUARTER), 1)
    quad_group = lax.broadcasted_iota(jnp.int32, (8, 128), 1) // 32

    def window(ref, r, offset):
        tile = offset // 128
        rest = offset - tile * 128
        shift = lax.rem(128 - rest, 128)
        pieces = [pltpu.roll(ref[tile + i, pl.ds(r, BPD, stride=RPD), :], shift, 1) for i in range(3)]
        keep = lane4 < 128 - rest
        return jnp.concatenate(
            [jnp.where(keep, pieces[0], pieces[1]), jnp.where(keep, pieces[1], pieces[2])], axis=1
        )

    def analyse(r, carry):
        length = length_of[r]
        scale = weight[r] * (1.0 / math.sqrt(512 * 1024))
        inside = pixel < length // 4
        x0 = jnp.concatenate([xs[i, pl.ds(r, BPD, stride=RPD), :] for i in range(2)], axis=1)
        x1 = window(xr, r, 1024 - length // 2)
        x2 = window(xs, r, length // 2)
        x3 = window(xr, r, 1024 - length)
        x0, x1, x2, x3 = [jnp.where(inside, v, 0.0) * scale for v in (x0, x1, x2, x3)]
        even = ((x0 + x3) + (x1 + x2), (x0 + x3) - (x1 + x2))
        odd = ((x0 - x3) - (x1 - x2), (x0 - x3) + (x1 - x2))
        cos_p, sin_p = trig_tables(inner, length)
        cos_q, sin_q = trig_tables(outer, length)
        ch, cl = split(cos_q)
        sh, sl = split(sin_q)
        tp[r, 0:32, :] = cos_p
        tp[r, 32:64, :] = sin_p
        th[r] = jnp.concatenate([ch, sh], axis=1)
        tl[r] = jnp.concatenate([cl, sl], axis=1)
        cqh, cql, sqh, sql = [jnp.concatenate([v] * 4, axis=0) for v in (ch, cl, sh, sl)]

        def rows(pair, table):
            pieces = []
            for b in range(BPD):
                for c in range(4):
                    source = pair[c % 2][b:b + 1]
                    pieces.append(jnp.broadcast_to(source, (8, QUARTER)) * table[c * 8:c * 8 + 8])
            return split(jnp.concatenate(pieces, axis=0))

        ech, ecl = rows(even, cos_p)
        esh, esl = rows(even, -sin_p)
        och, ocl = rows(odd, -cos_p)
        osh, osl = rows(odd, -sin_p)
        right_c = jnp.concatenate([cqh, cql, cqh], axis=1)
        right_s = jnp.concatenate([sqh, sql, sqh], axis=1)
        real = mm(jnp.concatenate([ech, ech, ecl], axis=1), right_c, NT) + mm(
            jnp.concatenate([esh, esh, esl], axis=1), right_s, NT
        )
        imag = mm(jnp.concatenate([och, och, ocl], axis=1), right_s, NT) + mm(
            jnp.concatenate([osh, osh, osl], axis=1), right_c, NT
        )
        for b in range(BPD):
            for half, val in enumerate((real, imag)):
                v = [val[b * 32 + c * 8:b * 32 + c * 8 + 8] for c in range(4)]
                picked = jnp.where(
                    quad_group == 0, v[0], jnp.where(quad_group == 1, v[1], jnp.where(quad_group == 2, v[2], v[3]))
                )
                at = pl.multiple_of(((b * 2 + half) * RPD + r) * 8, 8)
                cs[pl.ds(at, 8), :] = picked
        return carry

    def analyse_four(i, carry):
        for j in range(4):
            analyse(4 * i + j, carry)
        return carry

    lax.fori_loop(2, 32, lambda i, carry: (greet(i), carry)[1], 0)
    lax.fori_loop(0, RPD // 4, analyse_four, 0)

    flat = jnp.concatenate([cs[pl.ds(a, 128, stride=8), :].astype(BF) for a in range(8)], axis=1)
    slots = order_vec[...]
    where_to = (slots % 32 // 4 * 128 + slots % 4 * 32 + slots // 32).astype(F32)
    lane128 = lax.broadcasted_iota(jnp.int32, (128, 128), 1).astype(F32)
    for block in range(8):
        target = jnp.broadcast_to(where_to[block:block + 1], (128, 128)).T
        row_hot = jnp.concatenate(
            [jnp.where(target == lane128 + 128.0 * a, 1.0, 0.0).astype(BF) for a in range(8)], axis=1
        )
        hot[block * 128:block * 128 + 128, :] = row_hot
        moved = mm(row_hot, flat, NT)
        msg[block * 16:block * 16 + 16] = moved.reshape(16, SLOTS, 128).astype(BF)

    own = pltpu.make_async_copy(msg.at[me], arrived.at[me], local_sem)
    own.start()
    pl.semaphore_wait(barrier, NDEV - 1)

    def everyone(src, dst, phase):
        def one(row, column):
            pltpu.make_async_remote_copy(
                src_ref=src.at[row * 4 + column], dst_ref=dst.at[me], send_sem=send_sem.at[phase],
                recv_sem=recv_sem.at[phase], device_id=(row, column), device_id_type=MESH,
            ).start()

        for column in others:
            one(sky, column)

        def rows(i, carry):
            row = lax.rem(sky + i, 32)
            for column in bands:
                one(row, column)
            return carry

        lax.fori_loop(1, 32, rows, 0)
        return pltpu.make_async_remote_copy(
            src_ref=src.at[pl.ds(0, NDEV - 1)], dst_ref=dst.at[pl.ds(0, NDEV - 1)], send_sem=send_sem.at[phase],
            recv_sem=recv_sem.at[phase], device_id=(sky, others[0]), device_id_type=MESH,
        )

    out_copies = everyone(msg, arrived, 0)
    window_at = lax.broadcasted_iota(jnp.int32, (8, LB), 1).astype(F32)
    taper = window_taper(window_at)[0:1] * (1.0 / math.sqrt(LB))
    degree = lax.broadcasted_iota(jnp.int32, (1, LB), 1) + start[0]
    own.wait()
    out_copies.wait_recv()

    lane_group = lax.broadcasted_iota(jnp.int32, (SLOTS, 128), 1) // 16
    for tile in range(4):
        for source in range(4):
            here = [arrived[(tile * 8 + i) * 4 + source].astype(F32) for i in range(8)]
            for g, val in enumerate(swap_blocks(here, lane_group)):
                at = (source * GROUPS + g) * 8
                hx[tile, at:at + 8, :] = val
    for m in range(SLOTS):
        keep = jnp.where(degree >= order[me * SLOTS + m], taper, 0.0)
        coeff = jnp.concatenate(
            [hx[tile, pl.ds(m, 4 * GROUPS, stride=8), :].astype(BF) for tile in range(4)], axis=1
        )
        loads[m].wait()
        table = leg[m]
        harmonic = mm(coeff, table, NT)
        result = mm((harmonic * keep).astype(BF), table, NN)
        for tile in range(4):
            hy[tile, pl.ds(m, 4 * GROUPS, stride=8), :] = result[:, tile * 128:tile * 128 + 128]
    for tile in range(4):
        for source in range(4):
            done = []
            for g in range(GROUPS):
                at = (source * GROUPS + g) * 8
                done.append(hy[tile, at:at + 8, :])
            for i, val in enumerate(swap_blocks(done, lane_group)):
                back[(tile * 8 + i) * 4 + source] = val.astype(back.dtype)

    own_back = pltpu.make_async_copy(back.at[me], returned.at[me], local_sem)
    own_back.start()
    back_copies = everyone(back, returned, 1)
    for i in range(3):
        for tile in range(20):
            if tile not in (8, 9, 10):
                pb[i, tile] = jnp.zeros((BPD, 128), F32)
    flip16 = flip.astype(BF)
    own_back.wait()
    back_copies.wait_recv()

    turned = jnp.concatenate(
        [returned[d * 16:d * 16 + 16].astype(F32).reshape(128, 128).T for d in range(8)], axis=1
    )
    stacked = jnp.concatenate(split(turned), axis=0)
    lane1 = lax.broadcasted_iota(jnp.int32, (128, 128), 1)
    for pair in range(4):
        moved = mm(stacked, hot[:, pair * QUARTER:(pair + 1) * QUARTER], NN)
        natural = (moved[0:128] + moved[128:256]) * (2.0 / math.sqrt(M))
        for half in range(2):
            a = pair * 2 + half
            val = natural[:, half * 128:half * 128 + 128]
            if a == 0:
                val = jnp.where(lane1 == 0, 0.5 * val, val)
            cs[pl.ds(a, 128, stride=8), :] = val

    def synthesise(r, carry):
        cos_p = tp[r, 0:32, :]
        sin_p = tp[r, 32:64, :]
        table_hi = jnp.concatenate([th[r]] * 4, axis=0)
        table_lo = jnp.concatenate([tl[r]] * 4, axis=0)
        pieces = []
        for g in range(GROUPS):
            at = pl.multiple_of((g * RPD + r) * 8, 8)
            v = cs[pl.ds(at, 8), :]
            for c in range(4):
                pieces.append(jnp.where(quad_group == c, v, 0.0))
        hi, lo = split(jnp.concatenate(pieces, axis=0))
        full = mm(jnp.concatenate([hi, lo], axis=1), jnp.concatenate([table_hi, table_hi], axis=0), NN) + mm(
            hi, table_lo, NN
        )
        quarters = [[], [], [], []]
        for b in range(BPD):
            re = full[(2 * b) * 32:(2 * b) * 32 + 32]
            im = full[(2 * b + 1) * 32:(2 * b + 1) * 32 + 32]
            even = cos_p * re[:, :QUARTER] - sin_p * re[:, QUARTER:]
            odd = cos_p * im[:, QUARTER:] + sin_p * im[:, :QUARTER]
            ce, co = even[0:8] + even[16:24], even[8:16] + even[24:32]
            de, do = odd[0:8] + odd[16:24], odd[8:16] + odd[24:32]
            for i, total in enumerate((ce + co - de - do, ce - co + de - do, ce - co - de + do, ce + co + de + do)):
                quarters[i].append(jnp.sum(total, axis=0, keepdims=True))
        inside = pixel < length_of[r] // 4
        for i in range(4):
            val = jnp.where(inside, jnp.concatenate(quarters[i], axis=0), 0.0)
            nq[i, r] = val.astype(BF).astype(F32)
        return carry

    lax.fori_loop(0, RPD, synthesise, 0, unroll=4)
    for i in (1, 3):
        whole = nq[i].reshape(RPD * BPD, QUARTER).astype(BF)
        nq[i] = mm(whole, flip16, NN).reshape(RPD, BPD, QUARTER)

    def place(r, carry):
        length = length_of[r]
        tiles = []
        for i, offset in ((1, length // 2 - QUARTER), (2, length // 2), (3, length - QUARTER)):
            tile = (offset + 1024) // 128 - 8
            rest = offset - tile * 128
            val = nq[i, r]
            low = pltpu.roll(val[:, :128], rest, 1)
            high = pltpu.roll(val[:, 128:], rest, 1)
            wrapped = lane4 < rest
            pb[i - 1, 8] = jnp.where(wrapped, 0.0, low)
            pb[i - 1, 9] = jnp.where(wrapped, low, high)
            pb[i - 1, 10] = jnp.where(wrapped, high, 0.0)
            tiles.append(tile)
        first = nq[0, r]
        for t in range(8):
            total = pb[0, 8 + t - tiles[0]] + pb[1, 8 + t - tiles[1]] + pb[2, 8 + t - tiles[2]]
            if t < 2:
                total = total + first[:, t * 128:t * 128 + 128]
            nd[t, pl.ds(r, BPD, stride=RPD), :] = total
        return carry

    lax.fori_loop(0, RPD, place, 0, unroll=2)
    for t in range(4):
        ndb[t] = jnp.concatenate([nd[2 * t], nd[2 * t + 1]], axis=1).astype(BF)

    own_pixels = pltpu.make_async_copy(ndb.at[band], got.at[band], local_sem)
    own_pixels.start()
    copies = []
    for i, other in enumerate(others):
        copies.append(pltpu.make_async_remote_copy(
            src_ref=ndb.at[other], dst_ref=got.at[band], send_sem=pix_send.at[i], recv_sem=pix_recv.at[i],
            device_id=(sky, other), device_id_type=MESH,
        ))
        copies[-1].start()
    own_pixels.wait()
    for copy in copies:
        copy.wait_recv()
    for t in range(4):
        val = got[t].astype(F32)
        for half in range(2):
            wide[half, t * BPD * RPD:(t + 1) * BPD * RPD, :] = val[:, half * 128:half * 128 + 128]
    pixels = [[wide[half, pl.ds(r, BANDS, stride=RPD), :] for half in range(2)] for r in range(RPD)]
    gram = jnp.zeros((BANDS, 128), F32)
    for d in range(4):
        x = jnp.concatenate([v for r in range(DOM) for v in pixels[d * DOM + r]], axis=1).astype(BF)
        x = jnp.concatenate([x, jnp.zeros((128 - BANDS, x.shape[1]), BF)], axis=0)
        block = mm(x[:BANDS], x, NT)
        gram = gram + (pltpu.roll(block, 32 * d, 1) if d else block)
    part[...] = gram
    for i, other in enumerate(others):
        copies.append(pltpu.make_async_remote_copy(
            src_ref=part, dst_ref=parts.at[i], send_sem=cov_send.at[i], recv_sem=cov_recv.at[i],
            device_id=(sky, other), device_id_type=MESH,
        ))
        copies[-1].start()
    for copy in copies[3:]:
        copy.wait_recv()
    total = (gram + parts[1]) + (parts[0] + parts[2])
    row = lax.broadcasted_iota(jnp.int32, (BANDS, 128), 0)
    col = lax.broadcasted_iota(jnp.int32, (BANDS, 128), 1)
    systems = []
    for d in range(4):
        count = length_of[d * DOM] + length_of[d * DOM + 1] + length_of[d * DOM + 2] + length_of[d * DOM + 3]
        cov = pltpu.roll(total, 128 - 32 * d, 1) if d else total
        cov = cov / jnp.full((1, 128), count, jnp.int32).astype(F32)
        diagonal = jnp.where(row == col, cov, 0.0)
        trace = jnp.sum(jnp.sum(diagonal, axis=1, keepdims=True), axis=0, keepdims=True)
        work = jnp.where(col < BANDS, cov, 0.0) + jnp.where(row == col, (RIDGE / BANDS) * trace, 0.0)
        systems.append(jnp.where(col == BANDS, 1.0, work))
    for j in range(BANDS):
        for d in range(4):
            work = systems[d]
            pivot = work[j:j + 1, :] / work[j:j + 1, j:j + 1]
            systems[d] = jnp.where(row == j, pivot, work - work[:, j:j + 1] * pivot)
    for d in range(4):
        solved = systems[d][:, BANDS:BANDS + 1]
        weights = solved / jnp.sum(solved, axis=0, keepdims=True)
        for r in range(DOM):
            at = d * DOM + r
            clean = [jnp.sum(weights * v, axis=0, keepdims=True) for v in pixels[at]]
            out_ref[at:at + 1, :] = jnp.concatenate(clean, axis=1)
    out_copies.wait_send()
    back_copies.wait_send()
    for copy in copies:
        copy.wait_send()


def on_device(band_maps, cycle_weight, cycle_len, m_order, legendre, band_start):
    whole = pl.BlockSpec(memory_space=pl.ANY)
    vmem = pltpu.VMEM
    dma = pltpu.SemaphoreType.DMA
    return pl.pallas_call(
        whole_kernel,
        out_shape=jax.ShapeDtypeStruct((RPD, QUARTER), F32),
        in_specs=[whole] * 7,
        out_specs=pl.BlockSpec(memory_space=vmem),
        scratch_shapes=[
            vmem((BPD * RPD, 4 * QUARTER), F32),
            pltpu.SMEM((RPD,), F32),
            pltpu.SMEM((RPD,), jnp.int32),
            pltpu.SMEM((M,), jnp.int32),
            vmem((8, 128), jnp.int32),
            pltpu.SMEM((1,), jnp.int32),
            vmem((SLOTS, LB, 512), BF),
            vmem((11, BPD * RPD, 128), F32),
            vmem((11, BPD * RPD, 128), F32),
            vmem((M, 128), F32),
            vmem((RPD, 64, QUARTER), F32),
            vmem((RPD, 32, 2 * QUARTER), BF),
            vmem((RPD, 32, 2 * QUARTER), BF),
            vmem((M, M), BF),
            vmem((NDEV, SLOTS, 128), BF),
            vmem((NDEV, SLOTS, 128), BF),
            vmem((4, 4 * GROUPS * SLOTS, 128), F32),
            vmem((4, 4 * GROUPS * SLOTS, 128), F32),
            vmem((NDEV, SLOTS, 128), BACK),
            vmem((NDEV, SLOTS, 128), BACK),
            vmem((4, RPD, BPD, QUARTER), F32),
            vmem((3, 20, BPD, 128), F32),
            vmem((8, BPD * RPD, 128), F32),
            vmem((4, BPD * RPD, QUARTER), BF),
            vmem((4, BPD * RPD, QUARTER), BF),
            vmem((2, 4 * BPD * RPD, 128), F32),
            vmem((BANDS, 128), F32),
            vmem((3, BANDS, 128), F32),
            dma((6,)),
            dma((SLOTS,)),
            dma,
            dma((2,)),
            dma((2,)),
            dma((3,)),
            dma((3,)),
            dma((3,)),
            dma((3,)),
        ],
        compiler_params=pltpu.CompilerParams(
            collective_id=0, has_side_effects=True, vmem_limit_bytes=56 << 20
        ),
        name="needlet_ilc",
    )(
        band_maps.reshape(BPD * RPD, 4 * QUARTER), cycle_weight, cycle_len, m_order, m_order.reshape(8, 128),
        legendre, band_start,
    )


def solution(mesh):
    placed = (P("band", "sky", None), P("sky"), P("sky"), P(), P(("sky", "band"), None, None), P())
    return jax.shard_map(
        on_device, mesh=mesh, in_specs=placed, out_specs=P("sky", "band"), check_vma=False
    )
```

```python
import functools
import math

import jax
import jax.numpy as jnp
from jax import lax
from jax.experimental import pallas as pl
from jax.experimental.pallas import tpu as pltpu
from jax.sharding import PartitionSpec as P

BANDS = 16
M = 1024
LB = 1024
DOM = 4
RIDGE = 0.05
QUARTER = 256
NDEV = 128
BPD = 4
RPD = 16
GROUPS = 2 * BPD
SLOTS = 8
MESH = pl.DeviceIdType.MESH
BF = jnp.bfloat16
F32 = jnp.float32
BACK = jnp.float32
NT = (((1,), (1,)), ((), ()))
NN = (((1,), (0,)), ((), ()))


def mm(a, b, dims, precision=None):
    return lax.dot_general(a, b, dims, precision=precision, preferred_element_type=F32)


def split(x):
    hi = x.astype(BF)
    return hi, (x - hi.astype(F32)).astype(BF)


def trig_tables(order, length):
    pixel = lax.broadcasted_iota(jnp.int32, order.shape, 1)
    turns = order * (2 * pixel + 1).astype(F32)
    lf = jnp.full((1, QUARTER), length, jnp.int32).astype(F32)
    quarter = 0.5 * lf
    count = jnp.floor(turns * (1.0 / quarter) + 0.5)
    y = (turns - count * quarter) * (math.pi / lf)
    z = y * y
    s = ((-1.9515295891e-4 * z + 8.3321608736e-3) * z - 1.6666654611e-1) * z * y + y
    c = ((2.443315711809948e-5 * z - 1.388731625493765e-3) * z + 4.166664568298827e-2) * (z * z) - 0.5 * z + 1.0
    quad = count - 4.0 * jnp.floor(count * 0.25)
    upper = quad >= 2.0
    odd = (quad == 1.0) | (quad == 3.0)
    sin = jnp.where(odd, c, s)
    cos = jnp.where(odd, s, c)
    sin = jnp.where(upper, -sin, sin)
    cos = jnp.where((quad == 1.0) | (quad == 2.0), -cos, cos)
    return cos, sin


def order_rows():
    row = lax.broadcasted_iota(jnp.int32, (32, QUARTER), 0)
    inner = (4 * (row % 8) + row // 8).astype(F32)
    outer = (32 * row).astype(F32)
    return inner, outer


def reversal():
    row = lax.broadcasted_iota(jnp.int32, (QUARTER, QUARTER), 0)
    col = lax.broadcasted_iota(jnp.int32, (QUARTER, QUARTER), 1)
    return jnp.where(row + col == QUARTER - 1, 1.0, 0.0).astype(F32)


def window_taper(window):
    turns = 2.0 * window + 1.0
    count = jnp.floor(turns * (1.0 / LB) + 0.5)
    y = (turns - count * LB) * (math.pi / (2 * LB))
    z = y * y
    s = ((-1.9515295891e-4 * z + 8.3321608736e-3) * z - 1.6666654611e-1) * z * y + y
    c = ((2.443315711809948e-5 * z - 1.388731625493765e-3) * z + 4.166664568298827e-2) * (z * z) - 0.5 * z + 1.0
    return jnp.where(count == 0.0, s, jnp.where(count == 1.0, c, -s))


def swap_blocks(rows, lane_group):
    rows = list(rows)
    for bit in (1, 2, 4):
        low = (lane_group // bit) % 2 == 0
        for i in range(8):
            if i & bit:
                continue
            a, b = rows[i], rows[i + bit]
            rows[i] = jnp.where(low, a, pltpu.roll(b, 16 * bit, 1))
            rows[i + bit] = jnp.where(low, pltpu.roll(a, 128 - 16 * bit, 1), b)
    return rows


def whole_kernel(
    maps_hbm, weight_hbm, len_hbm, order_hbm, order_rows_hbm, leg_hbm, start_hbm, low_ref, high_ref,
    maps, weight, length_of, order, order_vec, start, leg,
    xs, xr, cs, tp, th, tl, hot, flat_ref, msg, arrived, hx, hy, filtered, back, returned, pb, ndb, got, wide,
    part, parts,
    small_sem, leg_sem, local_sem, send_sem, recv_sem, pix_send, pix_recv, cov_send, cov_recv,
):
    sky = lax.axis_index("sky")
    band = lax.axis_index("band")
    me = sky * 4 + band
    bands = [band] + [lax.rem(band + j, 4) for j in range(1, 4)]
    others = bands[1:]

    small = [
        pltpu.make_async_copy(src, dst, small_sem.at[i])
        for i, (src, dst) in enumerate((
            (maps_hbm, maps), (len_hbm, length_of), (weight_hbm, weight), (order_rows_hbm, order_vec),
            (order_hbm, order), (start_hbm, start),
        ))
    ]
    for copy in small:
        copy.start()
    loads = [pltpu.make_async_copy(leg_hbm.at[i], leg.at[i], leg_sem.at[i]) for i in range(SLOTS)]
    for copy in loads:
        copy.start()

    barrier = pltpu.get_barrier_semaphore()

    def signal(row, column):
        pl.semaphore_signal(barrier, inc=1, device_id=(row, column), device_id_type=MESH)

    node = lax.rem(sky, 8)
    branch = sky // 8
    leader = band == 0
    inner_leader = leader & (node != 0)
    branch_leader = leader & (node == 0) & (branch != 0)
    root = leader & (sky == 0)

    def leaders_below():
        for i in range(1, 8):
            signal(branch * 8 + i, 0)

    def bands_below():
        for i in range(1, 4):
            signal(sky, i)

    def enter(step):
        if step == 0:
            @pl.when(band != 0)
            def _():
                signal(sky, 0)
        if step == 1:
            @pl.when(inner_leader)
            def _():
                pl.semaphore_wait(barrier, 3)
                signal(branch * 8, 0)
        if step == 2:
            @pl.when(branch_leader)
            def _():
                pl.semaphore_wait(barrier, 10)
                signal(0, 0)
        if step == 3:
            @pl.when(root)
            def _():
                pl.semaphore_wait(barrier, 13)
                for i in range(1, 4):
                    signal(8 * i, 0)
                leaders_below()
                bands_below()
        if step == 4:
            @pl.when(branch_leader)
            def _():
                pl.semaphore_wait(barrier, 1)
                leaders_below()
                bands_below()
        if step == 5:
            @pl.when(inner_leader)
            def _():
                pl.semaphore_wait(barrier, 1)
                bands_below()
        if step == 6:
            @pl.when(band != 0)
            def _():
                pl.semaphore_wait(barrier, 1)

    enter(0)

    flip = reversal()
    for copy in small:
        copy.wait()
    for tile in range(8):
        xs[tile] = maps[:, tile * 128:tile * 128 + 128]
    for tile in (8, 9, 10):
        xs[tile] = jnp.zeros((BPD * RPD, 128), F32)
        xr[tile] = jnp.zeros((BPD * RPD, 128), F32)
    for block in range(4):
        turned = mm(maps[:, block * QUARTER:(block + 1) * QUARTER], flip, NN, lax.Precision.HIGHEST)
        xr[6 - 2 * block] = turned[:, 0:128]
        xr[7 - 2 * block] = turned[:, 128:256]
    enter(1)
    inner, outer = order_rows()
    lane4 = lax.broadcasted_iota(jnp.int32, (BPD, 128), 1)
    pixel = lax.broadcasted_iota(jnp.int32, (BPD, QUARTER), 1)
    quad_group = lax.broadcasted_iota(jnp.int32, (8, 128), 1) // 32

    def window(ref, r, offset):
        tile = offset // 128
        rest = offset - tile * 128
        shift = lax.rem(128 - rest, 128)
        pieces = [pltpu.roll(ref[tile + i, pl.ds(r, BPD, stride=RPD), :], shift, 1) for i in range(3)]
        keep = lane4 < 128 - rest
        return jnp.concatenate(
            [jnp.where(keep, pieces[0], pieces[1]), jnp.where(keep, pieces[1], pieces[2])], axis=1
        )

    def analyse(r, carry):
        length = length_of[r]
        scale = weight[r] * (1.0 / math.sqrt(512 * 1024))
        inside = pixel < length // 4
        x0 = jnp.concatenate([xs[i, pl.ds(r, BPD, stride=RPD), :] for i in range(2)], axis=1)
        x1 = window(xr, r, 1024 - length // 2)
        x2 = window(xs, r, length // 2)
        x3 = window(xr, r, 1024 - length)
        x0, x1, x2, x3 = [jnp.where(inside, v, 0.0) * scale for v in (x0, x1, x2, x3)]
        even = ((x0 + x3) + (x1 + x2), (x0 + x3) - (x1 + x2))
        odd = ((x0 - x3) - (x1 - x2), (x0 - x3) + (x1 - x2))
        cos_p, sin_p = trig_tables(inner, length)
        cos_q, sin_q = trig_tables(outer, length)
        ch, cl = split(cos_q)
        sh, sl = split(sin_q)
        tp[r, 0:32, :] = cos_p
        tp[r, 32:64, :] = sin_p
        th[r] = jnp.concatenate([ch, sh], axis=1)
        tl[r] = jnp.concatenate([cl, sl], axis=1)
        cqh, cql, sqh, sql = [jnp.concatenate([v] * 4, axis=0) for v in (ch, cl, sh, sl)]

        def rows(pair, table):
            pieces = []
            for b in range(BPD):
                for c in range(4):
                    source = pair[c % 2][b:b + 1]
                    pieces.append(jnp.broadcast_to(source, (8, QUARTER)) * table[c * 8:c * 8 + 8])
            return split(jnp.concatenate(pieces, axis=0))

        ech, ecl = rows(even, cos_p)
        esh, esl = rows(even, -sin_p)
        och, ocl = rows(odd, -cos_p)
        osh, osl = rows(odd, -sin_p)
        right_c = jnp.concatenate([cqh, cql, cqh], axis=1)
        right_s = jnp.concatenate([sqh, sql, sqh], axis=1)
        real = mm(jnp.concatenate([ech, ech, ecl], axis=1), right_c, NT) + mm(
            jnp.concatenate([esh, esh, esl], axis=1), right_s, NT
        )
        imag = mm(jnp.concatenate([och, och, ocl], axis=1), right_s, NT) + mm(
            jnp.concatenate([osh, osh, osl], axis=1), right_c, NT
        )
        for b in range(BPD):
            for half, val in enumerate((real, imag)):
                v = [val[b * 32 + c * 8:b * 32 + c * 8 + 8] for c in range(4)]
                picked = jnp.where(
                    quad_group == 0, v[0], jnp.where(quad_group == 1, v[1], jnp.where(quad_group == 2, v[2], v[3]))
                )
                at = pl.multiple_of(((b * 2 + half) * RPD + r) * 8, 8)
                cs[pl.ds(at, 8), :] = picked
        return carry

    def analyse_four(i, carry):
        for j in range(4):
            analyse(4 * i + j, carry)
        for step in range(4):
            pl.when(i == step)(functools.partial(enter, step + 2))
        return carry

    lax.fori_loop(0, RPD // 4, analyse_four, 0)

    flat = jnp.concatenate([cs[pl.ds(a, 128, stride=8), :].astype(BF) for a in range(8)], axis=1)
    slots = order_vec[...]
    where_to = (slots % 32 // 4 * 128 + slots % 4 * 32 + slots // 32).astype(F32)
    lane128 = lax.broadcasted_iota(jnp.int32, (128, 128), 1).astype(F32)
    for block in range(8):
        target = jnp.broadcast_to(where_to[block:block + 1], (128, 128)).T
        hot[block * 128:block * 128 + 128, :] = jnp.concatenate(
            [jnp.where(target == lane128 + 128.0 * a, 1.0, 0.0).astype(BF) for a in range(8)], axis=1
        )

    def send(src, dst, phase, row, column):
        pltpu.make_async_remote_copy(
            src_ref=src.at[row * 4 + column], dst_ref=dst.at[me], send_sem=send_sem.at[phase],
            recv_sem=recv_sem.at[phase], device_id=(row, column), device_id_type=MESH,
        ).start()

    def sent(src, dst, phase):
        return pltpu.make_async_remote_copy(
            src_ref=src.at[pl.ds(0, NDEV - 1)], dst_ref=dst.at[pl.ds(0, NDEV - 1)], send_sem=send_sem.at[phase],
            recv_sem=recv_sem.at[phase], device_id=(sky, others[0]), device_id_type=MESH,
        )

    def send_rows(src, dst, phase, base, count, here):
        def rows(i, carry):
            row = base + lax.rem(here + i, count)
            for column in bands:
                send(src, dst, phase, row, column)
            return carry

        lax.fori_loop(1, count, rows, 0)
        twin = base + here
        for column in others:
            send(src, dst, phase, twin, column)
        pl.when(twin != sky)(lambda: send(src, dst, phase, twin, band))

    enter(6)

    def slot_block(i, carry):
        block = lax.rem(sky // 4 + i, 8)
        at = pl.multiple_of(block * 128, 128)
        moved = mm(hot[pl.ds(at, 128), :], flat_ref[...], NT)
        msg[pl.ds(pl.multiple_of(block * 16, 16), 16)] = moved.reshape(16, SLOTS, 128).astype(BF)
        send_rows(msg, arrived, 0, block * 4, 4, lax.rem(sky, 4))
        return carry

    flat_ref[...] = flat
    lax.fori_loop(0, 8, slot_block, 0)
    own = pltpu.make_async_copy(msg.at[me], arrived.at[me], local_sem)
    own.start()
    out_copies = sent(msg, arrived, 0)
    window_at = lax.broadcasted_iota(jnp.int32, (8, LB), 1).astype(F32)
    taper = window_taper(window_at)[0:1] * (1.0 / math.sqrt(LB))
    degree = lax.broadcasted_iota(jnp.int32, (1, LB), 1) + start[0]
    own.wait()
    out_copies.wait_recv()

    lane_group = lax.broadcasted_iota(jnp.int32, (SLOTS, 128), 1) // 16
    for tile in range(4):
        for source in range(4):
            here = [arrived[(tile * 8 + i) * 4 + source].astype(F32) for i in range(8)]
            for g, val in enumerate(swap_blocks(here, lane_group)):
                at = (source * GROUPS + g) * 8
                hx[tile, at:at + 8, :] = val
    for m in range(SLOTS):
        keep = jnp.where(degree >= order[me * SLOTS + m], taper, 0.0)
        coeff = jnp.concatenate(
            [hx[tile, pl.ds(m, 4 * GROUPS, stride=8), :].astype(BF) for tile in range(4)], axis=1
        )
        loads[m].wait()
        filtered[m] = (mm(coeff, leg[m], NT) * keep).astype(BF)

    def cycle_half(i, carry):
        half = lax.rem(sky + i, 2)
        at = pl.multiple_of(half * QUARTER, QUARTER)
        for m in range(SLOTS):
            result = mm(filtered[m], leg[m, :, pl.ds(at, QUARTER)], NN)
            for side in range(2):
                hy[side, pl.ds(m, 4 * GROUPS, stride=8), :] = result[:, side * 128:side * 128 + 128]
        for side in range(2):
            for source in range(4):
                done = []
                for g in range(GROUPS):
                    row = (source * GROUPS + g) * 8
                    done.append(hy[side, row:row + 8, :])
                for k, val in enumerate(swap_blocks(done, lane_group)):
                    back[(half * 16 + side * 8 + k) * 4 + source] = val.astype(back.dtype)
        send_rows(back, returned, 1, half * 16, 16, lax.rem(sky, 16))
        return carry

    lax.fori_loop(0, 2, cycle_half, 0)
    own_back = pltpu.make_async_copy(back.at[me], returned.at[me], local_sem)
    own_back.start()
    back_copies = sent(back, returned, 1)
    for k in range(4):
        for i in range(3):
            for tile in range(20):
                if tile not in (8, 9, 10):
                    pb[k, i, tile] = jnp.zeros((BPD, 128), F32)
    flip16 = flip.astype(BF)
    own_back.wait()
    back_copies.wait_recv()

    turned = jnp.concatenate(
        [returned[d * 16:d * 16 + 16].astype(F32).reshape(128, 128).T for d in range(8)], axis=1
    )
    stacked = jnp.concatenate(split(turned), axis=0)
    lane1 = lax.broadcasted_iota(jnp.int32, (128, 128), 1)
    for pair in range(4):
        moved = mm(stacked, hot[:, pair * QUARTER:(pair + 1) * QUARTER], NN)
        natural = (moved[0:128] + moved[128:256]) * (2.0 / math.sqrt(M))
        for half in range(2):
            a = pair * 2 + half
            val = natural[:, half * 128:half * 128 + 128]
            if a == 0:
                val = jnp.where(lane1 == 0, 0.5 * val, val)
            cs[pl.ds(a, 128, stride=8), :] = val

    def cycle(r):
        cos_p = tp[r, 0:32, :]
        sin_p = tp[r, 32:64, :]
        table_hi = jnp.concatenate([th[r]] * 4, axis=0)
        table_lo = jnp.concatenate([tl[r]] * 4, axis=0)
        pieces = []
        for g in range(GROUPS):
            at = pl.multiple_of((g * RPD + r) * 8, 8)
            v = cs[pl.ds(at, 8), :]
            for c in range(4):
                pieces.append(jnp.where(quad_group == c, v, 0.0))
        hi, lo = split(jnp.concatenate(pieces, axis=0))
        full = mm(jnp.concatenate([hi, lo], axis=1), jnp.concatenate([table_hi, table_hi], axis=0), NN) + mm(
            hi, table_lo, NN
        )
        quarters = [[], [], [], []]
        for b in range(BPD):
            re = full[(2 * b) * 32:(2 * b) * 32 + 32]
            im = full[(2 * b + 1) * 32:(2 * b + 1) * 32 + 32]
            even = cos_p * re[:, :QUARTER] - sin_p * re[:, QUARTER:]
            odd = cos_p * im[:, QUARTER:] + sin_p * im[:, :QUARTER]
            ce, co = even[0:8] + even[16:24], even[8:16] + even[24:32]
            de, do = odd[0:8] + odd[16:24], odd[8:16] + odd[24:32]
            for i, total in enumerate((ce + co - de - do, ce - co + de - do, ce - co - de + do, ce + co + de + do)):
                quarters[i].append(jnp.sum(total, axis=0, keepdims=True))
        inside = pixel < length_of[r] // 4
        return [jnp.where(inside, jnp.concatenate(q, axis=0), 0.0).astype(BF).astype(F32) for q in quarters]

    def pixel_copy(d, i):
        return pltpu.make_async_remote_copy(
            src_ref=ndb.at[d, others[i]], dst_ref=got.at[d, band], send_sem=pix_send.at[d, i],
            recv_sem=pix_recv.at[d, i], device_id=(sky, others[i]), device_id_type=MESH,
        )

    def gram_copy(d, i):
        return pltpu.make_async_remote_copy(
            src_ref=part.at[d], dst_ref=parts.at[d, i], send_sem=cov_send.at[d, i], recv_sem=cov_recv.at[d, i],
            device_id=(sky, others[i]), device_id_type=MESH,
        )

    def pixels_of(d):
        cycles = [cycle(d * DOM + k) for k in range(DOM)]
        turned = mm(
            jnp.concatenate([q[i] for i in (1, 3) for q in cycles], axis=0).astype(BF), flip16, NN
        )
        columns = [[] for _ in range(8)]
        for k in range(DOM):
            length = length_of[d * DOM + k]
            tiles = []
            vals = (turned[k * 4:k * 4 + 4], cycles[k][2], turned[16 + k * 4:16 + k * 4 + 4])
            for i, offset in enumerate((length // 2 - QUARTER, length // 2, length - QUARTER)):
                tile = (offset + 1024) // 128 - 8
                rest = offset - tile * 128
                low = pltpu.roll(vals[i][:, :128], rest, 1)
                high = pltpu.roll(vals[i][:, 128:], rest, 1)
                wrapped = lane4 < rest
                pb[k, i, 8] = jnp.where(wrapped, 0.0, low)
                pb[k, i, 9] = jnp.where(wrapped, low, high)
                pb[k, i, 10] = jnp.where(wrapped, high, 0.0)
                tiles.append(tile)
            for t in range(8):
                total = pb[k, 0, 8 + t - tiles[0]] + pb[k, 1, 8 + t - tiles[1]] + pb[k, 2, 8 + t - tiles[2]]
                if t < 2:
                    total = total + cycles[k][0][:, t * 128:t * 128 + 128]
                columns[t].append(total)
        for t in range(4):
            ndb[d, t] = jnp.concatenate(
                [jnp.concatenate(columns[2 * t + half], axis=0) for half in range(2)], axis=1
            ).astype(BF)
        for i in range(3):
            pixel_copy(d, i).start()
        got[d, band] = ndb[d, band]

    def gram_of(d):
        for i in range(3):
            pixel_copy(d, i).wait_recv()
        for t in range(4):
            val = got[d, t].astype(F32)
            for k in range(DOM):
                for half in range(2):
                    wide[d, k, half, 4 * t:4 * t + 4, :] = val[4 * k:4 * k + 4, half * 128:half * 128 + 128]
        x = jnp.concatenate([wide[d, k, half] for k in range(DOM) for half in range(2)], axis=1).astype(BF)
        tall = jnp.concatenate([x, jnp.zeros((128 - BANDS, x.shape[1]), BF)], axis=0)
        part[d] = mm(x, tall, NT)
        for i in range(3):
            gram_copy(d, i).start()

    def domain(d, carry):
        pixels_of(d)
        pl.when(d > 0)(lambda: gram_of(d - 1))
        return carry

    lax.fori_loop(0, 4, domain, 0)

    gram_of(3)
    row = lax.broadcasted_iota(jnp.int32, (BANDS, 128), 0)
    col = lax.broadcasted_iota(jnp.int32, (BANDS, 128), 1)
    systems = []
    for d in range(4):
        for i in range(3):
            gram_copy(d, i).wait_recv()
        count = length_of[d * DOM] + length_of[d * DOM + 1] + length_of[d * DOM + 2] + length_of[d * DOM + 3]
        cov = (part[d] + parts[d, 1]) + (parts[d, 0] + parts[d, 2])
        cov = cov / jnp.full((1, 128), count, jnp.int32).astype(F32)
        diagonal = jnp.where(row == col, cov, 0.0)
        trace = jnp.sum(jnp.sum(diagonal, axis=1, keepdims=True), axis=0, keepdims=True)
        work = cov + jnp.where(row == col, (RIDGE / BANDS) * trace, 0.0)
        systems.append(jnp.where(col == BANDS, 1.0, work))
    for j in range(BANDS):
        for d in range(4):
            work = systems[d]
            pivot = work[j:j + 1, :] / work[j:j + 1, j:j + 1]
            systems[d] = jnp.where(row == j, pivot, work - work[:, j:j + 1] * pivot)
    for d in range(4):
        solved = systems[d][:, BANDS:BANDS + 1]
        weights = solved / jnp.sum(solved, axis=0, keepdims=True)
        for k in range(DOM):
            at = d * DOM + k
            terms = [weights * wide[d, k, half] for half in range(2)]
            for ref, first in ((low_ref, 0), (high_ref, 8)):
                ref[at:at + 1, :] = jnp.concatenate(
                    [jnp.sum(v[first:first + 8], axis=0, keepdims=True) for v in terms], axis=1
                )
    out_copies.wait_send()
    back_copies.wait_send()
    for d in range(4):
        for i in range(3):
            pixel_copy(d, i).wait_send()
            gram_copy(d, i).wait_send()


def on_device(band_maps, cycle_weight, cycle_len, m_order, legendre, band_start):
    whole = pl.BlockSpec(memory_space=pl.ANY)
    vmem = pltpu.VMEM
    dma = pltpu.SemaphoreType.DMA
    low, high = pl.pallas_call(
        whole_kernel,
        out_shape=[jax.ShapeDtypeStruct((RPD, QUARTER), F32)] * 2,
        in_specs=[whole] * 7,
        out_specs=[pl.BlockSpec(memory_space=vmem)] * 2,
        scratch_shapes=[
            vmem((BPD * RPD, 4 * QUARTER), F32),
            pltpu.SMEM((RPD,), F32),
            pltpu.SMEM((RPD,), jnp.int32),
            pltpu.SMEM((M,), jnp.int32),
            vmem((8, 128), jnp.int32),
            pltpu.SMEM((1,), jnp.int32),
            vmem((SLOTS, LB, 512), BF),
            vmem((11, BPD * RPD, 128), F32),
            vmem((11, BPD * RPD, 128), F32),
            vmem((M, 128), F32),
            vmem((RPD, 64, QUARTER), F32),
            vmem((RPD, 32, 2 * QUARTER), BF),
            vmem((RPD, 32, 2 * QUARTER), BF),
            vmem((M, M), BF),
            vmem((128, M), BF),
            vmem((NDEV, SLOTS, 128), BF),
            vmem((NDEV, SLOTS, 128), BF),
            vmem((4, 4 * GROUPS * SLOTS, 128), F32),
            vmem((2, 4 * GROUPS * SLOTS, 128), F32),
            vmem((SLOTS, 4 * GROUPS, LB), BF),
            vmem((NDEV, SLOTS, 128), BACK),
            vmem((NDEV, SLOTS, 128), BACK),
            vmem((DOM, 3, 20, BPD, 128), F32),
            vmem((4, 4, 4 * DOM, QUARTER), BF),
            vmem((4, 4, 4 * DOM, QUARTER), BF),
            vmem((4, DOM, 2, BANDS, 128), F32),
            vmem((4, BANDS, 128), F32),
            vmem((4, 3, BANDS, 128), F32),
            dma((6,)),
            dma((SLOTS,)),
            dma,
            dma((2,)),
            dma((2,)),
            dma((4, 3)),
            dma((4, 3)),
            dma((4, 3)),
            dma((4, 3)),
        ],
        compiler_params=pltpu.CompilerParams(
            collective_id=0, has_side_effects=True, vmem_limit_bytes=56 << 20
        ),
        name="needlet_ilc",
    )(
        band_maps.reshape(BPD * RPD, 4 * QUARTER), cycle_weight, cycle_len, m_order, m_order.reshape(8, 128),
        legendre, band_start,
    )
    return low + high


def solution(mesh):
    placed = (P("band", "sky", None), P("sky"), P("sky"), P(), P(("sky", "band"), None, None), P())
    return jax.shard_map(
        on_device, mesh=mesh, in_specs=placed, out_specs=P("sky", "band"), check_vma=False
    )
```

```python
import functools
import math

import jax
import jax.numpy as jnp
from jax import lax
from jax.experimental import pallas as pl
from jax.experimental.pallas import tpu as pltpu
from jax.sharding import PartitionSpec as P

BANDS = 16
M = 1024
LB = 1024
DOM = 4
RIDGE = 0.05
QUARTER = 256
NDEV = 128
BPD = 4
RPD = 16
GROUPS = 2 * BPD
SLOTS = 8
MESH = pl.DeviceIdType.MESH
BF = jnp.bfloat16
F32 = jnp.float32
BACK = jnp.bfloat16
NT = (((1,), (1,)), ((), ()))
NN = (((1,), (0,)), ((), ()))


def mm(a, b, dims, precision=None):
    return lax.dot_general(a, b, dims, precision=precision, preferred_element_type=F32)


def split(x):
    hi = x.astype(BF)
    return hi, (x - hi.astype(F32)).astype(BF)


def trig_tables(order, length):
    pixel = lax.broadcasted_iota(jnp.int32, order.shape, 1)
    turns = order * (2 * pixel + 1).astype(F32)
    lf = jnp.full((1, QUARTER), length, jnp.int32).astype(F32)
    quarter = 0.5 * lf
    count = jnp.floor(turns * (1.0 / quarter) + 0.5)
    y = (turns - count * quarter) * (math.pi / lf)
    z = y * y
    s = ((-1.9515295891e-4 * z + 8.3321608736e-3) * z - 1.6666654611e-1) * z * y + y
    c = ((2.443315711809948e-5 * z - 1.388731625493765e-3) * z + 4.166664568298827e-2) * (z * z) - 0.5 * z + 1.0
    quad = count - 4.0 * jnp.floor(count * 0.25)
    upper = quad >= 2.0
    odd = (quad == 1.0) | (quad == 3.0)
    sin = jnp.where(odd, c, s)
    cos = jnp.where(odd, s, c)
    sin = jnp.where(upper, -sin, sin)
    cos = jnp.where((quad == 1.0) | (quad == 2.0), -cos, cos)
    return cos, sin


def order_rows():
    row = lax.broadcasted_iota(jnp.int32, (32, QUARTER), 0)
    inner = (4 * (row % 8) + row // 8).astype(F32)
    outer = (32 * row).astype(F32)
    return inner, outer


def reversal():
    row = lax.broadcasted_iota(jnp.int32, (QUARTER, QUARTER), 0)
    col = lax.broadcasted_iota(jnp.int32, (QUARTER, QUARTER), 1)
    return jnp.where(row + col == QUARTER - 1, 1.0, 0.0).astype(F32)


def window_taper(window):
    turns = 2.0 * window + 1.0
    count = jnp.floor(turns * (1.0 / LB) + 0.5)
    y = (turns - count * LB) * (math.pi / (2 * LB))
    z = y * y
    s = ((-1.9515295891e-4 * z + 8.3321608736e-3) * z - 1.6666654611e-1) * z * y + y
    c = ((2.443315711809948e-5 * z - 1.388731625493765e-3) * z + 4.166664568298827e-2) * (z * z) - 0.5 * z + 1.0
    return jnp.where(count == 0.0, s, jnp.where(count == 1.0, c, -s))


def swap_blocks(rows, lane_group):
    rows = list(rows)
    for bit in (1, 2, 4):
        low = (lane_group // bit) % 2 == 0
        for i in range(8):
            if i & bit:
                continue
            a, b = rows[i], rows[i + bit]
            rows[i] = jnp.where(low, a, pltpu.roll(b, 16 * bit, 1))
            rows[i + bit] = jnp.where(low, pltpu.roll(a, 128 - 16 * bit, 1), b)
    return rows


def whole_kernel(
    maps_hbm, weight_hbm, len_hbm, order_hbm, order_rows_hbm, leg_hbm, start_hbm, out_ref,
    maps, weight, length_of, order, order_vec, start, leg,
    xs, xr, cs, tp, th, tl, hot, msg, arrived, hx, hy, back, returned, nq, pb, nd, ndb, got, wide, part, parts,
    small_sem, leg_sem, local_sem, send_sem, recv_sem, pix_send, pix_recv, cov_send, cov_recv,
):
    sky = lax.axis_index("sky")
    band = lax.axis_index("band")
    me = sky * 4 + band
    bands = [band] + [lax.rem(band + j, 4) for j in range(1, 4)]
    others = bands[1:]

    small = [
        pltpu.make_async_copy(src, dst, small_sem.at[i])
        for i, (src, dst) in enumerate((
            (maps_hbm, maps), (len_hbm, length_of), (weight_hbm, weight), (order_rows_hbm, order_vec),
            (order_hbm, order), (start_hbm, start),
        ))
    ]
    for copy in small:
        copy.start()
    loads = [pltpu.make_async_copy(leg_hbm.at[i], leg.at[i], leg_sem.at[i]) for i in range(SLOTS)]
    for copy in loads:
        copy.start()

    barrier = pltpu.get_barrier_semaphore()

    def greet(i):
        row = lax.rem(sky + i, 32)
        for column in bands:
            pl.semaphore_signal(barrier, inc=1, device_id=(row, column), device_id_type=MESH)

    for column in others:
        pl.semaphore_signal(barrier, inc=1, device_id=(sky, column), device_id_type=MESH)
    greet(1)

    flip = reversal()
    for copy in small:
        copy.wait()
    for tile in range(8):
        xs[tile] = maps[:, tile * 128:tile * 128 + 128]
    for tile in (8, 9, 10):
        xs[tile] = jnp.zeros((BPD * RPD, 128), F32)
        xr[tile] = jnp.zeros((BPD * RPD, 128), F32)
    for block in range(4):
        turned = mm(maps[:, block * QUARTER:(block + 1) * QUARTER], flip, NN, lax.Precision.HIGHEST)
        xr[6 - 2 * block] = turned[:, 0:128]
        xr[7 - 2 * block] = turned[:, 128:256]
    inner, outer = order_rows()
    lane4 = lax.broadcasted_iota(jnp.int32, (BPD, 128), 1)
    pixel = lax.broadcasted_iota(jnp.int32, (BPD, QUARTER), 1)
    quad_group = lax.broadcasted_iota(jnp.int32, (8, 128), 1) // 32

    def window(ref, r, offset):
        tile = offset // 128
        rest = offset - tile * 128
        shift = lax.rem(128 - rest, 128)
        pieces = [pltpu.roll(ref[tile + i, pl.ds(r, BPD, stride=RPD), :], shift, 1) for i in range(3)]
        keep = lane4 < 128 - rest
        return jnp.concatenate(
            [jnp.where(keep, pieces[0], pieces[1]), jnp.where(keep, pieces[1], pieces[2])], axis=1
        )

    def analyse(r, carry):
        length = length_of[r]
        scale = weight[r] * (1.0 / math.sqrt(512 * 1024))
        inside = pixel < length // 4
        x0 = jnp.concatenate([xs[i, pl.ds(r, BPD, stride=RPD), :] for i in range(2)], axis=1)
        x1 = window(xr, r, 1024 - length // 2)
        x2 = window(xs, r, length // 2)
        x3 = window(xr, r, 1024 - length)
        x0, x1, x2, x3 = [jnp.where(inside, v, 0.0) * scale for v in (x0, x1, x2, x3)]
        even = ((x0 + x3) + (x1 + x2), (x0 + x3) - (x1 + x2))
        odd = ((x0 - x3) - (x1 - x2), (x0 - x3) + (x1 - x2))
        cos_p, sin_p = trig_tables(inner, length)
        cos_q, sin_q = trig_tables(outer, length)
        ch, cl = split(cos_q)
        sh, sl = split(sin_q)
        tp[r, 0:32, :] = cos_p
        tp[r, 32:64, :] = sin_p
        th[r] = jnp.concatenate([ch, sh], axis=1)
        tl[r] = jnp.concatenate([cl, sl], axis=1)
        cqh, cql, sqh, sql = [jnp.concatenate([v] * 4, axis=0) for v in (ch, cl, sh, sl)]

        def rows(pair, table):
            pieces = []
            for b in range(BPD):
                for c in range(4):
                    source = pair[c % 2][b:b + 1]
                    pieces.append(jnp.broadcast_to(source, (8, QUARTER)) * table[c * 8:c * 8 + 8])
            return split(jnp.concatenate(pieces, axis=0))

        ech, ecl = rows(even, cos_p)
        esh, esl = rows(even, -sin_p)
        och, ocl = rows(odd, -cos_p)
        osh, osl = rows(odd, -sin_p)
        right_c = jnp.concatenate([cqh, cql, cqh], axis=1)
        right_s = jnp.concatenate([sqh, sql, sqh], axis=1)
        real = mm(jnp.concatenate([ech, ech, ecl], axis=1), right_c, NT) + mm(
            jnp.concatenate([esh, esh, esl], axis=1), right_s, NT
        )
        imag = mm(jnp.concatenate([och, och, ocl], axis=1), right_s, NT) + mm(
            jnp.concatenate([osh, osh, osl], axis=1), right_c, NT
        )
        for b in range(BPD):
            for half, val in enumerate((real, imag)):
                v = [val[b * 32 + c * 8:b * 32 + c * 8 + 8] for c in range(4)]
                picked = jnp.where(
                    quad_group == 0, v[0], jnp.where(quad_group == 1, v[1], jnp.where(quad_group == 2, v[2], v[3]))
                )
                at = pl.multiple_of(((b * 2 + half) * RPD + r) * 8, 8)
                cs[pl.ds(at, 8), :] = picked
        return carry

    def analyse_four(i, carry):
        for j in range(4):
            analyse(4 * i + j, carry)
        return carry

    lax.fori_loop(2, 32, lambda i, carry: (greet(i), carry)[1], 0)
    lax.fori_loop(0, RPD // 4, analyse_four, 0)

    flat = jnp.concatenate([cs[pl.ds(a, 128, stride=8), :].astype(BF) for a in range(8)], axis=1)
    slots = order_vec[...]
    where_to = (slots % 32 // 4 * 128 + slots % 4 * 32 + slots // 32).astype(F32)
    lane128 = lax.broadcasted_iota(jnp.int32, (128, 128), 1).astype(F32)
    for block in range(8):
        target = jnp.broadcast_to(where_to[block:block + 1], (128, 128)).T
        row_hot = jnp.concatenate(
            [jnp.where(target == lane128 + 128.0 * a, 1.0, 0.0).astype(BF) for a in range(8)], axis=1
        )
        hot[block * 128:block * 128 + 128, :] = row_hot
        moved = mm(row_hot, flat, NT)
        msg[block * 16:block * 16 + 16] = moved.reshape(16, SLOTS, 128).astype(BF)

    own = pltpu.make_async_copy(msg.at[me], arrived.at[me], local_sem)
    own.start()
    pl.semaphore_wait(barrier, NDEV - 1)

    def everyone(src, dst, phase):
        def one(row, column):
            pltpu.make_async_remote_copy(
                src_ref=src.at[row * 4 + column], dst_ref=dst.at[me], send_sem=send_sem.at[phase],
                recv_sem=recv_sem.at[phase], device_id=(row, column), device_id_type=MESH,
            ).start()

        for column in others:
            one(sky, column)

        def rows(i, carry):
            row = lax.rem(sky + i, 32)
            for column in bands:
                one(row, column)
            return carry

        lax.fori_loop(1, 32, rows, 0)
        return pltpu.make_async_remote_copy(
            src_ref=src.at[pl.ds(0, NDEV - 1)], dst_ref=dst.at[pl.ds(0, NDEV - 1)], send_sem=send_sem.at[phase],
            recv_sem=recv_sem.at[phase], device_id=(sky, others[0]), device_id_type=MESH,
        )

    out_copies = everyone(msg, arrived, 0)
    window_at = lax.broadcasted_iota(jnp.int32, (8, LB), 1).astype(F32)
    taper = window_taper(window_at)[0:1] * (1.0 / math.sqrt(LB))
    degree = lax.broadcasted_iota(jnp.int32, (1, LB), 1) + start[0]
    own.wait()
    out_copies.wait_recv()

    lane_group = lax.broadcasted_iota(jnp.int32, (SLOTS, 128), 1) // 16
    for tile in range(4):
        for source in range(4):
            here = [arrived[(tile * 8 + i) * 4 + source].astype(F32) for i in range(8)]
            for g, val in enumerate(swap_blocks(here, lane_group)):
                at = (source * GROUPS + g) * 8
                hx[tile, at:at + 8, :] = val
    for m in range(SLOTS):
        keep = jnp.where(degree >= order[me * SLOTS + m], taper, 0.0)
        coeff = jnp.concatenate(
            [hx[tile, pl.ds(m, 4 * GROUPS, stride=8), :].astype(BF) for tile in range(4)], axis=1
        )
        loads[m].wait()
        table = leg[m]
        harmonic = mm(coeff, table, NT)
        result = mm((harmonic * keep).astype(BF), table, NN)
        for tile in range(4):
            hy[tile, pl.ds(m, 4 * GROUPS, stride=8), :] = result[:, tile * 128:tile * 128 + 128]
    for tile in range(4):
        for source in range(4):
            done = []
            for g in range(GROUPS):
                at = (source * GROUPS + g) * 8
                done.append(hy[tile, at:at + 8, :])
            for i, val in enumerate(swap_blocks(done, lane_group)):
                back[(tile * 8 + i) * 4 + source] = val.astype(back.dtype)

    own_back = pltpu.make_async_copy(back.at[me], returned.at[me], local_sem)
    own_back.start()
    back_copies = everyone(back, returned, 1)
    for i in range(3):
        for tile in range(20):
            if tile not in (8, 9, 10):
                pb[i, tile] = jnp.zeros((BPD, 128), F32)
    flip16 = flip.astype(BF)
    own_back.wait()
    back_copies.wait_recv()

    turned = jnp.concatenate(
        [returned[d * 16:d * 16 + 16].astype(F32).reshape(128, 128).T for d in range(8)], axis=1
    )
    stacked = turned.astype(BF)
    lane1 = lax.broadcasted_iota(jnp.int32, (128, 128), 1)
    for pair in range(4):
        moved = mm(stacked, hot[:, pair * QUARTER:(pair + 1) * QUARTER], NN)
        natural = moved
        for half in range(2):
            a = pair * 2 + half
            val = natural[:, half * 128:half * 128 + 128]
            if a == 0:
                val = jnp.where(lane1 == 0, 0.5 * val, val)
            cs[pl.ds(a, 128, stride=8), :] = val

    def synthesise(r, carry):
        cos_p = tp[r, 0:32, :]
        sin_p = tp[r, 32:64, :]
        table_hi = jnp.concatenate([th[r]] * 4, axis=0)
        table_lo = jnp.concatenate([tl[r]] * 4, axis=0)
        pieces = []
        for g in range(GROUPS):
            at = pl.multiple_of((g * RPD + r) * 8, 8)
            v = cs[pl.ds(at, 8), :]
            for c in range(4):
                pieces.append(jnp.where(quad_group == c, v, 0.0))
        hi = jnp.concatenate(pieces, axis=0).astype(BF)
        full = mm(jnp.concatenate([hi, hi], axis=1), jnp.concatenate([table_hi, table_lo], axis=0), NN)
        quarters = [[], [], [], []]
        for b in range(BPD):
            re = full[(2 * b) * 32:(2 * b) * 32 + 32]
            im = full[(2 * b + 1) * 32:(2 * b + 1) * 32 + 32]
            even = cos_p * re[:, :QUARTER] - sin_p * re[:, QUARTER:]
            odd = cos_p * im[:, QUARTER:] + sin_p * im[:, :QUARTER]
            ce, co = even[0:8] + even[16:24], even[8:16] + even[24:32]
            de, do = odd[0:8] + odd[16:24], odd[8:16] + odd[24:32]
            for i, total in enumerate((ce + co - de - do, ce - co + de - do, ce - co - de + do, ce + co + de + do)):
                quarters[i].append(jnp.sum(total, axis=0, keepdims=True))
        inside = pixel < length_of[r] // 4
        for i in range(4):
            val = jnp.where(inside, jnp.concatenate(quarters[i], axis=0) * (2.0 / math.sqrt(M)), 0.0)
            nq[i, r] = val.astype(BF).astype(F32)
        return carry

    lax.fori_loop(0, RPD, synthesise, 0, unroll=4)
    for i in (1, 3):
        whole = nq[i].reshape(RPD * BPD, QUARTER).astype(BF)
        nq[i] = mm(whole, flip16, NN).reshape(RPD, BPD, QUARTER)

    def place(r, carry):
        length = length_of[r]
        tiles = []
        for i, offset in ((1, length // 2 - QUARTER), (2, length // 2), (3, length - QUARTER)):
            tile = (offset + 1024) // 128 - 8
            rest = offset - tile * 128
            val = nq[i, r]
            low = pltpu.roll(val[:, :128], rest, 1)
            high = pltpu.roll(val[:, 128:], rest, 1)
            wrapped = lane4 < rest
            pb[i - 1, 8] = jnp.where(wrapped, 0.0, low)
            pb[i - 1, 9] = jnp.where(wrapped, low, high)
            pb[i - 1, 10] = jnp.where(wrapped, high, 0.0)
            tiles.append(tile)
        first = nq[0, r]
        for t in range(8):
            total = pb[0, 8 + t - tiles[0]] + pb[1, 8 + t - tiles[1]] + pb[2, 8 + t - tiles[2]]
            if t < 2:
                total = total + first[:, t * 128:t * 128 + 128]
            nd[t, pl.ds(r, BPD, stride=RPD), :] = total
        return carry

    lax.fori_loop(0, RPD, place, 0, unroll=2)
    for t in range(4):
        ndb[t] = jnp.concatenate([nd[2 * t], nd[2 * t + 1]], axis=1).astype(BF)

    own_pixels = pltpu.make_async_copy(ndb.at[band], got.at[band], local_sem)
    own_pixels.start()
    copies = []
    for i, other in enumerate(others):
        copies.append(pltpu.make_async_remote_copy(
            src_ref=ndb.at[other], dst_ref=got.at[band], send_sem=pix_send.at[i], recv_sem=pix_recv.at[i],
            device_id=(sky, other), device_id_type=MESH,
        ))
        copies[-1].start()
    own_pixels.wait()
    for copy in copies:
        copy.wait_recv()
    for t in range(4):
        val = got[t].astype(F32)
        for half in range(2):
            wide[half, t * BPD * RPD:(t + 1) * BPD * RPD, :] = val[:, half * 128:half * 128 + 128]
    pixels = [[wide[half, pl.ds(r, BANDS, stride=RPD), :] for half in range(2)] for r in range(RPD)]
    gram = jnp.zeros((BANDS, 128), F32)
    for d in range(4):
        x = jnp.concatenate([v for r in range(DOM) for v in pixels[d * DOM + r]], axis=1).astype(BF)
        x = jnp.concatenate([x, jnp.zeros((128 - BANDS, x.shape[1]), BF)], axis=0)
        block = mm(x[:BANDS], x, NT)
        gram = gram + (pltpu.roll(block, 32 * d, 1) if d else block)
    part[...] = gram
    for i, other in enumerate(others):
        copies.append(pltpu.make_async_remote_copy(
            src_ref=part, dst_ref=parts.at[i], send_sem=cov_send.at[i], recv_sem=cov_recv.at[i],
            device_id=(sky, other), device_id_type=MESH,
        ))
        copies[-1].start()
    for copy in copies[3:]:
        copy.wait_recv()
    total = (gram + parts[1]) + (parts[0] + parts[2])
    row = lax.broadcasted_iota(jnp.int32, (BANDS, 128), 0)
    col = lax.broadcasted_iota(jnp.int32, (BANDS, 128), 1)
    systems = []
    for d in range(4):
        count = length_of[d * DOM] + length_of[d * DOM + 1] + length_of[d * DOM + 2] + length_of[d * DOM + 3]
        cov = pltpu.roll(total, 128 - 32 * d, 1) if d else total
        cov = cov / jnp.full((1, 128), count, jnp.int32).astype(F32)
        diagonal = jnp.where(row == col, cov, 0.0)
        trace = jnp.sum(jnp.sum(diagonal, axis=1, keepdims=True), axis=0, keepdims=True)
        work = jnp.where(col < BANDS, cov, 0.0) + jnp.where(row == col, (RIDGE / BANDS) * trace, 0.0)
        systems.append(jnp.where(col == BANDS, 1.0, work))
    for j in range(BANDS):
        for d in range(4):
            work = systems[d]
            pivot = work[j:j + 1, :] / work[j:j + 1, j:j + 1]
            systems[d] = jnp.where(row == j, pivot, work - work[:, j:j + 1] * pivot)
    for d in range(4):
        solved = systems[d][:, BANDS:BANDS + 1]
        weights = solved / jnp.sum(solved, axis=0, keepdims=True)
        for r in range(DOM):
            at = d * DOM + r
            clean = [jnp.sum(weights * v, axis=0, keepdims=True) for v in pixels[at]]
            out_ref[at:at + 1, :] = jnp.concatenate(clean, axis=1)
    out_copies.wait_send()
    back_copies.wait_send()
    for copy in copies:
        copy.wait_send()


def on_device(band_maps, cycle_weight, cycle_len, m_order, legendre, band_start):
    whole = pl.BlockSpec(memory_space=pl.ANY)
    vmem = pltpu.VMEM
    dma = pltpu.SemaphoreType.DMA
    return pl.pallas_call(
        whole_kernel,
        out_shape=jax.ShapeDtypeStruct((RPD, QUARTER), F32),
        in_specs=[whole] * 7,
        out_specs=pl.BlockSpec(memory_space=vmem),
        scratch_shapes=[
            vmem((BPD * RPD, 4 * QUARTER), F32),
            pltpu.SMEM((RPD,), F32),
            pltpu.SMEM((RPD,), jnp.int32),
            pltpu.SMEM((M,), jnp.int32),
            vmem((8, 128), jnp.int32),
            pltpu.SMEM((1,), jnp.int32),
            vmem((SLOTS, LB, 512), BF),
            vmem((11, BPD * RPD, 128), F32),
            vmem((11, BPD * RPD, 128), F32),
            vmem((M, 128), F32),
            vmem((RPD, 64, QUARTER), F32),
            vmem((RPD, 32, 2 * QUARTER), BF),
            vmem((RPD, 32, 2 * QUARTER), BF),
            vmem((M, M), BF),
            vmem((NDEV, SLOTS, 128), BF),
            vmem((NDEV, SLOTS, 128), BF),
            vmem((4, 4 * GROUPS * SLOTS, 128), F32),
            vmem((4, 4 * GROUPS * SLOTS, 128), F32),
            vmem((NDEV, SLOTS, 128), BACK),
            vmem((NDEV, SLOTS, 128), BACK),
            vmem((4, RPD, BPD, QUARTER), F32),
            vmem((3, 20, BPD, 128), F32),
            vmem((8, BPD * RPD, 128), F32),
            vmem((4, BPD * RPD, QUARTER), BF),
            vmem((4, BPD * RPD, QUARTER), BF),
            vmem((2, 4 * BPD * RPD, 128), F32),
            vmem((BANDS, 128), F32),
            vmem((3, BANDS, 128), F32),
            dma((6,)),
            dma((SLOTS,)),
            dma,
            dma((2,)),
            dma((2,)),
            dma((3,)),
            dma((3,)),
            dma((3,)),
            dma((3,)),
        ],
        compiler_params=pltpu.CompilerParams(
            collective_id=0, has_side_effects=True, vmem_limit_bytes=56 << 20
        ),
        name="needlet_ilc",
    )(
        band_maps.reshape(BPD * RPD, 4 * QUARTER), cycle_weight, cycle_len, m_order, m_order.reshape(8, 128),
        legendre, band_start,
    )


def solution(mesh):
    placed = (P("band", "sky", None), P("sky"), P("sky"), P(), P(("sky", "band"), None, None), P())
    return jax.shard_map(
        on_device, mesh=mesh, in_specs=placed, out_specs=P("sky", "band"), check_vma=False
    )
```

```python
import functools
import math

import jax
import jax.numpy as jnp
from jax import lax
from jax.experimental import pallas as pl
from jax.experimental.pallas import tpu as pltpu
from jax.sharding import PartitionSpec as P

BANDS = 16
M = 1024
LB = 1024
DOM = 4
RIDGE = 0.05
QUARTER = 256
NDEV = 128
BPD = 4
RPD = 16
GROUPS = 2 * BPD
SLOTS = 8
MESH = pl.DeviceIdType.MESH
BF = jnp.bfloat16
F32 = jnp.float32
BACK = jnp.bfloat16
NT = (((1,), (1,)), ((), ()))
NN = (((1,), (0,)), ((), ()))


def mm(a, b, dims, precision=None):
    return lax.dot_general(a, b, dims, precision=precision, preferred_element_type=F32)


def split(x):
    hi = x.astype(BF)
    return hi, (x - hi.astype(F32)).astype(BF)


def trig_tables(order, length):
    pixel = lax.broadcasted_iota(jnp.int32, order.shape, 1)
    turns = order * (2 * pixel + 1).astype(F32)
    lf = jnp.full((1, QUARTER), length, jnp.int32).astype(F32)
    quarter = 0.5 * lf
    count = jnp.floor(turns * (1.0 / quarter) + 0.5)
    y = (turns - count * quarter) * (math.pi / lf)
    z = y * y
    s = ((-1.9515295891e-4 * z + 8.3321608736e-3) * z - 1.6666654611e-1) * z * y + y
    c = ((2.443315711809948e-5 * z - 1.388731625493765e-3) * z + 4.166664568298827e-2) * (z * z) - 0.5 * z + 1.0
    quad = count - 4.0 * jnp.floor(count * 0.25)
    upper = quad >= 2.0
    odd = (quad == 1.0) | (quad == 3.0)
    sin = jnp.where(odd, c, s)
    cos = jnp.where(odd, s, c)
    sin = jnp.where(upper, -sin, sin)
    cos = jnp.where((quad == 1.0) | (quad == 2.0), -cos, cos)
    return cos, sin


def order_rows():
    row = lax.broadcasted_iota(jnp.int32, (32, QUARTER), 0)
    inner = (4 * (row % 8) + row // 8).astype(F32)
    outer = (32 * row).astype(F32)
    return inner, outer


def reversal():
    row = lax.broadcasted_iota(jnp.int32, (QUARTER, QUARTER), 0)
    col = lax.broadcasted_iota(jnp.int32, (QUARTER, QUARTER), 1)
    return jnp.where(row + col == QUARTER - 1, 1.0, 0.0).astype(F32)


def window_taper(window):
    turns = 2.0 * window + 1.0
    count = jnp.floor(turns * (1.0 / LB) + 0.5)
    y = (turns - count * LB) * (math.pi / (2 * LB))
    z = y * y
    s = ((-1.9515295891e-4 * z + 8.3321608736e-3) * z - 1.6666654611e-1) * z * y + y
    c = ((2.443315711809948e-5 * z - 1.388731625493765e-3) * z + 4.166664568298827e-2) * (z * z) - 0.5 * z + 1.0
    return jnp.where(count == 0.0, s, jnp.where(count == 1.0, c, -s))


def swap_blocks(rows, lane_group):
    rows = list(rows)
    for bit in (1, 2, 4):
        low = (lane_group // bit) % 2 == 0
        for i in range(8):
            if i & bit:
                continue
            a, b = rows[i], rows[i + bit]
            rows[i] = jnp.where(low, a, pltpu.roll(b, 16 * bit, 1))
            rows[i + bit] = jnp.where(low, pltpu.roll(a, 128 - 16 * bit, 1), b)
    return rows


def whole_kernel(
    maps_hbm, weight_hbm, len_hbm, order_hbm, order_rows_hbm, leg_hbm, start_hbm, out_ref,
    maps, weight, length_of, order, order_vec, start, leg,
    xs, xr, cs, tp, th, tl, hot, flat_ref, msg, arrived, hx, hy, filtered, back, returned, pb, ndb, got, wide,
    part, parts,
    small_sem, leg_sem, local_sem, send_sem, recv_sem, pix_send, pix_recv, cov_send, cov_recv,
):
    sky = lax.axis_index("sky")
    band = lax.axis_index("band")
    me = sky * 4 + band
    bands = [band] + [lax.rem(band + j, 4) for j in range(1, 4)]
    others = bands[1:]

    small = [
        pltpu.make_async_copy(src, dst, small_sem.at[i])
        for i, (src, dst) in enumerate((
            (maps_hbm, maps), (len_hbm, length_of), (weight_hbm, weight), (order_rows_hbm, order_vec),
            (order_hbm, order), (start_hbm, start),
        ))
    ]
    for copy in small:
        copy.start()
    loads = [pltpu.make_async_copy(leg_hbm.at[i], leg.at[i], leg_sem.at[i]) for i in range(SLOTS)]
    for copy in loads:
        copy.start()

    barrier = pltpu.get_barrier_semaphore()

    def greet(i, carry):
        row = lax.rem(sky + i, 32)
        for column in bands:
            pl.semaphore_signal(barrier, inc=1, device_id=(row, column), device_id_type=MESH)
        return carry

    for column in others:
        pl.semaphore_signal(barrier, inc=1, device_id=(sky, column), device_id_type=MESH)
    lax.fori_loop(1, 32, greet, 0)

    flip = reversal()
    for copy in small:
        copy.wait()
    for tile in range(8):
        xs[tile] = maps[:, tile * 128:tile * 128 + 128]
    for tile in (8, 9, 10):
        xs[tile] = jnp.zeros((BPD * RPD, 128), F32)
        xr[tile] = jnp.zeros((BPD * RPD, 128), F32)
    for block in range(4):
        turned = mm(maps[:, block * QUARTER:(block + 1) * QUARTER], flip, NN, lax.Precision.HIGHEST)
        xr[6 - 2 * block] = turned[:, 0:128]
        xr[7 - 2 * block] = turned[:, 128:256]
    inner, outer = order_rows()
    lane4 = lax.broadcasted_iota(jnp.int32, (BPD, 128), 1)
    pixel = lax.broadcasted_iota(jnp.int32, (BPD, QUARTER), 1)
    quad_group = lax.broadcasted_iota(jnp.int32, (8, 128), 1) // 32

    def window(ref, r, offset):
        tile = offset // 128
        rest = offset - tile * 128
        shift = lax.rem(128 - rest, 128)
        pieces = [pltpu.roll(ref[tile + i, pl.ds(r, BPD, stride=RPD), :], shift, 1) for i in range(3)]
        keep = lane4 < 128 - rest
        return jnp.concatenate(
            [jnp.where(keep, pieces[0], pieces[1]), jnp.where(keep, pieces[1], pieces[2])], axis=1
        )

    def analyse(r, carry):
        length = length_of[r]
        scale = weight[r] * (1.0 / math.sqrt(512 * 1024))
        inside = pixel < length // 4
        x0 = jnp.concatenate([xs[i, pl.ds(r, BPD, stride=RPD), :] for i in range(2)], axis=1)
        x1 = window(xr, r, 1024 - length // 2)
        x2 = window(xs, r, length // 2)
        x3 = window(xr, r, 1024 - length)
        x0, x1, x2, x3 = [jnp.where(inside, v, 0.0) * scale for v in (x0, x1, x2, x3)]
        even = ((x0 + x3) + (x1 + x2), (x0 + x3) - (x1 + x2))
        odd = ((x0 - x3) - (x1 - x2), (x0 - x3) + (x1 - x2))
        cos_p, sin_p = trig_tables(inner, length)
        cos_q, sin_q = trig_tables(outer, length)
        ch, cl = split(cos_q)
        sh, sl = split(sin_q)
        tp[r, 0:32, :] = cos_p
        tp[r, 32:64, :] = sin_p
        th[r] = jnp.concatenate([ch, sh], axis=1)
        tl[r] = jnp.concatenate([cl, sl], axis=1)

        def rows(pair, table):
            pieces = []
            for b in range(BPD):
                for c in range(4):
                    source = pair[c % 2][b:b + 1]
                    pieces.append(jnp.broadcast_to(source, (8, QUARTER)) * table[c * 8:c * 8 + 8])
            return pieces

        minus_sin = -sin_p
        by_cos = split(jnp.concatenate(rows(even, cos_p) + rows(odd, minus_sin), axis=0))
        by_sin = split(jnp.concatenate(rows(even, minus_sin) + rows(odd, -cos_p), axis=0))
        product = mm(
            jnp.concatenate([by_cos[0], by_cos[0], by_cos[1]], axis=1), jnp.concatenate([ch, cl, ch], axis=1), NT
        ) + mm(
            jnp.concatenate([by_sin[0], by_sin[0], by_sin[1]], axis=1), jnp.concatenate([sh, sl, sh], axis=1), NT
        )
        for b in range(BPD):
            for half in range(2):
                base = half * 128 + b * 32
                picked = jnp.concatenate([product[base + c * 8:base + c * 8 + 8] for c in range(4)], axis=1)
                at = pl.multiple_of(((b * 2 + half) * RPD + r) * 8, 8)
                cs[pl.ds(at, 8), :] = picked
        return carry

    def analyse_four(i, carry):
        for j in range(4):
            analyse(4 * i + j, carry)
        return carry

    lax.fori_loop(0, RPD // 4, analyse_four, 0)

    flat = jnp.concatenate([cs[pl.ds(a, 128, stride=8), :].astype(BF) for a in range(8)], axis=1)
    slots = order_vec[...]
    where_to = (slots % 32 // 4 * 128 + slots % 4 * 32 + slots // 32).astype(F32)
    lane128 = lax.broadcasted_iota(jnp.int32, (128, 128), 1).astype(F32)
    for block in range(8):
        target = jnp.broadcast_to(where_to[block:block + 1], (128, 128)).T
        hot[block * 128:block * 128 + 128, :] = jnp.concatenate(
            [jnp.where(target == lane128 + 128.0 * a, 1.0, 0.0).astype(BF) for a in range(8)], axis=1
        )

    def send(src, dst, phase, row, column):
        pltpu.make_async_remote_copy(
            src_ref=src.at[row * 4 + column], dst_ref=dst.at[me], send_sem=send_sem.at[phase],
            recv_sem=recv_sem.at[phase], device_id=(row, column), device_id_type=MESH,
        ).start()

    def sent(src, dst, phase):
        return pltpu.make_async_remote_copy(
            src_ref=src.at[pl.ds(0, NDEV - 1)], dst_ref=dst.at[pl.ds(0, NDEV - 1)], send_sem=send_sem.at[phase],
            recv_sem=recv_sem.at[phase], device_id=(sky, others[0]), device_id_type=MESH,
        )

    def send_rows(src, dst, phase, base, count, here):
        def rows(i, carry):
            row = base + lax.rem(here + i, count)
            for column in bands:
                send(src, dst, phase, row, column)
            return carry

        lax.fori_loop(1, count, rows, 0)
        twin = base + here
        for column in others:
            send(src, dst, phase, twin, column)
        pl.when(twin != sky)(lambda: send(src, dst, phase, twin, band))

    pl.semaphore_wait(barrier, NDEV - 1)

    def slot_half(i, carry):
        half = lax.rem(sky + i, 2)
        moved = mm(hot[pl.ds(pl.multiple_of(half * 512, 512), 512), :], flat_ref[...], NT)
        msg[pl.ds(pl.multiple_of(half * 64, 64), 64)] = moved.reshape(64, SLOTS, 128).astype(BF)
        send_rows(msg, arrived, 0, half * 16, 16, lax.rem(sky, 16))
        return carry

    flat_ref[...] = flat
    lax.fori_loop(0, 2, slot_half, 0)
    own = pltpu.make_async_copy(msg.at[me], arrived.at[me], local_sem)
    own.start()
    out_copies = sent(msg, arrived, 0)
    window_at = lax.broadcasted_iota(jnp.int32, (8, LB), 1).astype(F32)
    taper = window_taper(window_at)[0:1] * (1.0 / math.sqrt(LB))
    degree = lax.broadcasted_iota(jnp.int32, (1, LB), 1) + start[0]
    own.wait()
    out_copies.wait_recv()

    lane_group = lax.broadcasted_iota(jnp.int32, (SLOTS, 128), 1) // 16
    for tile in range(4):
        for source in range(4):
            here = [arrived[(tile * 8 + i) * 4 + source].astype(F32) for i in range(8)]
            for g, val in enumerate(swap_blocks(here, lane_group)):
                at = (source * GROUPS + g) * 8
                hx[tile, at:at + 8, :] = val
    for m in range(SLOTS):
        keep = jnp.where(degree >= order[me * SLOTS + m], taper, 0.0)
        coeff = jnp.concatenate(
            [hx[tile, pl.ds(m, 4 * GROUPS, stride=8), :].astype(BF) for tile in range(4)], axis=1
        )
        loads[m].wait()
        filtered[m] = (mm(coeff, leg[m], NT) * keep).astype(BF)

    def cycle_half(i, carry):
        half = lax.rem(sky + i, 2)
        at = pl.multiple_of(half * QUARTER, QUARTER)
        for m in range(SLOTS):
            result = mm(filtered[m], leg[m, :, pl.ds(at, QUARTER)], NN)
            for side in range(2):
                hy[side, pl.ds(m, 4 * GROUPS, stride=8), :] = result[:, side * 128:side * 128 + 128]
        for side in range(2):
            for source in range(4):
                done = []
                for g in range(GROUPS):
                    row = (source * GROUPS + g) * 8
                    done.append(hy[side, row:row + 8, :])
                for k, val in enumerate(swap_blocks(done, lane_group)):
                    back[(half * 16 + side * 8 + k) * 4 + source] = val.astype(back.dtype)
        send_rows(back, returned, 1, half * 16, 16, lax.rem(sky, 16))
        return carry

    lax.fori_loop(0, 2, cycle_half, 0)
    own_back = pltpu.make_async_copy(back.at[me], returned.at[me], local_sem)
    own_back.start()
    back_copies = sent(back, returned, 1)
    for k in range(4):
        for i in range(3):
            for tile in range(20):
                if tile not in (8, 9, 10):
                    pb[k, i, tile] = jnp.zeros((BPD, 128), F32)
    flip16 = flip.astype(BF)
    own_back.wait()
    back_copies.wait_recv()

    turned = jnp.concatenate(
        [returned[d * 16:d * 16 + 16].astype(F32).reshape(128, 128).T for d in range(8)], axis=1
    )
    stacked = turned.astype(BF)
    lane1 = lax.broadcasted_iota(jnp.int32, (128, 128), 1)
    for pair in range(4):
        moved = mm(stacked, hot[:, pair * QUARTER:(pair + 1) * QUARTER], NN)
        for half in range(2):
            a = pair * 2 + half
            val = moved[:, half * 128:half * 128 + 128]
            if a == 0:
                val = jnp.where(lane1 == 0, 0.5 * val, val)
            cs[pl.ds(a, 128, stride=8), :] = val
    sub = lax.broadcasted_iota(jnp.int32, (8, QUARTER), 0)

    pixel8 = lax.broadcasted_iota(jnp.int32, (8, QUARTER), 1)

    def row_sums(vals):
        for bit in (4, 2, 1):
            low = (sub // bit) % 2 == 0
            merged = []
            for i in range(bit):
                a, b = vals[i], vals[i + bit]
                if bit == 4:
                    merged.append(jnp.where(low, a, b) + pltpu.roll(jnp.where(low, b, a), 4, 0))
                else:
                    here = jnp.where(low, a, b)
                    there = jnp.where(low, b, a)
                    merged.append(here + jnp.where(low, pltpu.roll(there, 8 - bit, 0), pltpu.roll(there, bit, 0)))
            vals = merged
        return vals[0]

    def cycle(r):
        cos_p = tp[r, 0:32, :]
        sin_p = tp[r, 32:64, :]
        table_hi = jnp.concatenate([th[r]] * 4, axis=0)
        table_lo = jnp.concatenate([tl[r]] * 4, axis=0)
        pieces = []
        for g in range(GROUPS):
            at = pl.multiple_of((g * RPD + r) * 8, 8)
            v = cs[pl.ds(at, 8), :]
            for c in range(4):
                pieces.append(jnp.where(quad_group == c, v, 0.0))
        hi = jnp.concatenate(pieces, axis=0).astype(BF)
        full = mm(jnp.concatenate([hi, hi], axis=1), jnp.concatenate([table_hi, table_lo], axis=0), NN)
        quarters = [[], [], [], []]
        for b in range(BPD):
            re = full[(2 * b) * 32:(2 * b) * 32 + 32]
            im = full[(2 * b + 1) * 32:(2 * b + 1) * 32 + 32]
            even = cos_p * re[:, :QUARTER] - sin_p * re[:, QUARTER:]
            odd = cos_p * im[:, QUARTER:] + sin_p * im[:, :QUARTER]
            ce, co = even[0:8] + even[16:24], even[8:16] + even[24:32]
            de, do = odd[0:8] + odd[16:24], odd[8:16] + odd[24:32]
            for i, total in enumerate((ce + co - de - do, ce - co - de + do, ce - co + de - do, ce + co + de + do)):
                quarters[i].append(total)
        inside = pixel8 < length_of[r] // 4
        return [
            jnp.where(inside, row_sums(q) * (2.0 / math.sqrt(M)), 0.0).astype(BF).astype(F32)
            for q in (quarters[0] + quarters[1], quarters[2] + quarters[3])
        ]

    def pixel_copy(d, i):
        return pltpu.make_async_remote_copy(
            src_ref=ndb.at[d, others[i]], dst_ref=got.at[d, band], send_sem=pix_send.at[d, i],
            recv_sem=pix_recv.at[d, i], device_id=(sky, others[i]), device_id_type=MESH,
        )

    def gram_copy(d, i):
        return pltpu.make_async_remote_copy(
            src_ref=part.at[d], dst_ref=parts.at[d, i], send_sem=cov_send.at[d, i], recv_sem=cov_recv.at[d, i],
            device_id=(sky, others[i]), device_id_type=MESH,
        )

    def pixels_of(d):
        cycles = [cycle(d * DOM + k) for k in range(DOM)]
        turned = mm(
            jnp.concatenate([q[1] for q in cycles], axis=0).astype(BF), flip16, NN
        )
        columns = [[] for _ in range(8)]
        for k in range(DOM):
            length = length_of[d * DOM + k]
            tiles = []
            vals = (turned[k * 8:k * 8 + 4], cycles[k][0][4:8], turned[k * 8 + 4:k * 8 + 8])
            for i, offset in enumerate((length // 2 - QUARTER, length // 2, length - QUARTER)):
                tile = (offset + 1024) // 128 - 8
                rest = offset - tile * 128
                low = pltpu.roll(vals[i][:, :128], rest, 1)
                high = pltpu.roll(vals[i][:, 128:], rest, 1)
                wrapped = lane4 < rest
                pb[k, i, 8] = jnp.where(wrapped, 0.0, low)
                pb[k, i, 9] = jnp.where(wrapped, low, high)
                pb[k, i, 10] = jnp.where(wrapped, high, 0.0)
                tiles.append(tile)
            for t in range(8):
                total = pb[k, 0, 8 + t - tiles[0]] + pb[k, 1, 8 + t - tiles[1]] + pb[k, 2, 8 + t - tiles[2]]
                if t < 2:
                    total = total + cycles[k][0][0:4, t * 128:t * 128 + 128]
                columns[t].append(total)
        for t in range(4):
            ndb[d, t] = jnp.concatenate(
                [jnp.concatenate(columns[2 * t + half], axis=0) for half in range(2)], axis=1
            ).astype(BF)
        for i in range(3):
            pixel_copy(d, i).start()
        got[d, band] = ndb[d, band]

    def gram_of(d):
        for i in range(3):
            pixel_copy(d, i).wait_recv()
        for t in range(4):
            val = got[d, t].astype(F32)
            for k in range(DOM):
                for half in range(2):
                    wide[d, k, half, 4 * t:4 * t + 4, :] = val[4 * k:4 * k + 4, half * 128:half * 128 + 128]
        x = jnp.concatenate([wide[d, k, half] for k in range(DOM) for half in range(2)], axis=1).astype(BF)
        tall = jnp.concatenate([x, jnp.zeros((128 - BANDS, x.shape[1]), BF)], axis=0)
        part[d] = mm(x, tall, NT)
        for i in range(3):
            gram_copy(d, i).start()

    def domain(d, carry):
        pixels_of(d)
        return carry

    lax.fori_loop(0, 4, domain, 0)

    for d in range(4):
        gram_of(d)
    row = lax.broadcasted_iota(jnp.int32, (BANDS, 128), 0)
    col = lax.broadcasted_iota(jnp.int32, (BANDS, 128), 1)
    systems = []
    for d in range(4):
        for i in range(3):
            gram_copy(d, i).wait_recv()
        count = length_of[d * DOM] + length_of[d * DOM + 1] + length_of[d * DOM + 2] + length_of[d * DOM + 3]
        cov = (part[d] + parts[d, 1]) + (parts[d, 0] + parts[d, 2])
        cov = cov / jnp.full((1, 128), count, jnp.int32).astype(F32)
        diagonal = jnp.where(row == col, cov, 0.0)
        trace = jnp.sum(jnp.sum(diagonal, axis=1, keepdims=True), axis=0, keepdims=True)
        work = cov + jnp.where(row == col, (RIDGE / BANDS) * trace, 0.0)
        systems.append(jnp.where(col == BANDS, 1.0, work))
    for j in range(BANDS):
        for d in range(4):
            work = systems[d]
            pivot = work[j:j + 1, :] / work[j:j + 1, j:j + 1]
            systems[d] = jnp.where(row == j, pivot, work - work[:, j:j + 1] * pivot)
    for d in range(4):
        solved = systems[d][:, BANDS:BANDS + 1]
        weights = solved / jnp.sum(solved, axis=0, keepdims=True)
        for k in range(DOM):
            at = d * DOM + k
            clean = [jnp.sum(weights * wide[d, k, half], axis=0, keepdims=True) for half in range(2)]
            out_ref[at:at + 1, :] = jnp.concatenate(clean, axis=1)
    out_copies.wait_send()
    back_copies.wait_send()
    for d in range(4):
        for i in range(3):
            pixel_copy(d, i).wait_send()
            gram_copy(d, i).wait_send()


def on_device(band_maps, cycle_weight, cycle_len, m_order, legendre, band_start):
    whole = pl.BlockSpec(memory_space=pl.ANY)
    vmem = pltpu.VMEM
    dma = pltpu.SemaphoreType.DMA
    return pl.pallas_call(
        whole_kernel,
        out_shape=jax.ShapeDtypeStruct((RPD, QUARTER), F32),
        in_specs=[whole] * 7,
        out_specs=pl.BlockSpec(memory_space=vmem),
        scratch_shapes=[
            vmem((BPD * RPD, 4 * QUARTER), F32),
            pltpu.SMEM((RPD,), F32),
            pltpu.SMEM((RPD,), jnp.int32),
            pltpu.SMEM((M,), jnp.int32),
            vmem((8, 128), jnp.int32),
            pltpu.SMEM((1,), jnp.int32),
            vmem((SLOTS, LB, 512), BF),
            vmem((11, BPD * RPD, 128), F32),
            vmem((11, BPD * RPD, 128), F32),
            vmem((M, 128), F32),
            vmem((RPD, 64, QUARTER), F32),
            vmem((RPD, 32, 2 * QUARTER), BF),
            vmem((RPD, 32, 2 * QUARTER), BF),
            vmem((M, M), BF),
            vmem((128, M), BF),
            vmem((NDEV, SLOTS, 128), BF),
            vmem((NDEV, SLOTS, 128), BF),
            vmem((4, 4 * GROUPS * SLOTS, 128), F32),
            vmem((2, 4 * GROUPS * SLOTS, 128), F32),
            vmem((SLOTS, 4 * GROUPS, LB), BF),
            vmem((NDEV, SLOTS, 128), BACK),
            vmem((NDEV, SLOTS, 128), BACK),
            vmem((DOM, 3, 20, BPD, 128), F32),
            vmem((4, 4, 4 * DOM, QUARTER), BF),
            vmem((4, 4, 4 * DOM, QUARTER), BF),
            vmem((4, DOM, 2, BANDS, 128), F32),
            vmem((4, BANDS, 128), F32),
            vmem((4, 3, BANDS, 128), F32),
            dma((6,)),
            dma((SLOTS,)),
            dma,
            dma((2,)),
            dma((2,)),
            dma((4, 3)),
            dma((4, 3)),
            dma((4, 3)),
            dma((4, 3)),
        ],
        compiler_params=pltpu.CompilerParams(
            collective_id=0, has_side_effects=True, vmem_limit_bytes=56 << 20
        ),
        name="needlet_ilc",
    )(
        band_maps.reshape(BPD * RPD, 4 * QUARTER), cycle_weight, cycle_len, m_order, m_order.reshape(8, 128),
        legendre, band_start,
    )


def solution(mesh):
    placed = (P("band", "sky", None), P("sky"), P("sky"), P(), P(("sky", "band"), None, None), P())
    return jax.shard_map(
        on_device, mesh=mesh, in_specs=placed, out_specs=P("sky", "band"), check_vma=False
    )
```

```python
import functools
import math

import jax
import jax.numpy as jnp
from jax import lax
from jax.experimental import pallas as pl
from jax.experimental.pallas import tpu as pltpu
from jax.sharding import PartitionSpec as P

BANDS = 16
M = 1024
LB = 1024
DOM = 4
RIDGE = 0.05
QUARTER = 256
NDEV = 128
BPD = 4
RPD = 16
GROUPS = 2 * BPD
SLOTS = 8
MESH = pl.DeviceIdType.MESH
BF = jnp.bfloat16
F32 = jnp.float32
BACK = jnp.bfloat16
NT = (((1,), (1,)), ((), ()))
NN = (((1,), (0,)), ((), ()))


def mm(a, b, dims, precision=None):
    return lax.dot_general(a, b, dims, precision=precision, preferred_element_type=F32)


def split(x):
    hi = x.astype(BF)
    return hi, (x - hi.astype(F32)).astype(BF)


def trig_tables(order, length):
    pixel = lax.broadcasted_iota(jnp.int32, order.shape, 1)
    turns = order * (2 * pixel + 1).astype(F32)
    lf = jnp.full((1, QUARTER), length, jnp.int32).astype(F32)
    quarter = 0.5 * lf
    count = jnp.floor(turns * (1.0 / quarter) + 0.5)
    y = (turns - count * quarter) * (math.pi / lf)
    z = y * y
    s = ((-1.9515295891e-4 * z + 8.3321608736e-3) * z - 1.6666654611e-1) * z * y + y
    c = ((2.443315711809948e-5 * z - 1.388731625493765e-3) * z + 4.166664568298827e-2) * (z * z) - 0.5 * z + 1.0
    quad = count - 4.0 * jnp.floor(count * 0.25)
    upper = quad >= 2.0
    odd = (quad == 1.0) | (quad == 3.0)
    sin = jnp.where(odd, c, s)
    cos = jnp.where(odd, s, c)
    sin = jnp.where(upper, -sin, sin)
    cos = jnp.where((quad == 1.0) | (quad == 2.0), -cos, cos)
    return cos, sin


def order_rows():
    row = lax.broadcasted_iota(jnp.int32, (32, QUARTER), 0)
    inner = (4 * (row % 8) + row // 8).astype(F32)
    outer = (32 * row).astype(F32)
    return inner, outer


def reversal():
    row = lax.broadcasted_iota(jnp.int32, (QUARTER, QUARTER), 0)
    col = lax.broadcasted_iota(jnp.int32, (QUARTER, QUARTER), 1)
    return jnp.where(row + col == QUARTER - 1, 1.0, 0.0).astype(F32)


def window_taper(window):
    turns = 2.0 * window + 1.0
    count = jnp.floor(turns * (1.0 / LB) + 0.5)
    y = (turns - count * LB) * (math.pi / (2 * LB))
    z = y * y
    s = ((-1.9515295891e-4 * z + 8.3321608736e-3) * z - 1.6666654611e-1) * z * y + y
    c = ((2.443315711809948e-5 * z - 1.388731625493765e-3) * z + 4.166664568298827e-2) * (z * z) - 0.5 * z + 1.0
    return jnp.where(count == 0.0, s, jnp.where(count == 1.0, c, -s))


def swap_blocks(rows, lane_group):
    rows = list(rows)
    for bit in (1, 2, 4):
        low = (lane_group // bit) % 2 == 0
        for i in range(8):
            if i & bit:
                continue
            a, b = rows[i], rows[i + bit]
            rows[i] = jnp.where(low, a, pltpu.roll(b, 16 * bit, 1))
            rows[i + bit] = jnp.where(low, pltpu.roll(a, 128 - 16 * bit, 1), b)
    return rows


def k_reach(chip, reach):
    k, j, x = chip
    return 1 - k + reach[j] + reach[x]


def whole_kernel(
    maps_hbm, weight_hbm, len_hbm, order_hbm, order_rows_hbm, leg_hbm, start_hbm, out_ref,
    maps, weight, length_of, order, order_vec, start, leg,
    xs, xr, cs, tp, th, tl, hot, flat_ref, msg, arrived, hx, hy, filtered, back, returned, pb, ndb, got, wide,
    part, parts,
    small_sem, leg_sem, local_sem, send_sem, recv_sem, pix_send, pix_recv, cov_send, cov_recv,
):
    sky = lax.axis_index("sky")
    band = lax.axis_index("band")
    me = sky * 4 + band
    bands = [lax.rem(band + j, 4) for j in range(4)]
    others = [bands[2], bands[1], bands[3]]
    core = lax.rem(sky, 2)
    layers = [lax.rem(sky // 2 + j, 4) for j in range(4)]

    small = [
        pltpu.make_async_copy(src, dst, small_sem.at[i])
        for i, (src, dst) in enumerate((
            (maps_hbm, maps), (len_hbm, length_of), (weight_hbm, weight), (order_rows_hbm, order_vec),
            (order_hbm, order), (start_hbm, start),
        ))
    ]
    for copy in small:
        copy.start()
    loads = [pltpu.make_async_copy(leg_hbm.at[i], leg.at[i], leg_sem.at[i]) for i in range(SLOTS)]
    for copy in loads:
        copy.start()

    barrier = pltpu.get_barrier_semaphore()

    group = sky // 4
    leader = (lax.rem(sky, 4) == 0) & (band == 0)
    root = (sky == 0) & (band == 0)
    branch = leader & (sky != 0)

    def signal(row, column):
        pl.semaphore_signal(barrier, inc=1, device_id=(row, column), device_id_type=MESH)

    def members():
        for i in range(1, 16):
            signal(group * 4 + i // 4, i % 4)

    def climb():
        pl.semaphore_wait(barrier, 15)
        signal(0, 0)

    def turn():
        pl.semaphore_wait(barrier, 22)
        for i in range(1, 8):
            signal(4 * i, 0)
        members()

    def descend():
        pl.semaphore_wait(barrier, 1)
        members()

    pl.when(jnp.logical_not(leader))(lambda: signal(group * 4, 0))

    flip = reversal()
    for copy in small:
        copy.wait()
    for tile in range(8):
        xs[tile] = maps[:, tile * 128:tile * 128 + 128]
    for tile in (8, 9, 10):
        xs[tile] = jnp.zeros((BPD * RPD, 128), F32)
        xr[tile] = jnp.zeros((BPD * RPD, 128), F32)
    for block in range(4):
        turned = mm(maps[:, block * QUARTER:(block + 1) * QUARTER], flip, NN, lax.Precision.HIGHEST)
        xr[6 - 2 * block] = turned[:, 0:128]
        xr[7 - 2 * block] = turned[:, 128:256]
    inner, outer = order_rows()
    lane4 = lax.broadcasted_iota(jnp.int32, (BPD, 128), 1)
    pixel = lax.broadcasted_iota(jnp.int32, (BPD, QUARTER), 1)
    quad_group = lax.broadcasted_iota(jnp.int32, (8, 128), 1) // 32

    def window(ref, r, offset):
        tile = offset // 128
        rest = offset - tile * 128
        shift = lax.rem(128 - rest, 128)
        pieces = [pltpu.roll(ref[tile + i, pl.ds(r, BPD, stride=RPD), :], shift, 1) for i in range(3)]
        keep = lane4 < 128 - rest
        return jnp.concatenate(
            [jnp.where(keep, pieces[0], pieces[1]), jnp.where(keep, pieces[1], pieces[2])], axis=1
        )

    def analyse(r, carry):
        length = length_of[r]
        scale = weight[r] * (1.0 / math.sqrt(512 * 1024))
        inside = pixel < length // 4
        x0 = jnp.concatenate([xs[i, pl.ds(r, BPD, stride=RPD), :] for i in range(2)], axis=1)
        x1 = window(xr, r, 1024 - length // 2)
        x2 = window(xs, r, length // 2)
        x3 = window(xr, r, 1024 - length)
        x0, x1, x2, x3 = [jnp.where(inside, v, 0.0) * scale for v in (x0, x1, x2, x3)]
        even = ((x0 + x3) + (x1 + x2), (x0 + x3) - (x1 + x2))
        odd = ((x0 - x3) - (x1 - x2), (x0 - x3) + (x1 - x2))
        cos_p, sin_p = trig_tables(inner, length)
        cos_q, sin_q = trig_tables(outer, length)
        ch, cl = split(cos_q)
        sh, sl = split(sin_q)
        tp[r, 0:32, :] = cos_p
        tp[r, 32:64, :] = sin_p
        th[r] = jnp.concatenate([ch, sh], axis=1)
        tl[r] = jnp.concatenate([cl, sl], axis=1)

        def rows(pair, table):
            pieces = []
            for b in range(BPD):
                for c in range(4):
                    source = pair[c % 2][b:b + 1]
                    pieces.append(jnp.broadcast_to(source, (8, QUARTER)) * table[c * 8:c * 8 + 8])
            return pieces

        minus_sin = -sin_p
        by_cos = split(jnp.concatenate(rows(even, cos_p) + rows(odd, minus_sin), axis=0))
        by_sin = split(jnp.concatenate(rows(even, minus_sin) + rows(odd, -cos_p), axis=0))
        product = mm(
            jnp.concatenate([by_cos[0], by_cos[0], by_cos[1]], axis=1), jnp.concatenate([ch, cl, ch], axis=1), NT
        ) + mm(
            jnp.concatenate([by_sin[0], by_sin[0], by_sin[1]], axis=1), jnp.concatenate([sh, sl, sh], axis=1), NT
        )
        for b in range(BPD):
            for half in range(2):
                base = half * 128 + b * 32
                picked = jnp.concatenate([product[base + c * 8:base + c * 8 + 8] for c in range(4)], axis=1)
                at = pl.multiple_of(((b * 2 + half) * RPD + r) * 8, 8)
                cs[pl.ds(at, 8), :] = picked
        return carry

    def analyse_four(i, carry):
        for j in range(4):
            analyse(4 * i + j, carry)
        pl.when(branch & (i == 0))(climb)
        pl.when(root & (i == 1))(turn)
        pl.when(branch & (i == 2))(descend)
        return carry

    lax.fori_loop(0, RPD // 4, analyse_four, 0)

    flat = jnp.concatenate([cs[pl.ds(a, 128, stride=8), :].astype(BF) for a in range(8)], axis=1)
    slots = order_vec[...]
    where_to = (slots % 32 // 4 * 128 + slots % 4 * 32 + slots // 32).astype(F32)
    lane128 = lax.broadcasted_iota(jnp.int32, (128, 128), 1).astype(F32)
    for block in range(8):
        target = jnp.broadcast_to(where_to[block:block + 1], (128, 128)).T
        hot[block * 128:block * 128 + 128, :] = jnp.concatenate(
            [jnp.where(target == lane128 + 128.0 * a, 1.0, 0.0).astype(BF) for a in range(8)], axis=1
        )

    def send(src, dst, phase, row, column):
        pltpu.make_async_remote_copy(
            src_ref=src.at[row * 4 + column], dst_ref=dst.at[me], send_sem=send_sem.at[phase],
            recv_sem=recv_sem.at[phase], device_id=(row, column), device_id_type=MESH,
        ).start()

    def sent(src, dst, phase):
        return pltpu.make_async_remote_copy(
            src_ref=src.at[pl.ds(0, NDEV - 1)], dst_ref=dst.at[pl.ds(0, NDEV - 1)], send_sem=send_sem.at[phase],
            recv_sem=recv_sem.at[phase], device_id=(sky, others[0]), device_id_type=MESH,
        )

    reach = {0: 0, 1: 1, 2: 2, 3: 1}
    chips = sorted(
        ((k, j, x) for k in range(2) for j in range(4) for x in range(4)),
        key=lambda c: k_reach(c, reach), reverse=True,
    )

    def half_of(i):
        return lax.rem(sky // 16 + 1 + i, 2)

    def send_half(src, dst, phase, i):
        half = half_of(i)
        same = half * 2 + lax.rem(sky // 8, 2)
        beside = half * 2 + 1 - lax.rem(sky // 8, 2)
        planes = [jnp.where(i == 0, same, beside), jnp.where(i == 0, beside, same)]
        for k, j, x in chips:
            row = planes[k] * 8 + layers[j] * 2
            send(src, dst, phase, row + 1 - core, bands[x])
            if (k, j, x) == (1, 0, 0):
                pl.when(i == 0)(lambda: send(src, dst, phase, row + core, bands[x]))
            else:
                send(src, dst, phase, row + core, bands[x])

    pl.when(jnp.logical_not(leader))(lambda: pl.semaphore_wait(barrier, 1))

    def slot_half(i, carry):
        half = half_of(i)
        moved = mm(hot[pl.ds(pl.multiple_of(half * 512, 512), 512), :], flat_ref[...], NT)
        msg[pl.ds(pl.multiple_of(half * 64, 64), 64)] = moved.reshape(64, SLOTS, 128).astype(BF)
        send_half(msg, arrived, 0, i)
        return carry

    flat_ref[...] = flat
    lax.fori_loop(0, 2, slot_half, 0)
    own = pltpu.make_async_copy(msg.at[me], arrived.at[me], local_sem)
    own.start()
    out_copies = sent(msg, arrived, 0)
    window_at = lax.broadcasted_iota(jnp.int32, (8, LB), 1).astype(F32)
    taper = window_taper(window_at)[0:1] * (1.0 / math.sqrt(LB))
    degree = lax.broadcasted_iota(jnp.int32, (1, LB), 1) + start[0]
    own.wait()
    out_copies.wait_recv()

    lane_group = lax.broadcasted_iota(jnp.int32, (SLOTS, 128), 1) // 16
    for tile in range(4):
        for source in range(4):
            here = [arrived[(tile * 8 + i) * 4 + source].astype(F32) for i in range(8)]
            for g, val in enumerate(swap_blocks(here, lane_group)):
                at = (source * GROUPS + g) * 8
                hx[tile, at:at + 8, :] = val
    for m in range(SLOTS):
        keep = jnp.where(degree >= order[me * SLOTS + m], taper, 0.0)
        coeff = jnp.concatenate(
            [hx[tile, pl.ds(m, 4 * GROUPS, stride=8), :].astype(BF) for tile in range(4)], axis=1
        )
        loads[m].wait()
        filtered[m] = (mm(coeff, leg[m], NT) * keep).astype(BF)

    def cycle_half(i, carry):
        half = half_of(i)
        at = pl.multiple_of(half * QUARTER, QUARTER)
        for m in range(SLOTS):
            result = mm(filtered[m], leg[m, :, pl.ds(at, QUARTER)], NN)
            for side in range(2):
                hy[side, pl.ds(m, 4 * GROUPS, stride=8), :] = result[:, side * 128:side * 128 + 128]
        for side in range(2):
            for source in range(4):
                done = []
                for g in range(GROUPS):
                    row = (source * GROUPS + g) * 8
                    done.append(hy[side, row:row + 8, :])
                for k, val in enumerate(swap_blocks(done, lane_group)):
                    back[(half * 16 + side * 8 + k) * 4 + source] = val.astype(back.dtype)
        send_half(back, returned, 1, i)
        return carry

    lax.fori_loop(0, 2, cycle_half, 0)
    own_back = pltpu.make_async_copy(back.at[me], returned.at[me], local_sem)
    own_back.start()
    back_copies = sent(back, returned, 1)
    for k in range(4):
        for i in range(3):
            for tile in range(20):
                if tile not in (8, 9, 10):
                    pb[k, i, tile] = jnp.zeros((BPD, 128), F32)
    flip16 = flip.astype(BF)
    own_back.wait()
    back_copies.wait_recv()

    turned = jnp.concatenate(
        [returned[d * 16:d * 16 + 16].astype(F32).reshape(128, 128).T for d in range(8)], axis=1
    )
    stacked = turned.astype(BF)
    lane1 = lax.broadcasted_iota(jnp.int32, (128, 128), 1)
    for pair in range(4):
        moved = mm(stacked, hot[:, pair * QUARTER:(pair + 1) * QUARTER], NN)
        for half in range(2):
            a = pair * 2 + half
            val = moved[:, half * 128:half * 128 + 128]
            if a == 0:
                val = jnp.where(lane1 == 0, 0.5 * val, val)
            cs[pl.ds(a, 128, stride=8), :] = val
    sub = lax.broadcasted_iota(jnp.int32, (8, QUARTER), 0)

    pixel8 = lax.broadcasted_iota(jnp.int32, (8, QUARTER), 1)

    def row_sums(vals):
        for bit in (4, 2, 1):
            low = (sub // bit) % 2 == 0
            merged = []
            for i in range(bit):
                a, b = vals[i], vals[i + bit]
                if bit == 4:
                    merged.append(jnp.where(low, a, b) + pltpu.roll(jnp.where(low, b, a), 4, 0))
                else:
                    here = jnp.where(low, a, b)
                    there = jnp.where(low, b, a)
                    merged.append(here + jnp.where(low, pltpu.roll(there, 8 - bit, 0), pltpu.roll(there, bit, 0)))
            vals = merged
        return vals[0]

    def cycle(r):
        cos_p = tp[r, 0:32, :]
        sin_p = tp[r, 32:64, :]
        table_hi = jnp.concatenate([th[r]] * 4, axis=0)
        table_lo = jnp.concatenate([tl[r]] * 4, axis=0)
        pieces = []
        for g in range(GROUPS):
            at = pl.multiple_of((g * RPD + r) * 8, 8)
            v = cs[pl.ds(at, 8), :]
            for c in range(4):
                pieces.append(jnp.where(quad_group == c, v, 0.0))
        hi = jnp.concatenate(pieces, axis=0).astype(BF)
        full = mm(jnp.concatenate([hi, hi], axis=1), jnp.concatenate([table_hi, table_lo], axis=0), NN)
        quarters = [[], [], [], []]
        for b in range(BPD):
            re = full[(2 * b) * 32:(2 * b) * 32 + 32]
            im = full[(2 * b + 1) * 32:(2 * b + 1) * 32 + 32]
            even = cos_p * re[:, :QUARTER] - sin_p * re[:, QUARTER:]
            odd = cos_p * im[:, QUARTER:] + sin_p * im[:, :QUARTER]
            ce, co = even[0:8] + even[16:24], even[8:16] + even[24:32]
            de, do = odd[0:8] + odd[16:24], odd[8:16] + odd[24:32]
            for i, total in enumerate((ce + co - de - do, ce - co - de + do, ce - co + de - do, ce + co + de + do)):
                quarters[i].append(total)
        inside = pixel8 < length_of[r] // 4
        return [
            jnp.where(inside, row_sums(q) * (2.0 / math.sqrt(M)), 0.0).astype(BF).astype(F32)
            for q in (quarters[0] + quarters[1], quarters[2] + quarters[3])
        ]

    def pixel_copy(d, i):
        return pltpu.make_async_remote_copy(
            src_ref=ndb.at[d, others[i]], dst_ref=got.at[d, band], send_sem=pix_send.at[d, i],
            recv_sem=pix_recv.at[d, i], device_id=(sky, others[i]), device_id_type=MESH,
        )

    def gram_copy(d, i):
        return pltpu.make_async_remote_copy(
            src_ref=part.at[d], dst_ref=parts.at[d, i], send_sem=cov_send.at[d, i], recv_sem=cov_recv.at[d, i],
            device_id=(sky, others[i]), device_id_type=MESH,
        )

    def pixels_of(d):
        cycles = [cycle(d * DOM + k) for k in range(DOM)]
        turned = mm(
            jnp.concatenate([q[1] for q in cycles], axis=0).astype(BF), flip16, NN
        )
        columns = [[] for _ in range(8)]
        for k in range(DOM):
            length = length_of[d * DOM + k]
            tiles = []
            vals = (turned[k * 8:k * 8 + 4], cycles[k][0][4:8], turned[k * 8 + 4:k * 8 + 8])
            for i, offset in enumerate((length // 2 - QUARTER, length // 2, length - QUARTER)):
                tile = (offset + 1024) // 128 - 8
                rest = offset - tile * 128
                low = pltpu.roll(vals[i][:, :128], rest, 1)
                high = pltpu.roll(vals[i][:, 128:], rest, 1)
                wrapped = lane4 < rest
                pb[k, i, 8] = jnp.where(wrapped, 0.0, low)
                pb[k, i, 9] = jnp.where(wrapped, low, high)
                pb[k, i, 10] = jnp.where(wrapped, high, 0.0)
                tiles.append(tile)
            for t in range(8):
                total = pb[k, 0, 8 + t - tiles[0]] + pb[k, 1, 8 + t - tiles[1]] + pb[k, 2, 8 + t - tiles[2]]
                if t < 2:
                    total = total + cycles[k][0][0:4, t * 128:t * 128 + 128]
                columns[t].append(total)
        for t in range(4):
            ndb[d, t] = jnp.concatenate(
                [jnp.concatenate(columns[2 * t + half], axis=0) for half in range(2)], axis=1
            ).astype(BF)
        for i in range(3):
            pixel_copy(d, i).start()
        got[d, band] = ndb[d, band]

    def gram_of(d):
        for i in range(3):
            pixel_copy(d, i).wait_recv()
        for t in range(4):
            val = got[d, t].astype(F32)
            for k in range(DOM):
                for half in range(2):
                    wide[d, k, half, 4 * t:4 * t + 4, :] = val[4 * k:4 * k + 4, half * 128:half * 128 + 128]
        x = jnp.concatenate([wide[d, k, half] for k in range(DOM) for half in range(2)], axis=1).astype(BF)
        tall = jnp.concatenate([x, jnp.zeros((128 - BANDS, x.shape[1]), BF)], axis=0)
        part[d] = mm(x, tall, NT)
        for i in range(3):
            gram_copy(d, i).start()

    def domain(d, carry):
        pixels_of(d)
        return carry

    lax.fori_loop(0, 4, domain, 0)

    for d in range(4):
        gram_of(d)
    row = lax.broadcasted_iota(jnp.int32, (BANDS, 128), 0)
    col = lax.broadcasted_iota(jnp.int32, (BANDS, 128), 1)
    systems = []
    for d in range(4):
        for i in range(3):
            gram_copy(d, i).wait_recv()
        count = length_of[d * DOM] + length_of[d * DOM + 1] + length_of[d * DOM + 2] + length_of[d * DOM + 3]
        cov = (part[d] + parts[d, 1]) + (parts[d, 0] + parts[d, 2])
        cov = cov / jnp.full((1, 128), count, jnp.int32).astype(F32)
        diagonal = jnp.where(row == col, cov, 0.0)
        trace = jnp.sum(jnp.sum(diagonal, axis=1, keepdims=True), axis=0, keepdims=True)
        work = cov + jnp.where(row == col, (RIDGE / BANDS) * trace, 0.0)
        systems.append(jnp.where(col == BANDS, 1.0, work))
    for j in range(BANDS):
        for d in range(4):
            work = systems[d]
            pivot = work[j:j + 1, :] / work[j:j + 1, j:j + 1]
            systems[d] = jnp.where(row == j, pivot, work - work[:, j:j + 1] * pivot)
    for d in range(4):
        solved = systems[d][:, BANDS:BANDS + 1]
        weights = solved / jnp.sum(solved, axis=0, keepdims=True)
        for k in range(DOM):
            at = d * DOM + k
            clean = [jnp.sum(weights * wide[d, k, half], axis=0, keepdims=True) for half in range(2)]
            out_ref[at:at + 1, :] = jnp.concatenate(clean, axis=1)
    out_copies.wait_send()
    back_copies.wait_send()
    for d in range(4):
        for i in range(3):
            pixel_copy(d, i).wait_send()
            gram_copy(d, i).wait_send()


def on_device(band_maps, cycle_weight, cycle_len, m_order, legendre, band_start):
    whole = pl.BlockSpec(memory_space=pl.ANY)
    vmem = pltpu.VMEM
    dma = pltpu.SemaphoreType.DMA
    return pl.pallas_call(
        whole_kernel,
        out_shape=jax.ShapeDtypeStruct((RPD, QUARTER), F32),
        in_specs=[whole] * 7,
        out_specs=pl.BlockSpec(memory_space=vmem),
        scratch_shapes=[
            vmem((BPD * RPD, 4 * QUARTER), F32),
            pltpu.SMEM((RPD,), F32),
            pltpu.SMEM((RPD,), jnp.int32),
            pltpu.SMEM((M,), jnp.int32),
            vmem((8, 128), jnp.int32),
            pltpu.SMEM((1,), jnp.int32),
            vmem((SLOTS, LB, 512), BF),
            vmem((11, BPD * RPD, 128), F32),
            vmem((11, BPD * RPD, 128), F32),
            vmem((M, 128), F32),
            vmem((RPD, 64, QUARTER), F32),
            vmem((RPD, 32, 2 * QUARTER), BF),
            vmem((RPD, 32, 2 * QUARTER), BF),
            vmem((M, M), BF),
            vmem((128, M), BF),
            vmem((NDEV, SLOTS, 128), BF),
            vmem((NDEV, SLOTS, 128), BF),
            vmem((4, 4 * GROUPS * SLOTS, 128), F32),
            vmem((2, 4 * GROUPS * SLOTS, 128), F32),
            vmem((SLOTS, 4 * GROUPS, LB), BF),
            vmem((NDEV, SLOTS, 128), BACK),
            vmem((NDEV, SLOTS, 128), BACK),
            vmem((DOM, 3, 20, BPD, 128), F32),
            vmem((4, 4, 4 * DOM, QUARTER), BF),
            vmem((4, 4, 4 * DOM, QUARTER), BF),
            vmem((4, DOM, 2, BANDS, 128), F32),
            vmem((4, BANDS, 128), F32),
            vmem((4, 3, BANDS, 128), F32),
            dma((6,)),
            dma((SLOTS,)),
            dma,
            dma((2,)),
            dma((2,)),
            dma((4, 3)),
            dma((4, 3)),
            dma((4, 3)),
            dma((4, 3)),
        ],
        compiler_params=pltpu.CompilerParams(
            collective_id=0, has_side_effects=True, vmem_limit_bytes=56 << 20
        ),
        name="needlet_ilc",
    )(
        band_maps.reshape(BPD * RPD, 4 * QUARTER), cycle_weight, cycle_len, m_order, m_order.reshape(8, 128),
        legendre, band_start,
    )


def solution(mesh):
    placed = (P("band", "sky", None), P("sky"), P("sky"), P(), P(("sky", "band"), None, None), P())
    return jax.shard_map(
        on_device, mesh=mesh, in_specs=placed, out_specs=P("sky", "band"), check_vma=False
    )
```

```python
import functools
import math

import jax
import jax.numpy as jnp
from jax import lax
from jax.experimental import pallas as pl
from jax.experimental.pallas import tpu as pltpu
from jax.sharding import PartitionSpec as P

BANDS = 16
M = 1024
LB = 1024
DOM = 4
RIDGE = 0.05
QUARTER = 256
NDEV = 128
HALF = 64
BPD = 4
RPD = 16
GROUPS = 2 * BPD
SLOTS = 8
MESH = pl.DeviceIdType.MESH
BF = jnp.bfloat16
F32 = jnp.float32
BACK = jnp.bfloat16
NT = (((1,), (1,)), ((), ()))
NN = (((1,), (0,)), ((), ()))


def mm(a, b, dims, precision=None):
    return lax.dot_general(a, b, dims, precision=precision, preferred_element_type=F32)


def split(x):
    hi = x.astype(BF)
    return hi, (x - hi.astype(F32)).astype(BF)


def trig_tables(order, length):
    pixel = lax.broadcasted_iota(jnp.int32, order.shape, 1)
    turns = order * (2 * pixel + 1).astype(F32)
    lf = jnp.full((1, QUARTER), length, jnp.int32).astype(F32)
    quarter = 0.5 * lf
    count = jnp.floor(turns * (1.0 / quarter) + 0.5)
    y = (turns - count * quarter) * (math.pi / lf)
    z = y * y
    s = ((-1.9515295891e-4 * z + 8.3321608736e-3) * z - 1.6666654611e-1) * z * y + y
    c = ((2.443315711809948e-5 * z - 1.388731625493765e-3) * z + 4.166664568298827e-2) * (z * z) - 0.5 * z + 1.0
    quad = count - 4.0 * jnp.floor(count * 0.25)
    upper = quad >= 2.0
    odd = (quad == 1.0) | (quad == 3.0)
    sin = jnp.where(odd, c, s)
    cos = jnp.where(odd, s, c)
    sin = jnp.where(upper, -sin, sin)
    cos = jnp.where((quad == 1.0) | (quad == 2.0), -cos, cos)
    return cos, sin


def order_rows():
    row = lax.broadcasted_iota(jnp.int32, (32, QUARTER), 0)
    inner = (4 * (row % 8) + row // 8).astype(F32)
    outer = (32 * row).astype(F32)
    return inner, outer


def reversal():
    row = lax.broadcasted_iota(jnp.int32, (QUARTER, QUARTER), 0)
    col = lax.broadcasted_iota(jnp.int32, (QUARTER, QUARTER), 1)
    return jnp.where(row + col == QUARTER - 1, 1.0, 0.0).astype(F32)


def window_taper(window):
    turns = 2.0 * window + 1.0
    count = jnp.floor(turns * (1.0 / LB) + 0.5)
    y = (turns - count * LB) * (math.pi / (2 * LB))
    z = y * y
    s = ((-1.9515295891e-4 * z + 8.3321608736e-3) * z - 1.6666654611e-1) * z * y + y
    c = ((2.443315711809948e-5 * z - 1.388731625493765e-3) * z + 4.166664568298827e-2) * (z * z) - 0.5 * z + 1.0
    return jnp.where(count == 0.0, s, jnp.where(count == 1.0, c, -s))


def swap_blocks(rows, lane_group):
    rows = list(rows)
    for bit in (1, 2, 4):
        low = (lane_group // bit) % 2 == 0
        for i in range(8):
            if i & bit:
                continue
            a, b = rows[i], rows[i + bit]
            rows[i] = jnp.where(low, a, pltpu.roll(b, 16 * bit, 1))
            rows[i + bit] = jnp.where(low, pltpu.roll(a, 128 - 16 * bit, 1), b)
    return rows


def k_reach(chip, reach):
    k, j, x = chip
    return 1 - k + reach[j] + reach[x]


def whole_kernel(
    maps_hbm, weight_hbm, len_hbm, order_hbm, order_rows_hbm, leg_hbm, start_hbm, out_ref,
    maps, weight, length_of, order, order_vec, start, leg,
    xs, xr, cs, tp, th, tl, hot, flat_ref, msg, arrived, hx, hy, partial, filtered, early, back, returned, pb, ndb, got, wide,
    part, parts,
    small_sem, leg_sem, local_sem, send_sem, recv_sem, pix_send, pix_recv, cov_send, cov_recv,
):
    sky = lax.axis_index("sky")
    band = lax.axis_index("band")
    me = sky * 4 + band
    bands = [lax.rem(band + j, 4) for j in range(4)]
    others = [bands[2], bands[1], bands[3]]
    core = lax.rem(sky, 2)
    layers = [lax.rem(sky // 2 + j, 4) for j in range(4)]

    small = [
        pltpu.make_async_copy(src, dst, small_sem.at[i])
        for i, (src, dst) in enumerate((
            (maps_hbm, maps), (len_hbm, length_of), (weight_hbm, weight), (order_rows_hbm, order_vec),
            (order_hbm, order), (start_hbm, start),
        ))
    ]
    for copy in small:
        copy.start()
    loads = [pltpu.make_async_copy(leg_hbm.at[i], leg.at[i], leg_sem.at[i]) for i in range(SLOTS)]
    for copy in loads:
        copy.start()

    barrier = pltpu.get_barrier_semaphore()

    def greet(i, carry):
        row = lax.rem(sky + i, 32)
        for column in bands:
            pl.semaphore_signal(barrier, inc=1, device_id=(row, column), device_id_type=MESH)
        return carry

    for column in others:
        pl.semaphore_signal(barrier, inc=1, device_id=(sky, column), device_id_type=MESH)
    lax.fori_loop(1, 32, greet, 0)

    flip = reversal()
    for copy in small:
        copy.wait()
    for tile in range(8):
        xs[tile] = maps[:, tile * 128:tile * 128 + 128]
    for tile in (8, 9, 10):
        xs[tile] = jnp.zeros((BPD * RPD, 128), F32)
        xr[tile] = jnp.zeros((BPD * RPD, 128), F32)
    for block in range(4):
        turned = mm(maps[:, block * QUARTER:(block + 1) * QUARTER], flip, NN, lax.Precision.HIGHEST)
        xr[6 - 2 * block] = turned[:, 0:128]
        xr[7 - 2 * block] = turned[:, 128:256]
    inner, outer = order_rows()
    lane4 = lax.broadcasted_iota(jnp.int32, (BPD, 128), 1)
    pixel = lax.broadcasted_iota(jnp.int32, (BPD, QUARTER), 1)
    quad_group = lax.broadcasted_iota(jnp.int32, (8, 128), 1) // 32

    def window(ref, r, offset):
        tile = offset // 128
        rest = offset - tile * 128
        shift = lax.rem(128 - rest, 128)
        pieces = [pltpu.roll(ref[tile + i, pl.ds(r, BPD, stride=RPD), :], shift, 1) for i in range(3)]
        keep = lane4 < 128 - rest
        return jnp.concatenate(
            [jnp.where(keep, pieces[0], pieces[1]), jnp.where(keep, pieces[1], pieces[2])], axis=1
        )

    def analyse(r, carry):
        length = length_of[r]
        scale = weight[r] * (1.0 / math.sqrt(512 * 1024))
        inside = pixel < length // 4
        x0 = jnp.concatenate([xs[i, pl.ds(r, BPD, stride=RPD), :] for i in range(2)], axis=1)
        x1 = window(xr, r, 1024 - length // 2)
        x2 = window(xs, r, length // 2)
        x3 = window(xr, r, 1024 - length)
        x0, x1, x2, x3 = [jnp.where(inside, v, 0.0) * scale for v in (x0, x1, x2, x3)]
        even = ((x0 + x3) + (x1 + x2), (x0 + x3) - (x1 + x2))
        odd = ((x0 - x3) - (x1 - x2), (x0 - x3) + (x1 - x2))
        cos_p, sin_p = trig_tables(inner, length)
        cos_q, sin_q = trig_tables(outer, length)
        ch, cl = split(cos_q)
        sh, sl = split(sin_q)
        tp[r, 0:32, :] = cos_p
        tp[r, 32:64, :] = sin_p
        th[r] = jnp.concatenate([ch, sh], axis=1)
        tl[r] = jnp.concatenate([cl, sl], axis=1)

        def rows(pair, table):
            pieces = []
            for b in range(BPD):
                for c in range(4):
                    source = pair[c % 2][b:b + 1]
                    pieces.append(jnp.broadcast_to(source, (8, QUARTER)) * table[c * 8:c * 8 + 8])
            return pieces

        minus_sin = -sin_p
        by_cos = split(jnp.concatenate(rows(even, cos_p) + rows(odd, minus_sin), axis=0))
        by_sin = split(jnp.concatenate(rows(even, minus_sin) + rows(odd, -cos_p), axis=0))
        product = mm(
            jnp.concatenate([by_cos[0], by_cos[0], by_cos[1]], axis=1), jnp.concatenate([ch, cl, ch], axis=1), NT
        ) + mm(
            jnp.concatenate([by_sin[0], by_sin[0], by_sin[1]], axis=1), jnp.concatenate([sh, sl, sh], axis=1), NT
        )
        for b in range(BPD):
            for half in range(2):
                base = half * 128 + b * 32
                picked = jnp.concatenate([product[base + c * 8:base + c * 8 + 8] for c in range(4)], axis=1)
                at = pl.multiple_of(((b * 2 + half) * RPD + r) * 8, 8)
                cs[pl.ds(at, 8), :] = picked
        return carry

    def analyse_four(i, carry):
        for j in range(4):
            analyse(4 * i + j, carry)
        return carry

    lax.fori_loop(0, RPD // 4, analyse_four, 0)

    flat = jnp.concatenate([cs[pl.ds(a, 128, stride=8), :].astype(BF) for a in range(8)], axis=1)
    slots = order_vec[...]
    where_to = (slots % 32 // 4 * 128 + slots % 4 * 32 + slots // 32).astype(F32)
    lane128 = lax.broadcasted_iota(jnp.int32, (128, 128), 1).astype(F32)
    for block in range(8):
        target = jnp.broadcast_to(where_to[block:block + 1], (128, 128)).T
        hot[block * 128:block * 128 + 128, :] = jnp.concatenate(
            [jnp.where(target == lane128 + 128.0 * a, 1.0, 0.0).astype(BF) for a in range(8)], axis=1
        )

    def send(src, dst, phase, i, row, column):
        pltpu.make_async_remote_copy(
            src_ref=src.at[row * 4 + column], dst_ref=dst.at[me], send_sem=send_sem.at[phase],
            recv_sem=recv_sem.at[phase, i], device_id=(row, column), device_id_type=MESH,
        ).start()

    def sent(src, dst, phase, i, count):
        return pltpu.make_async_remote_copy(
            src_ref=src.at[pl.ds(0, count)], dst_ref=dst.at[pl.ds(0, count)], send_sem=send_sem.at[phase],
            recv_sem=recv_sem.at[phase, i], device_id=(sky, others[0]), device_id_type=MESH,
        )

    reach = {0: 0, 1: 1, 2: 2, 3: 1}
    chips = sorted(
        ((k, j, x) for k in range(2) for j in range(4) for x in range(4)),
        key=lambda c: k_reach(c, reach), reverse=True,
    )

    def half_of(i):
        return lax.rem(sky // 16 + 1 + i, 2)

    def send_half(src, dst, phase, i):
        half = half_of(i)
        same = half * 2 + lax.rem(sky // 8, 2)
        beside = half * 2 + 1 - lax.rem(sky // 8, 2)
        planes = [jnp.where(i == 0, same, beside), jnp.where(i == 0, beside, same)]
        for k, j, x in chips:
            row = planes[k] * 8 + layers[j] * 2
            send(src, dst, phase, i, row + 1 - core, bands[x])
            if (k, j, x) == (1, 0, 0):
                pl.when(i == 0)(lambda: send(src, dst, phase, i, row + core, bands[x]))
            else:
                send(src, dst, phase, i, row + core, bands[x])

    pl.semaphore_wait(barrier, NDEV - 1)

    def slot_half(i, carry):
        half = half_of(i)
        moved = mm(hot[pl.ds(pl.multiple_of(half * 512, 512), 512), :], flat_ref[...], NT)
        msg[pl.ds(pl.multiple_of(half * 64, 64), 64)] = moved.reshape(64, SLOTS, 128).astype(BF)
        send_half(msg, arrived, 0, i)
        return carry

    flat_ref[...] = flat
    lax.fori_loop(0, 2, slot_half, 0)
    own = pltpu.make_async_copy(msg.at[me], arrived.at[me], local_sem)
    own.start()
    window_at = lax.broadcasted_iota(jnp.int32, (8, LB), 1).astype(F32)
    taper = window_taper(window_at)[0:1] * (1.0 / math.sqrt(LB))
    degree = lax.broadcasted_iota(jnp.int32, (1, LB), 1) + start[0]
    own.wait()

    lane_group = lax.broadcasted_iota(jnp.int32, (SLOTS, 128), 1) // 16
    for i in range(2):
        half = half_of(i)
        sent(msg, arrived, 0, i, HALF - i).wait_recv()
        for side in range(2):
            for source in range(4):
                here = [arrived[(half * 16 + side * 8 + k) * 4 + source].astype(F32) for k in range(8)]
                for g, val in enumerate(swap_blocks(here, lane_group)):
                    at = (source * GROUPS + g) * 8
                    hx[2 * i + side, at:at + 8, :] = val
        at = pl.multiple_of(half * QUARTER, QUARTER)
        for m in range(SLOTS):
            coeff = jnp.concatenate(
                [hx[2 * i + side, pl.ds(m, 4 * GROUPS, stride=8), :].astype(BF) for side in range(2)], axis=1
            )
            if i == 0:
                loads[m].wait()
            share = mm(coeff, leg[m, :, pl.ds(at, QUARTER)], NT)
            if i == 0:
                partial[m] = share
            else:
                keep = jnp.where(degree >= order[me * SLOTS + m], taper, 0.0)
                filtered[m] = ((partial[m] + share) * keep).astype(BF)

    def cycle_half(i, carry):
        half = half_of(i)
        at = pl.multiple_of(half * QUARTER, QUARTER)
        for m in range(SLOTS):
            result = mm(filtered[m], leg[m, :, pl.ds(at, QUARTER)], NN)
            for side in range(2):
                hy[side, pl.ds(m, 4 * GROUPS, stride=8), :] = result[:, side * 128:side * 128 + 128]
        for side in range(2):
            for source in range(4):
                done = []
                for g in range(GROUPS):
                    row = (source * GROUPS + g) * 8
                    done.append(hy[side, row:row + 8, :])
                for k, val in enumerate(swap_blocks(done, lane_group)):
                    back[(half * 16 + side * 8 + k) * 4 + source] = val.astype(back.dtype)
        send_half(back, returned, 1, i)
        return carry

    lax.fori_loop(0, 2, cycle_half, 0)
    own_back = pltpu.make_async_copy(back.at[me], returned.at[me], local_sem)
    own_back.start()
    for k in range(4):
        for i in range(3):
            for tile in range(20):
                if tile not in (8, 9, 10):
                    pb[k, i, tile] = jnp.zeros((BPD, 128), F32)
    flip16 = flip.astype(BF)
    own_back.wait()

    lane1 = lax.broadcasted_iota(jnp.int32, (128, 128), 1)
    for i in range(2):
        half = half_of(i)
        sent(back, returned, 1, i, HALF - i).wait_recv()
        turned = jnp.concatenate(
            [returned[pl.ds(half * HALF + d * 16, 16)].astype(F32).reshape(128, 128).T for d in range(4)], axis=1
        ).astype(BF)
        at = half * 512
        for pair in range(4):
            lanes = slice(pair * QUARTER, (pair + 1) * QUARTER)
            moved = mm(turned, hot[pl.ds(pl.multiple_of(at, 512), 512), lanes], NN)
            if i == 0:
                early[:, lanes] = moved
                continue
            moved = moved + early[:, lanes]
            for side in range(2):
                a = pair * 2 + side
                val = moved[:, side * 128:side * 128 + 128]
                if a == 0:
                    val = jnp.where(lane1 == 0, 0.5 * val, val)
                cs[pl.ds(a, 128, stride=8), :] = val
    sub = lax.broadcasted_iota(jnp.int32, (8, QUARTER), 0)
    pixel8 = lax.broadcasted_iota(jnp.int32, (8, QUARTER), 1)

    def row_sums(vals):
        for bit in (4, 2, 1):
            low = (sub // bit) % 2 == 0
            merged = []
            for i in range(bit):
                a, b = vals[i], vals[i + bit]
                if bit == 4:
                    merged.append(jnp.where(low, a, b) + pltpu.roll(jnp.where(low, b, a), 4, 0))
                else:
                    here = jnp.where(low, a, b)
                    there = jnp.where(low, b, a)
                    merged.append(here + jnp.where(low, pltpu.roll(there, 8 - bit, 0), pltpu.roll(there, bit, 0)))
            vals = merged
        return vals[0]

    def cycle(r):
        cos_p = tp[r, 0:32, :]
        sin_p = tp[r, 32:64, :]
        table_hi = jnp.concatenate([th[r]] * 4, axis=0)
        table_lo = jnp.concatenate([tl[r]] * 4, axis=0)
        pieces = []
        for g in range(GROUPS):
            at = pl.multiple_of((g * RPD + r) * 8, 8)
            v = cs[pl.ds(at, 8), :]
            for c in range(4):
                pieces.append(jnp.where(quad_group == c, v, 0.0))
        hi = jnp.concatenate(pieces, axis=0).astype(BF)
        full = mm(jnp.concatenate([hi, hi], axis=1), jnp.concatenate([table_hi, table_lo], axis=0), NN)
        quarters = [[], [], [], []]
        for b in range(BPD):
            re = full[(2 * b) * 32:(2 * b) * 32 + 32]
            im = full[(2 * b + 1) * 32:(2 * b + 1) * 32 + 32]
            even = cos_p * re[:, :QUARTER] - sin_p * re[:, QUARTER:]
            odd = cos_p * im[:, QUARTER:] + sin_p * im[:, :QUARTER]
            ce, co = even[0:8] + even[16:24], even[8:16] + even[24:32]
            de, do = odd[0:8] + odd[16:24], odd[8:16] + odd[24:32]
            for i, total in enumerate((ce + co - de - do, ce - co - de + do, ce - co + de - do, ce + co + de + do)):
                quarters[i].append(total)
        inside = pixel8 < length_of[r] // 4
        return [
            jnp.where(inside, row_sums(q) * (2.0 / math.sqrt(M)), 0.0).astype(BF).astype(F32)
            for q in (quarters[0] + quarters[1], quarters[2] + quarters[3])
        ]

    def pixel_copy(d, i):
        return pltpu.make_async_remote_copy(
            src_ref=ndb.at[d, others[i]], dst_ref=got.at[d, band], send_sem=pix_send.at[d, i],
            recv_sem=pix_recv.at[d, i], device_id=(sky, others[i]), device_id_type=MESH,
        )

    def gram_copy(d, i):
        return pltpu.make_async_remote_copy(
            src_ref=part.at[d], dst_ref=parts.at[d, i], send_sem=cov_send.at[d, i], recv_sem=cov_recv.at[d, i],
            device_id=(sky, others[i]), device_id_type=MESH,
        )

    def pixels_of(d):
        cycles = [cycle(d * DOM + k) for k in range(DOM)]
        turned = mm(
            jnp.concatenate([q[1] for q in cycles], axis=0).astype(BF), flip16, NN
        )
        columns = [[] for _ in range(8)]
        for k in range(DOM):
            length = length_of[d * DOM + k]
            tiles = []
            vals = (turned[k * 8:k * 8 + 4], cycles[k][0][4:8], turned[k * 8 + 4:k * 8 + 8])
            for i, offset in enumerate((length // 2 - QUARTER, length // 2, length - QUARTER)):
                tile = (offset + 1024) // 128 - 8
                rest = offset - tile * 128
                low = pltpu.roll(vals[i][:, :128], rest, 1)
                high = pltpu.roll(vals[i][:, 128:], rest, 1)
                wrapped = lane4 < rest
                pb[k, i, 8] = jnp.where(wrapped, 0.0, low)
                pb[k, i, 9] = jnp.where(wrapped, low, high)
                pb[k, i, 10] = jnp.where(wrapped, high, 0.0)
                tiles.append(tile)
            for t in range(8):
                total = pb[k, 0, 8 + t - tiles[0]] + pb[k, 1, 8 + t - tiles[1]] + pb[k, 2, 8 + t - tiles[2]]
                if t < 2:
                    total = total + cycles[k][0][0:4, t * 128:t * 128 + 128]
                columns[t].append(total)
        for t in range(4):
            ndb[d, t] = jnp.concatenate(
                [jnp.concatenate(columns[2 * t + half], axis=0) for half in range(2)], axis=1
            ).astype(BF)
        for i in range(3):
            pixel_copy(d, i).start()
        got[d, band] = ndb[d, band]

    def gram_of(d):
        for i in range(3):
            pixel_copy(d, i).wait_recv()
        for t in range(4):
            val = got[d, t].astype(F32)
            for k in range(DOM):
                for half in range(2):
                    wide[d, k, half, 4 * t:4 * t + 4, :] = val[4 * k:4 * k + 4, half * 128:half * 128 + 128]
        x = jnp.concatenate([wide[d, k, half] for k in range(DOM) for half in range(2)], axis=1).astype(BF)
        tall = jnp.concatenate([x, jnp.zeros((128 - BANDS, x.shape[1]), BF)], axis=0)
        part[d] = mm(x, tall, NT)
        for i in range(3):
            gram_copy(d, i).start()

    def domain(d, carry):
        pixels_of(d)
        return carry

    lax.fori_loop(0, 4, domain, 0)

    for d in range(4):
        gram_of(d)
    row = lax.broadcasted_iota(jnp.int32, (BANDS, 128), 0)
    col = lax.broadcasted_iota(jnp.int32, (BANDS, 128), 1)
    systems = []
    for d in range(4):
        for i in range(3):
            gram_copy(d, i).wait_recv()
        count = length_of[d * DOM] + length_of[d * DOM + 1] + length_of[d * DOM + 2] + length_of[d * DOM + 3]
        cov = (part[d] + parts[d, 1]) + (parts[d, 0] + parts[d, 2])
        cov = cov / jnp.full((1, 128), count, jnp.int32).astype(F32)
        diagonal = jnp.where(row == col, cov, 0.0)
        trace = jnp.sum(jnp.sum(diagonal, axis=1, keepdims=True), axis=0, keepdims=True)
        work = cov + jnp.where(row == col, (RIDGE / BANDS) * trace, 0.0)
        systems.append(jnp.where(col == BANDS, 1.0, work))
    for j in range(BANDS):
        for d in range(4):
            work = systems[d]
            pivot = work[j:j + 1, :] / work[j:j + 1, j:j + 1]
            systems[d] = jnp.where(row == j, pivot, work - work[:, j:j + 1] * pivot)
    for d in range(4):
        solved = systems[d][:, BANDS:BANDS + 1]
        weights = solved / jnp.sum(solved, axis=0, keepdims=True)
        for k in range(DOM):
            at = d * DOM + k
            clean = [jnp.sum(weights * wide[d, k, half], axis=0, keepdims=True) for half in range(2)]
            out_ref[at:at + 1, :] = jnp.concatenate(clean, axis=1)
    for i in range(2):
        sent(msg, arrived, 0, i, HALF - i).wait_send()
        sent(back, returned, 1, i, HALF - i).wait_send()
    for d in range(4):
        for i in range(3):
            pixel_copy(d, i).wait_send()
            gram_copy(d, i).wait_send()


def on_device(band_maps, cycle_weight, cycle_len, m_order, legendre, band_start):
    whole = pl.BlockSpec(memory_space=pl.ANY)
    vmem = pltpu.VMEM
    dma = pltpu.SemaphoreType.DMA
    return pl.pallas_call(
        whole_kernel,
        out_shape=jax.ShapeDtypeStruct((RPD, QUARTER), F32),
        in_specs=[whole] * 7,
        out_specs=pl.BlockSpec(memory_space=vmem),
        scratch_shapes=[
            vmem((BPD * RPD, 4 * QUARTER), F32),
            pltpu.SMEM((RPD,), F32),
            pltpu.SMEM((RPD,), jnp.int32),
            pltpu.SMEM((M,), jnp.int32),
            vmem((8, 128), jnp.int32),
            pltpu.SMEM((1,), jnp.int32),
            vmem((SLOTS, LB, 512), BF),
            vmem((11, BPD * RPD, 128), F32),
            vmem((11, BPD * RPD, 128), F32),
            vmem((M, 128), F32),
            vmem((RPD, 64, QUARTER), F32),
            vmem((RPD, 32, 2 * QUARTER), BF),
            vmem((RPD, 32, 2 * QUARTER), BF),
            vmem((M, M), BF),
            vmem((128, M), BF),
            vmem((NDEV, SLOTS, 128), BF),
            vmem((NDEV, SLOTS, 128), BF),
            vmem((4, 4 * GROUPS * SLOTS, 128), F32),
            vmem((2, 4 * GROUPS * SLOTS, 128), F32),
            vmem((SLOTS, 4 * GROUPS, LB), F32),
            vmem((SLOTS, 4 * GROUPS, LB), BF),
            vmem((128, M), F32),
            vmem((NDEV, SLOTS, 128), BACK),
            vmem((NDEV, SLOTS, 128), BACK),
            vmem((DOM, 3, 20, BPD, 128), F32),
            vmem((4, 4, 4 * DOM, QUARTER), BF),
            vmem((4, 4, 4 * DOM, QUARTER), BF),
            vmem((4, DOM, 2, BANDS, 128), F32),
            vmem((4, BANDS, 128), F32),
            vmem((4, 3, BANDS, 128), F32),
            dma((6,)),
            dma((SLOTS,)),
            dma,
            dma((2,)),
            dma((2, 2)),
            dma((4, 3)),
            dma((4, 3)),
            dma((4, 3)),
            dma((4, 3)),
        ],
        compiler_params=pltpu.CompilerParams(
            collective_id=0, has_side_effects=True, vmem_limit_bytes=56 << 20
        ),
        name="needlet_ilc",
    )(
        band_maps.reshape(BPD * RPD, 4 * QUARTER), cycle_weight, cycle_len, m_order, m_order.reshape(8, 128),
        legendre, band_start,
    )


def solution(mesh):
    placed = (P("band", "sky", None), P("sky"), P("sky"), P(), P(("sky", "band"), None, None), P())
    return jax.shard_map(
        on_device, mesh=mesh, in_specs=placed, out_specs=P("sky", "band"), check_vma=False
    )
```

```python
import functools
import math

import jax
import jax.numpy as jnp
from jax import lax
from jax.experimental import pallas as pl
from jax.experimental.pallas import tpu as pltpu
from jax.sharding import PartitionSpec as P

BANDS = 16
M = 1024
LB = 1024
DOM = 4
RIDGE = 0.05
QUARTER = 256
NDEV = 128
HALF = 64
BPD = 4
RPD = 16
GROUPS = 2 * BPD
SLOTS = 8
MESH = pl.DeviceIdType.MESH
BF = jnp.bfloat16
F32 = jnp.float32
BACK = jnp.bfloat16
NT = (((1,), (1,)), ((), ()))
NN = (((1,), (0,)), ((), ()))


def mm(a, b, dims, precision=None):
    return lax.dot_general(a, b, dims, precision=precision, preferred_element_type=F32)


def split(x):
    hi = x.astype(BF)
    return hi, (x - hi.astype(F32)).astype(BF)


def trig_tables(order, length):
    pixel = lax.broadcasted_iota(jnp.int32, order.shape, 1)
    turns = order * (2 * pixel + 1).astype(F32)
    lf = jnp.full((1, QUARTER), length, jnp.int32).astype(F32)
    quarter = 0.5 * lf
    count = jnp.floor(turns * (1.0 / quarter) + 0.5)
    y = (turns - count * quarter) * (math.pi / lf)
    z = y * y
    s = ((-1.9515295891e-4 * z + 8.3321608736e-3) * z - 1.6666654611e-1) * z * y + y
    c = ((2.443315711809948e-5 * z - 1.388731625493765e-3) * z + 4.166664568298827e-2) * (z * z) - 0.5 * z + 1.0
    quad = count - 4.0 * jnp.floor(count * 0.25)
    upper = quad >= 2.0
    odd = (quad == 1.0) | (quad == 3.0)
    sin = jnp.where(odd, c, s)
    cos = jnp.where(odd, s, c)
    sin = jnp.where(upper, -sin, sin)
    cos = jnp.where((quad == 1.0) | (quad == 2.0), -cos, cos)
    return cos, sin


def order_rows():
    row = lax.broadcasted_iota(jnp.int32, (24, QUARTER), 0)
    small = jnp.where(row < 20, row - 16, 256 * (row - 20))
    return jnp.where(row < 8, 4 * row, jnp.where(row < 16, 32 * (row - 8), small)).astype(F32)


def cycle_tables(orders, length):
    cos, sin = trig_tables(orders, length)
    tables = []
    for start, step in ((0, 16), (8, 20)):
        cb, sb = cos[start:start + 8], sin[start:start + 8]
        cs = [(cos[step + i:step + i + 1], sin[step + i:step + i + 1]) for i in range(4)]
        tables.append(jnp.concatenate([cb * c - sb * s for c, s in cs], axis=0))
        tables.append(jnp.concatenate([sb * c + cb * s for c, s in cs], axis=0))
    return tables


def reversal():
    row = lax.broadcasted_iota(jnp.int32, (QUARTER, QUARTER), 0)
    col = lax.broadcasted_iota(jnp.int32, (QUARTER, QUARTER), 1)
    return jnp.where(row + col == QUARTER - 1, 1.0, 0.0).astype(F32)


def window_taper(window):
    turns = 2.0 * window + 1.0
    count = jnp.floor(turns * (1.0 / LB) + 0.5)
    y = (turns - count * LB) * (math.pi / (2 * LB))
    z = y * y
    s = ((-1.9515295891e-4 * z + 8.3321608736e-3) * z - 1.6666654611e-1) * z * y + y
    c = ((2.443315711809948e-5 * z - 1.388731625493765e-3) * z + 4.166664568298827e-2) * (z * z) - 0.5 * z + 1.0
    return jnp.where(count == 0.0, s, jnp.where(count == 1.0, c, -s))


def swap_blocks(rows, lane_group):
    rows = list(rows)
    for bit in (1, 2, 4):
        low = (lane_group // bit) % 2 == 0
        for i in range(8):
            if i & bit:
                continue
            a, b = rows[i], rows[i + bit]
            rows[i] = jnp.where(low, a, pltpu.roll(b, 16 * bit, 1))
            rows[i + bit] = jnp.where(low, pltpu.roll(a, 128 - 16 * bit, 1), b)
    return rows


def k_reach(chip, reach):
    k, j, x = chip
    return 1 - k + reach[j] + reach[x]


def whole_kernel(
    maps_hbm, weight_hbm, len_hbm, order_hbm, order_rows_hbm, leg_hbm, start_hbm, out_ref,
    maps, weight, length_of, order, order_vec, start, leg,
    xs, xr, cs, tp, th, tl, hot, flat_ref, msg, arrived, hx, hy, partial, filtered, early, back, returned, pb, ndb, got, wide,
    part, parts,
    small_sem, leg_sem, local_sem, send_sem, recv_sem, pix_send, pix_recv, cov_send, cov_recv,
):
    sky = lax.axis_index("sky")
    band = lax.axis_index("band")
    me = sky * 4 + band
    bands = [lax.rem(band + j, 4) for j in range(4)]
    others = [bands[2], bands[1], bands[3]]
    core = lax.rem(sky, 2)
    layers = [lax.rem(sky // 2 + j, 4) for j in range(4)]

    small = [
        pltpu.make_async_copy(src, dst, small_sem.at[i])
        for i, (src, dst) in enumerate((
            (maps_hbm, maps), (len_hbm, length_of), (weight_hbm, weight), (order_rows_hbm, order_vec),
            (order_hbm, order), (start_hbm, start),
        ))
    ]
    for copy in small:
        copy.start()
    loads = [pltpu.make_async_copy(leg_hbm.at[i], leg.at[i], leg_sem.at[i]) for i in range(SLOTS)]
    for copy in loads:
        copy.start()

    barrier = pltpu.get_barrier_semaphore()

    def greet(i, carry):
        row = lax.rem(sky + i, 32)
        for column in bands:
            pl.semaphore_signal(barrier, inc=1, device_id=(row, column), device_id_type=MESH)
        return carry

    for column in others:
        pl.semaphore_signal(barrier, inc=1, device_id=(sky, column), device_id_type=MESH)
    lax.fori_loop(1, 32, greet, 0)

    flip = reversal()
    for copy in small:
        copy.wait()
    for tile in range(8):
        xs[tile] = maps[:, tile * 128:tile * 128 + 128]
    for tile in (8, 9, 10):
        xs[tile] = jnp.zeros((BPD * RPD, 128), F32)
        xr[tile] = jnp.zeros((BPD * RPD, 128), F32)
    for block in range(4):
        turned = mm(maps[:, block * QUARTER:(block + 1) * QUARTER], flip, NN, lax.Precision.HIGHEST)
        xr[6 - 2 * block] = turned[:, 0:128]
        xr[7 - 2 * block] = turned[:, 128:256]
    orders = order_rows()
    lane4 = lax.broadcasted_iota(jnp.int32, (BPD, 128), 1)
    pixel = lax.broadcasted_iota(jnp.int32, (BPD, QUARTER), 1)
    quad_group = lax.broadcasted_iota(jnp.int32, (8, 128), 1) // 32

    def window(ref, r, offset):
        tile = offset // 128
        rest = offset - tile * 128
        shift = lax.rem(128 - rest, 128)
        pieces = [pltpu.roll(ref[tile + i, pl.ds(r, BPD, stride=RPD), :], shift, 1) for i in range(3)]
        keep = lane4 < 128 - rest
        return jnp.concatenate(
            [jnp.where(keep, pieces[0], pieces[1]), jnp.where(keep, pieces[1], pieces[2])], axis=1
        )

    def analyse(r, carry):
        length = length_of[r]
        scale = weight[r] * (1.0 / math.sqrt(512 * 1024))
        inside = pixel < length // 4
        x0 = jnp.concatenate([xs[i, pl.ds(r, BPD, stride=RPD), :] for i in range(2)], axis=1)
        x1 = window(xr, r, 1024 - length // 2)
        x2 = window(xs, r, length // 2)
        x3 = window(xr, r, 1024 - length)
        x0, x1, x2, x3 = [jnp.where(inside, v, 0.0) * scale for v in (x0, x1, x2, x3)]
        even = ((x0 + x3) + (x1 + x2), (x0 + x3) - (x1 + x2))
        odd = ((x0 - x3) - (x1 - x2), (x0 - x3) + (x1 - x2))
        cos_p, sin_p, cos_q, sin_q = cycle_tables(orders, length)
        ch, cl = split(cos_q)
        sh, sl = split(sin_q)
        tp[r, 0:32, :] = cos_p
        tp[r, 32:64, :] = sin_p
        th[r] = jnp.concatenate([ch, sh], axis=1)
        tl[r] = jnp.concatenate([cl, sl], axis=1)

        def rows(pair, table):
            pieces = []
            for b in range(BPD):
                for c in range(4):
                    source = pair[c % 2][b:b + 1]
                    pieces.append(jnp.broadcast_to(source, (8, QUARTER)) * table[c * 8:c * 8 + 8])
            return pieces

        minus_sin = -sin_p
        by_cos = jnp.concatenate(rows(even, cos_p) + rows(odd, minus_sin), axis=0).astype(BF)
        by_sin = jnp.concatenate(rows(even, minus_sin) + rows(odd, -cos_p), axis=0).astype(BF)
        product = mm(
            jnp.concatenate([by_cos, by_cos], axis=1), jnp.concatenate([ch, cl], axis=1), NT
        ) + mm(
            jnp.concatenate([by_sin, by_sin], axis=1), jnp.concatenate([sh, sl], axis=1), NT
        )
        for b in range(BPD):
            for half in range(2):
                base = half * 128 + b * 32
                picked = jnp.concatenate([product[base + c * 8:base + c * 8 + 8] for c in range(4)], axis=1)
                at = pl.multiple_of(((b * 2 + half) * RPD + r) * 8, 8)
                cs[pl.ds(at, 8), :] = picked
        return carry

    def analyse_four(i, carry):
        for j in range(4):
            analyse(4 * i + j, carry)
        return carry

    lax.fori_loop(0, RPD // 4, analyse_four, 0)

    flat = jnp.concatenate([cs[pl.ds(a, 128, stride=8), :].astype(BF) for a in range(8)], axis=1)
    slots = order_vec[...]
    where_to = (slots % 32 // 4 * 128 + slots % 4 * 32 + slots // 32).astype(F32)
    lane128 = lax.broadcasted_iota(jnp.int32, (128, 128), 1).astype(F32)
    for block in range(8):
        target = jnp.broadcast_to(where_to[block:block + 1], (128, 128)).T
        hot[block * 128:block * 128 + 128, :] = jnp.concatenate(
            [jnp.where(target == lane128 + 128.0 * a, 1.0, 0.0).astype(BF) for a in range(8)], axis=1
        )

    def send(src, dst, phase, i, row, column):
        pltpu.make_async_remote_copy(
            src_ref=src.at[row * 4 + column], dst_ref=dst.at[me], send_sem=send_sem.at[phase],
            recv_sem=recv_sem.at[phase, i], device_id=(row, column), device_id_type=MESH,
        ).start()

    def sent(src, dst, phase, i, count):
        return pltpu.make_async_remote_copy(
            src_ref=src.at[pl.ds(0, count)], dst_ref=dst.at[pl.ds(0, count)], send_sem=send_sem.at[phase],
            recv_sem=recv_sem.at[phase, i], device_id=(sky, others[0]), device_id_type=MESH,
        )

    reach = {0: 0, 1: 1, 2: 2, 3: 1}
    chips = sorted(
        ((k, j, x) for k in range(2) for j in range(4) for x in range(4)),
        key=lambda c: k_reach(c, reach), reverse=True,
    )

    def half_of(i):
        return lax.rem(sky // 16 + 1 + i, 2)

    def send_half(src, dst, phase, i):
        half = half_of(i)
        same = half * 2 + lax.rem(sky // 8, 2)
        beside = half * 2 + 1 - lax.rem(sky // 8, 2)
        planes = [jnp.where(i == 0, same, beside), jnp.where(i == 0, beside, same)]
        for k, j, x in chips:
            row = planes[k] * 8 + layers[j] * 2
            send(src, dst, phase, i, row + 1 - core, bands[x])
            if (k, j, x) == (1, 0, 0):
                pl.when(i == 0)(lambda: send(src, dst, phase, i, row + core, bands[x]))
            else:
                send(src, dst, phase, i, row + core, bands[x])

    pl.semaphore_wait(barrier, NDEV - 1)

    def slot_half(i, carry):
        half = half_of(i)
        moved = mm(hot[pl.ds(pl.multiple_of(half * 512, 512), 512), :], flat_ref[...], NT)
        msg[pl.ds(pl.multiple_of(half * 64, 64), 64)] = moved.reshape(64, SLOTS, 128).astype(BF)
        send_half(msg, arrived, 0, i)
        return carry

    flat_ref[...] = flat
    lax.fori_loop(0, 2, slot_half, 0)
    own = pltpu.make_async_copy(msg.at[me], arrived.at[me], local_sem)
    own.start()
    window_at = lax.broadcasted_iota(jnp.int32, (8, LB), 1).astype(F32)
    taper = window_taper(window_at)[0:1] * (1.0 / math.sqrt(LB))
    degree = lax.broadcasted_iota(jnp.int32, (1, LB), 1) + start[0]
    own.wait()

    lane_group = lax.broadcasted_iota(jnp.int32, (SLOTS, 128), 1) // 16
    for i in range(2):
        half = half_of(i)
        sent(msg, arrived, 0, i, HALF - i).wait_recv()
        for side in range(2):
            for source in range(4):
                here = [arrived[(half * 16 + side * 8 + k) * 4 + source].astype(F32) for k in range(8)]
                for g, val in enumerate(swap_blocks(here, lane_group)):
                    at = (source * GROUPS + g) * 8
                    hx[2 * i + side, at:at + 8, :] = val
        at = pl.multiple_of(half * QUARTER, QUARTER)
        for m in range(SLOTS):
            coeff = jnp.concatenate(
                [hx[2 * i + side, pl.ds(m, 4 * GROUPS, stride=8), :].astype(BF) for side in range(2)], axis=1
            )
            if i == 0:
                loads[m].wait()
            share = mm(coeff, leg[m, :, pl.ds(at, QUARTER)], NT)
            if i == 0:
                partial[m] = share
            else:
                keep = jnp.where(degree >= order[me * SLOTS + m], taper, 0.0)
                filtered[m] = ((partial[m] + share) * keep).astype(BF)

    def cycle_half(i, carry):
        half = half_of(i)
        at = pl.multiple_of(half * QUARTER, QUARTER)
        for m in range(SLOTS):
            result = mm(filtered[m], leg[m, :, pl.ds(at, QUARTER)], NN)
            for side in range(2):
                hy[side, pl.ds(m, 4 * GROUPS, stride=8), :] = result[:, side * 128:side * 128 + 128]
        for side in range(2):
            for source in range(4):
                done = []
                for g in range(GROUPS):
                    row = (source * GROUPS + g) * 8
                    done.append(hy[side, row:row + 8, :])
                for k, val in enumerate(swap_blocks(done, lane_group)):
                    back[(half * 16 + side * 8 + k) * 4 + source] = val.astype(back.dtype)
        send_half(back, returned, 1, i)
        return carry

    lax.fori_loop(0, 2, cycle_half, 0)
    own_back = pltpu.make_async_copy(back.at[me], returned.at[me], local_sem)
    own_back.start()
    for k in range(4):
        for i in range(3):
            for tile in range(20):
                if tile not in (8, 9, 10):
                    pb[k, i, tile] = jnp.zeros((BPD, 128), F32)
    flip16 = flip.astype(BF)
    own_back.wait()

    lane1 = lax.broadcasted_iota(jnp.int32, (128, 128), 1)
    for i in range(2):
        half = half_of(i)
        sent(back, returned, 1, i, HALF - i).wait_recv()
        turned = jnp.concatenate(
            [returned[pl.ds(half * HALF + d * 16, 16)].astype(F32).reshape(128, 128).T for d in range(4)], axis=1
        ).astype(BF)
        at = half * 512
        for pair in range(4):
            lanes = slice(pair * QUARTER, (pair + 1) * QUARTER)
            moved = mm(turned, hot[pl.ds(pl.multiple_of(at, 512), 512), lanes], NN)
            if i == 0:
                early[:, lanes] = moved
                continue
            moved = moved + early[:, lanes]
            for side in range(2):
                a = pair * 2 + side
                val = moved[:, side * 128:side * 128 + 128]
                if a == 0:
                    val = jnp.where(lane1 == 0, 0.5 * val, val)
                cs[pl.ds(a, 128, stride=8), :] = val
    sub = lax.broadcasted_iota(jnp.int32, (8, QUARTER), 0)
    pixel8 = lax.broadcasted_iota(jnp.int32, (8, QUARTER), 1)

    def row_sums(vals):
        for bit in (4, 2, 1):
            low = (sub // bit) % 2 == 0
            merged = []
            for i in range(bit):
                a, b = vals[i], vals[i + bit]
                if bit == 4:
                    merged.append(jnp.where(low, a, b) + pltpu.roll(jnp.where(low, b, a), 4, 0))
                else:
                    here = jnp.where(low, a, b)
                    there = jnp.where(low, b, a)
                    merged.append(here + jnp.where(low, pltpu.roll(there, 8 - bit, 0), pltpu.roll(there, bit, 0)))
            vals = merged
        return vals[0]

    def cycle(r):
        cos_p = tp[r, 0:32, :]
        sin_p = tp[r, 32:64, :]
        table_hi = jnp.concatenate([th[r]] * 4, axis=0)
        table_lo = jnp.concatenate([tl[r]] * 4, axis=0)
        pieces = []
        for g in range(GROUPS):
            at = pl.multiple_of((g * RPD + r) * 8, 8)
            v = cs[pl.ds(at, 8), :]
            for c in range(4):
                pieces.append(jnp.where(quad_group == c, v, 0.0))
        hi = jnp.concatenate(pieces, axis=0).astype(BF)
        full = mm(jnp.concatenate([hi, hi], axis=1), jnp.concatenate([table_hi, table_lo], axis=0), NN)
        quarters = [[], [], [], []]
        for b in range(BPD):
            re = full[(2 * b) * 32:(2 * b) * 32 + 32]
            im = full[(2 * b + 1) * 32:(2 * b + 1) * 32 + 32]
            even = cos_p * re[:, :QUARTER] - sin_p * re[:, QUARTER:]
            odd = cos_p * im[:, QUARTER:] + sin_p * im[:, :QUARTER]
            ce, co = even[0:8] + even[16:24], even[8:16] + even[24:32]
            de, do = odd[0:8] + odd[16:24], odd[8:16] + odd[24:32]
            for i, total in enumerate((ce + co - de - do, ce - co - de + do, ce - co + de - do, ce + co + de + do)):
                quarters[i].append(total)
        inside = pixel8 < length_of[r] // 4
        return [
            jnp.where(inside, row_sums(q) * (2.0 / math.sqrt(M)), 0.0).astype(BF).astype(F32)
            for q in (quarters[0] + quarters[1], quarters[2] + quarters[3])
        ]

    def pixel_copy(d, i):
        return pltpu.make_async_remote_copy(
            src_ref=ndb.at[d, others[i]], dst_ref=got.at[d, band], send_sem=pix_send.at[d, i],
            recv_sem=pix_recv.at[d, i], device_id=(sky, others[i]), device_id_type=MESH,
        )

    def gram_copy(d, i):
        return pltpu.make_async_remote_copy(
            src_ref=part.at[d], dst_ref=parts.at[d, i], send_sem=cov_send.at[d, i], recv_sem=cov_recv.at[d, i],
            device_id=(sky, others[i]), device_id_type=MESH,
        )

    def pixels_of(d):
        cycles = [cycle(d * DOM + k) for k in range(DOM)]
        turned = mm(
            jnp.concatenate([q[1] for q in cycles], axis=0).astype(BF), flip16, NN
        )
        columns = [[] for _ in range(8)]
        for k in range(DOM):
            length = length_of[d * DOM + k]
            tiles = []
            vals = (turned[k * 8:k * 8 + 4], cycles[k][0][4:8], turned[k * 8 + 4:k * 8 + 8])
            for i, offset in enumerate((length // 2 - QUARTER, length // 2, length - QUARTER)):
                tile = (offset + 1024) // 128 - 8
                rest = offset - tile * 128
                low = pltpu.roll(vals[i][:, :128], rest, 1)
                high = pltpu.roll(vals[i][:, 128:], rest, 1)
                wrapped = lane4 < rest
                pb[k, i, 8] = jnp.where(wrapped, 0.0, low)
                pb[k, i, 9] = jnp.where(wrapped, low, high)
                pb[k, i, 10] = jnp.where(wrapped, high, 0.0)
                tiles.append(tile)
            for t in range(8):
                total = pb[k, 0, 8 + t - tiles[0]] + pb[k, 1, 8 + t - tiles[1]] + pb[k, 2, 8 + t - tiles[2]]
                if t < 2:
                    total = total + cycles[k][0][0:4, t * 128:t * 128 + 128]
                columns[t].append(total)
        for t in range(4):
            ndb[d, t] = jnp.concatenate(
                [jnp.concatenate(columns[2 * t + half], axis=0) for half in range(2)], axis=1
            ).astype(BF)
        for i in range(3):
            pixel_copy(d, i).start()
        got[d, band] = ndb[d, band]

    def gram_of(d):
        for i in range(3):
            pixel_copy(d, i).wait_recv()
        for t in range(4):
            val = got[d, t].astype(F32)
            for k in range(DOM):
                for half in range(2):
                    wide[d, k, half, 4 * t:4 * t + 4, :] = val[4 * k:4 * k + 4, half * 128:half * 128 + 128]
        x = jnp.concatenate([wide[d, k, half] for k in range(DOM) for half in range(2)], axis=1).astype(BF)
        tall = jnp.concatenate([x, jnp.zeros((128 - BANDS, x.shape[1]), BF)], axis=0)
        part[d] = mm(x, tall, NT)
        for i in range(3):
            gram_copy(d, i).start()

    def domain(d, carry):
        pixels_of(d)
        return carry

    lax.fori_loop(0, 4, domain, 0)

    for d in range(4):
        gram_of(d)
    row = lax.broadcasted_iota(jnp.int32, (BANDS, 128), 0)
    col = lax.broadcasted_iota(jnp.int32, (BANDS, 128), 1)
    systems = []
    for d in range(4):
        for i in range(3):
            gram_copy(d, i).wait_recv()
        count = length_of[d * DOM] + length_of[d * DOM + 1] + length_of[d * DOM + 2] + length_of[d * DOM + 3]
        cov = (part[d] + parts[d, 1]) + (parts[d, 0] + parts[d, 2])
        cov = cov / jnp.full((1, 128), count, jnp.int32).astype(F32)
        diagonal = jnp.where(row == col, cov, 0.0)
        trace = jnp.sum(jnp.sum(diagonal, axis=1, keepdims=True), axis=0, keepdims=True)
        work = cov + jnp.where(row == col, (RIDGE / BANDS) * trace, 0.0)
        systems.append(jnp.where(col == BANDS, 1.0, work))
    for j in range(BANDS):
        for d in range(4):
            work = systems[d]
            pivot = work[j:j + 1, :] / work[j:j + 1, j:j + 1]
            systems[d] = jnp.where(row == j, pivot, work - work[:, j:j + 1] * pivot)
    for d in range(4):
        solved = systems[d][:, BANDS:BANDS + 1]
        weights = solved / jnp.sum(solved, axis=0, keepdims=True)
        for k in range(DOM):
            at = d * DOM + k
            clean = [jnp.sum(weights * wide[d, k, half], axis=0, keepdims=True) for half in range(2)]
            out_ref[at:at + 1, :] = jnp.concatenate(clean, axis=1)
    for i in range(2):
        sent(msg, arrived, 0, i, HALF - i).wait_send()
        sent(back, returned, 1, i, HALF - i).wait_send()
    for d in range(4):
        for i in range(3):
            pixel_copy(d, i).wait_send()
            gram_copy(d, i).wait_send()


def on_device(band_maps, cycle_weight, cycle_len, m_order, legendre, band_start):
    whole = pl.BlockSpec(memory_space=pl.ANY)
    vmem = pltpu.VMEM
    dma = pltpu.SemaphoreType.DMA
    return pl.pallas_call(
        whole_kernel,
        out_shape=jax.ShapeDtypeStruct((RPD, QUARTER), F32),
        in_specs=[whole] * 7,
        out_specs=pl.BlockSpec(memory_space=vmem),
        scratch_shapes=[
            vmem((BPD * RPD, 4 * QUARTER), F32),
            pltpu.SMEM((RPD,), F32),
            pltpu.SMEM((RPD,), jnp.int32),
            pltpu.SMEM((M,), jnp.int32),
            vmem((8, 128), jnp.int32),
            pltpu.SMEM((1,), jnp.int32),
            vmem((SLOTS, LB, 512), BF),
            vmem((11, BPD * RPD, 128), F32),
            vmem((11, BPD * RPD, 128), F32),
            vmem((M, 128), F32),
            vmem((RPD, 64, QUARTER), F32),
            vmem((RPD, 32, 2 * QUARTER), BF),
            vmem((RPD, 32, 2 * QUARTER), BF),
            vmem((M, M), BF),
            vmem((128, M), BF),
            vmem((NDEV, SLOTS, 128), BF),
            vmem((NDEV, SLOTS, 128), BF),
            vmem((4, 4 * GROUPS * SLOTS, 128), F32),
            vmem((2, 4 * GROUPS * SLOTS, 128), F32),
            vmem((SLOTS, 4 * GROUPS, LB), F32),
            vmem((SLOTS, 4 * GROUPS, LB), BF),
            vmem((128, M), F32),
            vmem((NDEV, SLOTS, 128), BACK),
            vmem((NDEV, SLOTS, 128), BACK),
            vmem((DOM, 3, 20, BPD, 128), F32),
            vmem((4, 4, 4 * DOM, QUARTER), BF),
            vmem((4, 4, 4 * DOM, QUARTER), BF),
            vmem((4, DOM, 2, BANDS, 128), F32),
            vmem((4, BANDS, 128), F32),
            vmem((4, 3, BANDS, 128), F32),
            dma((6,)),
            dma((SLOTS,)),
            dma,
            dma((2,)),
            dma((2, 2)),
            dma((4, 3)),
            dma((4, 3)),
            dma((4, 3)),
            dma((4, 3)),
        ],
        compiler_params=pltpu.CompilerParams(
            collective_id=0, has_side_effects=True, vmem_limit_bytes=56 << 20
        ),
        name="needlet_ilc",
    )(
        band_maps.reshape(BPD * RPD, 4 * QUARTER), cycle_weight, cycle_len, m_order, m_order.reshape(8, 128),
        legendre, band_start,
    )


def solution(mesh):
    placed = (P("band", "sky", None), P("sky"), P("sky"), P(), P(("sky", "band"), None, None), P())
    return jax.shard_map(
        on_device, mesh=mesh, in_specs=placed, out_specs=P("sky", "band"), check_vma=False
    )
```

```python
import functools
import math

import jax
import jax.numpy as jnp
from jax import lax
from jax.experimental import pallas as pl
from jax.experimental.pallas import tpu as pltpu
from jax.sharding import PartitionSpec as P

BANDS = 16
M = 1024
LB = 1024
DOM = 4
RIDGE = 0.05
QUARTER = 256
NDEV = 128
HALF = 64
BPD = 4
RPD = 16
GROUPS = 2 * BPD
SLOTS = 8
MESH = pl.DeviceIdType.MESH
BF = jnp.bfloat16
F32 = jnp.float32
BACK = jnp.bfloat16
NT = (((1,), (1,)), ((), ()))
NN = (((1,), (0,)), ((), ()))


def mm(a, b, dims, precision=None):
    return lax.dot_general(a, b, dims, precision=precision, preferred_element_type=F32)


def split(x):
    hi = x.astype(BF)
    return hi, (x - hi.astype(F32)).astype(BF)


def trig_tables(order, length):
    pixel = lax.broadcasted_iota(jnp.int32, order.shape, 1)
    turns = order * (2 * pixel + 1).astype(F32)
    lf = jnp.full((1, QUARTER), length, jnp.int32).astype(F32)
    quarter = 0.5 * lf
    count = jnp.floor(turns * (1.0 / quarter) + 0.5)
    y = (turns - count * quarter) * (math.pi / lf)
    z = y * y
    s = ((-1.9515295891e-4 * z + 8.3321608736e-3) * z - 1.6666654611e-1) * z * y + y
    c = ((2.443315711809948e-5 * z - 1.388731625493765e-3) * z + 4.166664568298827e-2) * (z * z) - 0.5 * z + 1.0
    quad = count - 4.0 * jnp.floor(count * 0.25)
    upper = quad >= 2.0
    odd = (quad == 1.0) | (quad == 3.0)
    sin = jnp.where(odd, c, s)
    cos = jnp.where(odd, s, c)
    sin = jnp.where(upper, -sin, sin)
    cos = jnp.where((quad == 1.0) | (quad == 2.0), -cos, cos)
    return cos, sin


def order_rows():
    row = lax.broadcasted_iota(jnp.int32, (24, QUARTER), 0)
    small = jnp.where(row < 20, row - 16, 256 * (row - 20))
    return jnp.where(row < 8, 4 * row, jnp.where(row < 16, 32 * (row - 8), small)).astype(F32)


def cycle_tables(orders, length):
    cos, sin = trig_tables(orders, length)
    tables = []
    for start, step in ((0, 16), (8, 20)):
        cb, sb = cos[start:start + 8], sin[start:start + 8]
        cs = [(cos[step + i:step + i + 1], sin[step + i:step + i + 1]) for i in range(4)]
        tables.append(jnp.concatenate([cb * c - sb * s for c, s in cs], axis=0))
        tables.append(jnp.concatenate([sb * c + cb * s for c, s in cs], axis=0))
    return tables


def reversal():
    row = lax.broadcasted_iota(jnp.int32, (QUARTER, QUARTER), 0)
    col = lax.broadcasted_iota(jnp.int32, (QUARTER, QUARTER), 1)
    return jnp.where(row + col == QUARTER - 1, 1.0, 0.0).astype(F32)


def window_taper(window):
    turns = 2.0 * window + 1.0
    count = jnp.floor(turns * (1.0 / LB) + 0.5)
    y = (turns - count * LB) * (math.pi / (2 * LB))
    z = y * y
    s = ((-1.9515295891e-4 * z + 8.3321608736e-3) * z - 1.6666654611e-1) * z * y + y
    c = ((2.443315711809948e-5 * z - 1.388731625493765e-3) * z + 4.166664568298827e-2) * (z * z) - 0.5 * z + 1.0
    return jnp.where(count == 0.0, s, jnp.where(count == 1.0, c, -s))


def swap_blocks(rows, lane_group):
    rows = list(rows)
    for bit in (1, 2, 4):
        low = (lane_group // bit) % 2 == 0
        for i in range(8):
            if i & bit:
                continue
            a, b = rows[i], rows[i + bit]
            rows[i] = jnp.where(low, a, pltpu.roll(b, 16 * bit, 1))
            rows[i + bit] = jnp.where(low, pltpu.roll(a, 128 - 16 * bit, 1), b)
    return rows


def k_reach(chip, reach):
    k, j, x = chip
    return 1 - k + reach[j] + reach[x]


def whole_kernel(
    maps_hbm, weight_hbm, len_hbm, order_hbm, order_rows_hbm, leg_hbm, start_hbm, out_ref,
    maps, weight, length_of, order, order_vec, start, leg,
    xs, xr, cs, tp, th, tl, hot, flat_ref, msg, arrived, hx, hy, partial, filtered, early, back, returned, pb, ndb, got, wide,
    part, parts,
    small_sem, leg_sem, local_sem, send_sem, recv_sem, pix_send, pix_recv, cov_send, cov_recv,
):
    sky = lax.axis_index("sky")
    band = lax.axis_index("band")
    me = sky * 4 + band
    bands = [lax.rem(band + j, 4) for j in range(4)]
    others = [bands[2], bands[1], bands[3]]
    core = lax.rem(sky, 2)
    layers = [lax.rem(sky // 2 + j, 4) for j in range(4)]

    small = [
        pltpu.make_async_copy(src, dst, small_sem.at[i])
        for i, (src, dst) in enumerate((
            (maps_hbm, maps), (len_hbm, length_of), (weight_hbm, weight), (order_rows_hbm, order_vec),
            (order_hbm, order), (start_hbm, start),
        ))
    ]
    for copy in small:
        copy.start()
    loads = [pltpu.make_async_copy(leg_hbm.at[i], leg.at[i], leg_sem.at[i]) for i in range(SLOTS)]
    for copy in loads:
        copy.start()

    barrier = pltpu.get_barrier_semaphore()

    def greet(i, carry):
        row = lax.rem(sky + i, 32)
        for column in bands:
            pl.semaphore_signal(barrier, inc=1, device_id=(row, column), device_id_type=MESH)
        return carry

    for column in others:
        pl.semaphore_signal(barrier, inc=1, device_id=(sky, column), device_id_type=MESH)
    lax.fori_loop(1, 32, greet, 0)

    flip = reversal()
    for copy in small:
        copy.wait()
    for tile in range(8):
        xs[tile] = maps[:, tile * 128:tile * 128 + 128]
    for tile in (8, 9, 10):
        xs[tile] = jnp.zeros((BPD * RPD, 128), F32)
        xr[tile] = jnp.zeros((BPD * RPD, 128), F32)
    for block in range(4):
        turned = mm(maps[:, block * QUARTER:(block + 1) * QUARTER], flip, NN, lax.Precision.HIGHEST)
        xr[6 - 2 * block] = turned[:, 0:128]
        xr[7 - 2 * block] = turned[:, 128:256]
    orders = order_rows()
    lane4 = lax.broadcasted_iota(jnp.int32, (BPD, 128), 1)
    pixel = lax.broadcasted_iota(jnp.int32, (BPD, QUARTER), 1)
    quad_group = lax.broadcasted_iota(jnp.int32, (8, 128), 1) // 32

    def window(ref, r, offset):
        tile = offset // 128
        rest = offset - tile * 128
        shift = lax.rem(128 - rest, 128)
        pieces = [pltpu.roll(ref[tile + i, pl.ds(r, BPD, stride=RPD), :], shift, 1) for i in range(3)]
        keep = lane4 < 128 - rest
        return jnp.concatenate(
            [jnp.where(keep, pieces[0], pieces[1]), jnp.where(keep, pieces[1], pieces[2])], axis=1
        )

    def analyse(r, carry):
        length = length_of[r]
        scale = weight[r] * (1.0 / math.sqrt(512 * 1024))
        inside = pixel < length // 4
        x0 = jnp.concatenate([xs[i, pl.ds(r, BPD, stride=RPD), :] for i in range(2)], axis=1)
        x1 = window(xr, r, 1024 - length // 2)
        x2 = window(xs, r, length // 2)
        x3 = window(xr, r, 1024 - length)
        x0, x1, x2, x3 = [jnp.where(inside, v, 0.0) * scale for v in (x0, x1, x2, x3)]
        even = ((x0 + x3) + (x1 + x2), (x0 + x3) - (x1 + x2))
        odd = ((x0 - x3) - (x1 - x2), (x0 - x3) + (x1 - x2))
        cos_p, sin_p, cos_q, sin_q = cycle_tables(orders, length)
        ch, cl = split(cos_q)
        sh, sl = split(sin_q)
        tp[r, 0:32, :] = cos_p
        tp[r, 32:64, :] = sin_p
        th[r] = jnp.concatenate([ch, sh], axis=1)
        tl[r] = jnp.concatenate([cl, sl], axis=1)

        def rows(pair, table):
            pieces = []
            for b in range(BPD):
                for c in range(4):
                    source = pair[c % 2][b:b + 1]
                    pieces.append(jnp.broadcast_to(source, (8, QUARTER)) * table[c * 8:c * 8 + 8])
            return pieces

        minus_sin = -sin_p
        by_cos = split(jnp.concatenate(rows(even, cos_p) + rows(odd, minus_sin), axis=0))
        by_sin = split(jnp.concatenate(rows(even, minus_sin) + rows(odd, -cos_p), axis=0))
        product = mm(
            jnp.concatenate([by_cos[0], by_cos[0], by_cos[1]], axis=1), jnp.concatenate([ch, cl, ch], axis=1), NT
        ) + mm(
            jnp.concatenate([by_sin[0], by_sin[0], by_sin[1]], axis=1), jnp.concatenate([sh, sl, sh], axis=1), NT
        )
        for b in range(BPD):
            for half in range(2):
                base = half * 128 + b * 32
                picked = jnp.concatenate([product[base + c * 8:base + c * 8 + 8] for c in range(4)], axis=1)
                at = pl.multiple_of(((b * 2 + half) * RPD + r) * 8, 8)
                cs[pl.ds(at, 8), :] = picked
        return carry

    def analyse_four(i, carry):
        for j in range(8):
            analyse(8 * i + j, carry)
        return carry

    lax.fori_loop(0, RPD // 8, analyse_four, 0)

    flat = jnp.concatenate([cs[pl.ds(a, 128, stride=8), :].astype(BF) for a in range(8)], axis=1)
    slots = order_vec[...]
    where_to = (slots % 32 // 4 * 128 + slots % 4 * 32 + slots // 32).astype(F32)
    lane128 = lax.broadcasted_iota(jnp.int32, (128, 128), 1).astype(F32)
    for block in range(8):
        target = jnp.broadcast_to(where_to[block:block + 1], (128, 128)).T
        hot[block * 128:block * 128 + 128, :] = jnp.concatenate(
            [jnp.where(target == lane128 + 128.0 * a, 1.0, 0.0).astype(BF) for a in range(8)], axis=1
        )

    def send(src, dst, phase, i, row, column):
        pltpu.make_async_remote_copy(
            src_ref=src.at[row * 4 + column], dst_ref=dst.at[me], send_sem=send_sem.at[phase],
            recv_sem=recv_sem.at[phase, i], device_id=(row, column), device_id_type=MESH,
        ).start()

    def sent(src, dst, phase, i, count):
        return pltpu.make_async_remote_copy(
            src_ref=src.at[pl.ds(0, count)], dst_ref=dst.at[pl.ds(0, count)], send_sem=send_sem.at[phase],
            recv_sem=recv_sem.at[phase, i], device_id=(sky, others[0]), device_id_type=MESH,
        )

    reach = {0: 0, 1: 1, 2: 2, 3: 1}
    chips = sorted(
        ((k, j, x) for k in range(2) for j in range(4) for x in range(4)),
        key=lambda c: k_reach(c, reach), reverse=True,
    )

    def half_of(i):
        return lax.rem(sky // 16 + 1 + i, 2)

    def send_half(src, dst, phase, i):
        half = half_of(i)
        same = half * 2 + lax.rem(sky // 8, 2)
        beside = half * 2 + 1 - lax.rem(sky // 8, 2)
        planes = [jnp.where(i == 0, same, beside), jnp.where(i == 0, beside, same)]
        for k, j, x in chips:
            row = planes[k] * 8 + layers[j] * 2
            send(src, dst, phase, i, row + 1 - core, bands[x])
            if (k, j, x) == (1, 0, 0):
                pl.when(i == 0)(lambda: send(src, dst, phase, i, row + core, bands[x]))
            else:
                send(src, dst, phase, i, row + core, bands[x])

    pl.semaphore_wait(barrier, NDEV - 1)

    def slot_half(i, carry):
        half = half_of(i)
        moved = mm(hot[pl.ds(pl.multiple_of(half * 512, 512), 512), :], flat_ref[...], NT)
        msg[pl.ds(pl.multiple_of(half * 64, 64), 64)] = moved.reshape(64, SLOTS, 128).astype(BF)
        send_half(msg, arrived, 0, i)
        return carry

    flat_ref[...] = flat
    lax.fori_loop(0, 2, slot_half, 0)
    own = pltpu.make_async_copy(msg.at[me], arrived.at[me], local_sem)
    own.start()
    window_at = lax.broadcasted_iota(jnp.int32, (8, LB), 1).astype(F32)
    taper = window_taper(window_at)[0:1] * (1.0 / math.sqrt(LB))
    degree = lax.broadcasted_iota(jnp.int32, (1, LB), 1) + start[0]
    own.wait()

    lane_group = lax.broadcasted_iota(jnp.int32, (SLOTS, 128), 1) // 16
    for i in range(2):
        half = half_of(i)
        sent(msg, arrived, 0, i, HALF - i).wait_recv()
        for side in range(2):
            for source in range(4):
                here = [arrived[(half * 16 + side * 8 + k) * 4 + source].astype(F32) for k in range(8)]
                for g, val in enumerate(swap_blocks(here, lane_group)):
                    at = (source * GROUPS + g) * 8
                    hx[2 * i + side, at:at + 8, :] = val
        at = pl.multiple_of(half * QUARTER, QUARTER)
        for m in range(SLOTS):
            coeff = jnp.concatenate(
                [hx[2 * i + side, pl.ds(m, 4 * GROUPS, stride=8), :].astype(BF) for side in range(2)], axis=1
            )
            if i == 0:
                loads[m].wait()
            share = mm(coeff, leg[m, :, pl.ds(at, QUARTER)], NT)
            if i == 0:
                partial[m] = share
            else:
                keep = jnp.where(degree >= order[me * SLOTS + m], taper, 0.0)
                filtered[m] = ((partial[m] + share) * keep).astype(BF)

    def cycle_half(i, carry):
        half = half_of(i)
        at = pl.multiple_of(half * QUARTER, QUARTER)
        for m in range(SLOTS):
            result = mm(filtered[m], leg[m, :, pl.ds(at, QUARTER)], NN)
            for side in range(2):
                hy[side, pl.ds(m, 4 * GROUPS, stride=8), :] = result[:, side * 128:side * 128 + 128]
        for side in range(2):
            for source in range(4):
                done = []
                for g in range(GROUPS):
                    row = (source * GROUPS + g) * 8
                    done.append(hy[side, row:row + 8, :])
                for k, val in enumerate(swap_blocks(done, lane_group)):
                    back[(half * 16 + side * 8 + k) * 4 + source] = val.astype(back.dtype)
        send_half(back, returned, 1, i)
        return carry

    lax.fori_loop(0, 2, cycle_half, 0)
    own_back = pltpu.make_async_copy(back.at[me], returned.at[me], local_sem)
    own_back.start()
    for k in range(4):
        for i in range(3):
            for tile in range(20):
                if tile not in (8, 9, 10):
                    pb[k, i, tile] = jnp.zeros((BPD, 128), F32)
    flip16 = flip.astype(BF)
    own_back.wait()

    lane1 = lax.broadcasted_iota(jnp.int32, (128, 128), 1)
    for i in range(2):
        half = half_of(i)
        sent(back, returned, 1, i, HALF - i).wait_recv()
        turned = jnp.concatenate(
            [returned[pl.ds(half * HALF + d * 16, 16)].astype(F32).reshape(128, 128).T for d in range(4)], axis=1
        ).astype(BF)
        at = half * 512
        for pair in range(4):
            lanes = slice(pair * QUARTER, (pair + 1) * QUARTER)
            moved = mm(turned, hot[pl.ds(pl.multiple_of(at, 512), 512), lanes], NN)
            if i == 0:
                early[:, lanes] = moved
                continue
            moved = moved + early[:, lanes]
            for side in range(2):
                a = pair * 2 + side
                val = moved[:, side * 128:side * 128 + 128]
                if a == 0:
                    val = jnp.where(lane1 == 0, 0.5 * val, val)
                cs[pl.ds(a, 128, stride=8), :] = val
    sub = lax.broadcasted_iota(jnp.int32, (8, QUARTER), 0)
    pixel8 = lax.broadcasted_iota(jnp.int32, (8, QUARTER), 1)

    def row_sums(vals):
        for bit in (4, 2, 1):
            low = (sub // bit) % 2 == 0
            merged = []
            for i in range(bit):
                a, b = vals[i], vals[i + bit]
                if bit == 4:
                    merged.append(jnp.where(low, a, b) + pltpu.roll(jnp.where(low, b, a), 4, 0))
                else:
                    here = jnp.where(low, a, b)
                    there = jnp.where(low, b, a)
                    merged.append(here + jnp.where(low, pltpu.roll(there, 8 - bit, 0), pltpu.roll(there, bit, 0)))
            vals = merged
        return vals[0]

    def cycle(r):
        cos_p = tp[r, 0:32, :]
        sin_p = tp[r, 32:64, :]
        table_hi = jnp.concatenate([th[r]] * 4, axis=0)
        table_lo = jnp.concatenate([tl[r]] * 4, axis=0)
        pieces = []
        for g in range(GROUPS):
            at = pl.multiple_of((g * RPD + r) * 8, 8)
            v = cs[pl.ds(at, 8), :]
            for c in range(4):
                pieces.append(jnp.where(quad_group == c, v, 0.0))
        hi = jnp.concatenate(pieces, axis=0).astype(BF)
        full = mm(jnp.concatenate([hi, hi], axis=1), jnp.concatenate([table_hi, table_lo], axis=0), NN)
        quarters = [[], [], [], []]
        for b in range(BPD):
            re = full[(2 * b) * 32:(2 * b) * 32 + 32]
            im = full[(2 * b + 1) * 32:(2 * b + 1) * 32 + 32]
            even = cos_p * re[:, :QUARTER] - sin_p * re[:, QUARTER:]
            odd = cos_p * im[:, QUARTER:] + sin_p * im[:, :QUARTER]
            ce, co = even[0:8] + even[16:24], even[8:16] + even[24:32]
            de, do = odd[0:8] + odd[16:24], odd[8:16] + odd[24:32]
            for i, total in enumerate((ce + co - de - do, ce - co - de + do, ce - co + de - do, ce + co + de + do)):
                quarters[i].append(total)
        inside = pixel8 < length_of[r] // 4
        return [
            jnp.where(inside, row_sums(q) * (2.0 / math.sqrt(M)), 0.0).astype(BF).astype(F32)
            for q in (quarters[0] + quarters[1], quarters[2] + quarters[3])
        ]

    def pixel_copy(d, i):
        return pltpu.make_async_remote_copy(
            src_ref=ndb.at[d, others[i]], dst_ref=got.at[d, band], send_sem=pix_send.at[d, i],
            recv_sem=pix_recv.at[d, i], device_id=(sky, others[i]), device_id_type=MESH,
        )

    def gram_copy(d, i):
        return pltpu.make_async_remote_copy(
            src_ref=part.at[d], dst_ref=parts.at[d, i], send_sem=cov_send.at[d, i], recv_sem=cov_recv.at[d, i],
            device_id=(sky, others[i]), device_id_type=MESH,
        )

    def pixels_of(d):
        cycles = [cycle(d * DOM + k) for k in range(DOM)]
        turned = mm(
            jnp.concatenate([q[1] for q in cycles], axis=0).astype(BF), flip16, NN
        )
        columns = [[] for _ in range(8)]
        for k in range(DOM):
            length = length_of[d * DOM + k]
            tiles = []
            vals = (turned[k * 8:k * 8 + 4], cycles[k][0][4:8], turned[k * 8 + 4:k * 8 + 8])
            for i, offset in enumerate((length // 2 - QUARTER, length // 2, length - QUARTER)):
                tile = (offset + 1024) // 128 - 8
                rest = offset - tile * 128
                low = pltpu.roll(vals[i][:, :128], rest, 1)
                high = pltpu.roll(vals[i][:, 128:], rest, 1)
                wrapped = lane4 < rest
                pb[k, i, 8] = jnp.where(wrapped, 0.0, low)
                pb[k, i, 9] = jnp.where(wrapped, low, high)
                pb[k, i, 10] = jnp.where(wrapped, high, 0.0)
                tiles.append(tile)
            for t in range(8):
                total = pb[k, 0, 8 + t - tiles[0]] + pb[k, 1, 8 + t - tiles[1]] + pb[k, 2, 8 + t - tiles[2]]
                if t < 2:
                    total = total + cycles[k][0][0:4, t * 128:t * 128 + 128]
                columns[t].append(total)
        for t in range(4):
            ndb[d, t] = jnp.concatenate(
                [jnp.concatenate(columns[2 * t + half], axis=0) for half in range(2)], axis=1
            ).astype(BF)
        for i in range(3):
            pixel_copy(d, i).start()
        got[d, band] = ndb[d, band]

    def gram_of(d):
        for i in range(3):
            pixel_copy(d, i).wait_recv()
        for t in range(4):
            val = got[d, t].astype(F32)
            for k in range(DOM):
                for half in range(2):
                    wide[d, k, half, 4 * t:4 * t + 4, :] = val[4 * k:4 * k + 4, half * 128:half * 128 + 128]
        x = jnp.concatenate([wide[d, k, half] for k in range(DOM) for half in range(2)], axis=1).astype(BF)
        tall = jnp.concatenate([x, jnp.zeros((128 - BANDS, x.shape[1]), BF)], axis=0)
        part[d] = mm(x, tall, NT)
        for i in range(3):
            gram_copy(d, i).start()

    def domain(d, carry):
        pixels_of(d)
        return carry

    lax.fori_loop(0, 4, domain, 0)

    for d in range(4):
        gram_of(d)
    row = lax.broadcasted_iota(jnp.int32, (BANDS, 128), 0)
    col = lax.broadcasted_iota(jnp.int32, (BANDS, 128), 1)
    systems = []
    for d in range(4):
        for i in range(3):
            gram_copy(d, i).wait_recv()
        count = length_of[d * DOM] + length_of[d * DOM + 1] + length_of[d * DOM + 2] + length_of[d * DOM + 3]
        cov = (part[d] + parts[d, 1]) + (parts[d, 0] + parts[d, 2])
        cov = cov / jnp.full((1, 128), count, jnp.int32).astype(F32)
        diagonal = jnp.where(row == col, cov, 0.0)
        trace = jnp.sum(jnp.sum(diagonal, axis=1, keepdims=True), axis=0, keepdims=True)
        work = cov + jnp.where(row == col, (RIDGE / BANDS) * trace, 0.0)
        systems.append(jnp.where(col == BANDS, 1.0, work))
    for j in range(BANDS):
        for d in range(4):
            work = systems[d]
            pivot = work[j:j + 1, :] / work[j:j + 1, j:j + 1]
            systems[d] = jnp.where(row == j, pivot, work - work[:, j:j + 1] * pivot)
    for d in range(4):
        solved = systems[d][:, BANDS:BANDS + 1]
        weights = solved / jnp.sum(solved, axis=0, keepdims=True)
        for k in range(DOM):
            at = d * DOM + k
            clean = [jnp.sum(weights * wide[d, k, half], axis=0, keepdims=True) for half in range(2)]
            out_ref[at:at + 1, :] = jnp.concatenate(clean, axis=1)
    for i in range(2):
        sent(msg, arrived, 0, i, HALF - i).wait_send()
        sent(back, returned, 1, i, HALF - i).wait_send()
    for d in range(4):
        for i in range(3):
            pixel_copy(d, i).wait_send()
            gram_copy(d, i).wait_send()


def on_device(band_maps, cycle_weight, cycle_len, m_order, legendre, band_start):
    whole = pl.BlockSpec(memory_space=pl.ANY)
    vmem = pltpu.VMEM
    dma = pltpu.SemaphoreType.DMA
    return pl.pallas_call(
        whole_kernel,
        out_shape=jax.ShapeDtypeStruct((RPD, QUARTER), F32),
        in_specs=[whole] * 7,
        out_specs=pl.BlockSpec(memory_space=vmem),
        scratch_shapes=[
            vmem((BPD * RPD, 4 * QUARTER), F32),
            pltpu.SMEM((RPD,), F32),
            pltpu.SMEM((RPD,), jnp.int32),
            pltpu.SMEM((M,), jnp.int32),
            vmem((8, 128), jnp.int32),
            pltpu.SMEM((1,), jnp.int32),
            vmem((SLOTS, LB, 512), BF),
            vmem((11, BPD * RPD, 128), F32),
            vmem((11, BPD * RPD, 128), F32),
            vmem((M, 128), F32),
            vmem((RPD, 64, QUARTER), F32),
            vmem((RPD, 32, 2 * QUARTER), BF),
            vmem((RPD, 32, 2 * QUARTER), BF),
            vmem((M, M), BF),
            vmem((128, M), BF),
            vmem((NDEV, SLOTS, 128), BF),
            vmem((NDEV, SLOTS, 128), BF),
            vmem((4, 4 * GROUPS * SLOTS, 128), F32),
            vmem((2, 4 * GROUPS * SLOTS, 128), F32),
            vmem((SLOTS, 4 * GROUPS, LB), F32),
            vmem((SLOTS, 4 * GROUPS, LB), BF),
            vmem((128, M), F32),
            vmem((NDEV, SLOTS, 128), BACK),
            vmem((NDEV, SLOTS, 128), BACK),
            vmem((DOM, 3, 20, BPD, 128), F32),
            vmem((4, 4, 4 * DOM, QUARTER), BF),
            vmem((4, 4, 4 * DOM, QUARTER), BF),
            vmem((4, DOM, 2, BANDS, 128), F32),
            vmem((4, BANDS, 128), F32),
            vmem((4, 3, BANDS, 128), F32),
            dma((6,)),
            dma((SLOTS,)),
            dma,
            dma((2,)),
            dma((2, 2)),
            dma((4, 3)),
            dma((4, 3)),
            dma((4, 3)),
            dma((4, 3)),
        ],
        compiler_params=pltpu.CompilerParams(
            collective_id=0, has_side_effects=True, vmem_limit_bytes=56 << 20
        ),
        name="needlet_ilc",
    )(
        band_maps.reshape(BPD * RPD, 4 * QUARTER), cycle_weight, cycle_len, m_order, m_order.reshape(8, 128),
        legendre, band_start,
    )


def solution(mesh):
    placed = (P("band", "sky", None), P("sky"), P("sky"), P(), P(("sky", "band"), None, None), P())
    return jax.shard_map(
        on_device, mesh=mesh, in_specs=placed, out_specs=P("sky", "band"), check_vma=False
    )
```
